512 devices in a mesh: band: 4 (over x), ty: 16 (over y, core), tx: 8 (over z).
Axes of the slice: x: 4, y: 8, z: 8, core: 2. Of those that a mesh axis runs over, the one named last changes fastest.
Arguments:
- dirty: float32 [8, 4096, 2048], P('band', 'ty', 'tx'), may hold values from -6 to 6
- psf: bfloat16 [8, 20, 2304], P('band'), may hold values from -4 to 4
- comp_tile: int32 [16384, 1], P(('ty', 'tx')), may hold values from 0 to 127; in each aligned block of 128 rows (0 to 127, 128 to 255, ...) at most 2 rows name the same one
- comp_offset: int32 [16384, 2], P(('ty', 'tx')), may hold values from 0 to 255
- comp_scale: int32 [16384], P(('ty', 'tx')), may hold values from 0 to 4
- comp_amp: float32 [16384, 4], P(('ty', 'tx')), may hold values from -6 to 6
- fit_weight: float32 [8, 4], P('band'), may hold values from -5 to 5
Outputs:
- residual: float32 [8, 4096, 2048], P('band', 'ty', 'tx')
- taylor_fit: float32 [4, 4096, 2048], P('band', 'ty', 'tx')
The draws below stay inside these ranges and needn't reach their ends.
Inputs may be any that keep to these rules, and one draw needn't show every extreme that they name: `comp_tile`: the 128 components of one device name at most 2 components for one tile, and exactly 2 for some tile on some device.
All inputs are finite; a program needn't handle non-finite values.
Results may differ from the reference program's by a relative error of at most 0.0022.
Values may be sent and summed in bfloat16 or wider, within the bound.
A program may use at most 64 MiB of HBM per device.

```python
import math
import jax
import jax.numpy as jnp
import numpy as np
from jax import lax

BANDS = 8
TAYLOR = 4
SCALES = 5
PATCH = 48
TILE = 256
K_DEV = 128
CAP = 2
COMPS = 16384
NY = 4096
NX = 2048
N_TY = 16
N_TX = 8


def plant(array, key, least, top_value):
    longest = array.shape.index(max(array.shape))
    spots = []
    for shift in (0, 1):
        where = [jax.random.randint(jax.random.fold_in(key, axis), (), 0, length) for axis, length in enumerate(array.shape)]
        where[longest] = (where[longest] + shift) % array.shape[longest]
        spots.append(tuple(where))
    return array.at[spots[0]].set(least).at[spots[1]].set(top_value)


def levels(stream_key, dims, split, least, high):
    level, own = 1.0, jax.random.fold_in(stream_key, 6)
    for dim, shards_of in split:
        steps = jnp.exp(jax.random.uniform(jax.random.fold_in(own, dim), (shards_of,), jnp.float32, least / len(split), high / len(split)))
        level = level * jnp.repeat(steps, dims[dim] // shards_of).reshape([-1 if axis == dim else 1 for axis in range(len(dims))])
    return level


def shared_out(key, own, number, rows, amount, top, reach, skew):
    sequence = jax.random.permutation(key, amount)
    heavy_load, usual = load_shares(amount, rows * top, reach, skew, True), load_shares(amount, rows * top, reach, skew, False)
    places = jnp.arange(amount)

    def named(sizes, offset_by):
        used = int((sizes > 0).sum())
        fixed = max(1, used // 4)
        moved = fixed + (places - fixed + offset_by * (used - fixed)) % max(1, amount - fixed)
        return jnp.zeros((amount,), jnp.int32).at[sequence[jnp.where(places < fixed, places, moved)]].set(jnp.asarray(sizes, jnp.int32))

    sizes = jnp.where(number % 4 == 0, named(heavy_load, number // 4), named(usual, number - number // 4 - 1))
    mixed = jax.random.permutation(jax.random.fold_in(own, 3), amount)
    source_of, taker = mixed[0:amount // 2 * 2:2], mixed[1:amount // 2 * 2:2]
    room = jnp.minimum(sizes[source_of] - 1, reach - sizes[taker]) // 2
    room = jnp.where((source_of == sequence[0]) | (taker == sequence[0]) | (sizes[taker] == 0), 0, jnp.maximum(room, 0))
    moved = jax.random.randint(jax.random.fold_in(own, 4), (amount // 2,), 0, 1 << 20) % (room + 1)
    sizes = sizes.at[source_of].add(-moved).at[taker].add(moved)
    members = jnp.searchsorted(jnp.cumsum(sizes), jnp.arange(rows * top), side="right").astype(jnp.int32)
    table = members.reshape(top, rows).T
    table = table[jax.random.permutation(jax.random.fold_in(own, 1), rows)]
    offset_by = jax.random.randint(jax.random.fold_in(own, 2), (rows, 1), 0, top)
    return jnp.take_along_axis(table, (jnp.arange(top)[None, :] + offset_by) % top, axis=1)


def load_shares(number_of, total, most, slope, full):
    weights = [(1 << 20) // math.isqrt(grade ** slope) + 1 for grade in range(1, number_of + 1)]
    largest = most if full else min(most, max(-(-total // number_of), total * weights[0] // sum(weights)))
    least = 1 if total - largest >= number_of - 1 else 0
    counts, rest = [largest] + [least] * (number_of - 1), total - largest - least * (number_of - 1)
    while rest > 0:
        free = [i for i in range(1, number_of) if counts[i] < largest] or [i for i in range(1, number_of) if counts[i] < most]
        pool, left = sum([weights[i] for i in free]), rest
        for i in free:
            addition = min(most - counts[i], max(1, left * weights[i] // pool), rest)
            counts[i] = counts[i] + addition
            rest = rest - addition
    return np.array(counts)


def centred(key, dims, scale, limit, shards=(), kind=jnp.bfloat16):
    array = jax.random.normal(key, dims, jnp.float32) * scale
    if len(shards) > 0:
        array = levels(key, dims, shards, -0.22, 0.18) * array
    return jnp.clip(array, min=-limit, max=limit).astype(kind)


def setup_inputs(seed: int = 0) -> dict:
    seeds = jax.random.split(jax.random.key(seed), 8)
    dirty = centred(seeds[0], (BANDS, NY, NX), 1.0, 6.0, ((0, 4), (1, 16), (2, 8)), jnp.float32)
    psf = centred(seeds[1], (BANDS, TAYLOR * SCALES, PATCH * PATCH), 0.25, 4.0, ((0, 4),))
    comp_tile_keys = jax.random.split(jax.random.fold_in(seeds[2], 1), COMPS // K_DEV)
    comp_tile_turns = jax.random.permutation(jax.random.fold_in(seeds[2], 3), COMPS // K_DEV)
    comp_tile = jax.vmap(lambda own, number: shared_out(jax.random.fold_in(seeds[2], 2), own, number, K_DEV, N_TY * N_TX, 1, CAP, 2))(comp_tile_keys, comp_tile_turns).reshape((COMPS, 1))
    comp_offset = plant(jax.random.randint(seeds[3], (COMPS, 2), 0, TILE), jax.random.fold_in(seeds[3], 1), 0, TILE - 1).astype(jnp.int32)
    comp_scale = plant(jax.random.randint(seeds[4], (COMPS,), 0, SCALES), jax.random.fold_in(seeds[4], 1), 0, SCALES - 1).astype(jnp.int32)
    comp_amp = centred(seeds[5], (COMPS, TAYLOR), 1.0, 6.0, ((0, 128),), jnp.float32)
    fit_weight = centred(seeds[6], (BANDS, TAYLOR), 0.35, 5.0, ((0, 4),), jnp.float32)
    return {"dirty": dirty, "psf": psf, "comp_tile": comp_tile, "comp_offset": comp_offset, "comp_scale": comp_scale, "comp_amp": comp_amp, "fit_weight": fit_weight}


def reference(dirty, psf, comp_tile, comp_offset, comp_scale, comp_amp, fit_weight):
    tiles = comp_tile[:, 0]
    row_start = (tiles // N_TX) * TILE + comp_offset[:, 0]
    col_start = (tiles % N_TX) * TILE + comp_offset[:, 1]
    select = (comp_scale[:, None] == jnp.arange(SCALES, dtype=jnp.int32)[None, :]).astype(jnp.float32)
    coef = (comp_amp[:, :, None] * select[:, None, :]).reshape(COMPS, TAYLOR * SCALES)
    span = jnp.arange(PATCH, dtype=jnp.int32)
    rows = row_start[:, None, None] + span[None, :, None]
    cols = col_start[:, None, None] + span[None, None, :]

    def one_band(pair):
        psf_band, dirty_band = pair
        patches = jnp.dot(coef, psf_band.astype(jnp.float32), precision=lax.Precision.HIGHEST)
        patches = lax.optimization_barrier(patches.astype(jnp.bfloat16)).astype(jnp.float32)
        patches = patches.reshape(COMPS, PATCH, PATCH)
        model = jnp.zeros((NY + PATCH, NX + PATCH), jnp.float32).at[rows, cols].add(patches)
        return dirty_band - model[:NY, :NX]

    residual = lax.map(one_band, (psf, dirty))
    taylor_fit = jnp.einsum("bt,byx->tyx", fit_weight, residual, precision=lax.Precision.HIGHEST)
    return residual, taylor_fit
```

```python
import functools

import jax
import jax.numpy as jnp
from jax import lax
from jax.experimental import pallas as pl
from jax.experimental.pallas import tpu as pltpu
from jax.sharding import PartitionSpec as P

TAYLOR = 4
SCALES = 5
PATCH = 48
ROWS_K = TAYLOR * SCALES
PAD_K = 24
HALF = PATCH // 2
WIDE = HALF * PATCH
SIDE = 256
SLOTS = 8
WORDS = 8
ROW_BASE = 48
COL_BASE = 64
BLOCKS = 6
CANVAS = 352
GROUP = 8
MESH = pl.DeviceIdType.MESH


def sends_of_tiles(tile, off, scale, amp, n_ty, n_tx):
    count = tile.shape[1]
    tiles, n_yp = n_ty * n_tx, n_ty // 2
    comp_y = lax.shift_right_logical(tile, n_tx.bit_length() - 1)
    comp_x = lax.bitwise_and(tile, n_tx - 1)
    over_r = (off[0:1] + PATCH > SIDE).astype(jnp.int32)
    over_c = (off[1:2] + PATCH > SIDE).astype(jnp.int32)
    dest = lax.broadcasted_iota(jnp.int32, (tiles, count), 0)
    half = tiles // 2
    bits = n_yp.bit_length() - 1
    core = lax.shift_right_logical(dest, half.bit_length() - 1)
    inner = lax.bitwise_and(dest, half - 1)
    dest_x = lax.shift_right_logical(inner, bits)
    dest_y = 2 * lax.bitwise_and(inner, n_yp - 1) + core
    down, right = dest_y - comp_y, dest_x - comp_x
    touches = ((down == 0) | ((down == 1) & (over_r == 1))) & (
        (right == 0) | ((right == 1) & (over_c == 1))
    )
    before = (
        lax.broadcasted_iota(jnp.int32, (count, count), 0)
        < lax.broadcasted_iota(jnp.int32, (count, count), 1)
    ).astype(jnp.float32)
    rank = jnp.dot(
        jnp.where(touches, 1.0, 0.0).astype(jnp.bfloat16),
        before.astype(jnp.bfloat16),
        preferred_element_type=jnp.float32,
    )
    rank = jnp.where(touches, rank, -1.0)
    chosen = jnp.concatenate(
        [jnp.where(rank == float(k), 1.0, 0.0).astype(jnp.bfloat16) for k in range(SLOTS)], axis=1
    )
    rows = (comp_y * SIDE + off[0:1]).astype(jnp.float32)
    cols = (comp_x * SIDE + off[1:2]).astype(jnp.float32)
    record = jnp.concatenate(
        [rows, cols, scale.astype(jnp.float32), jnp.ones((1, count), jnp.float32), amp], axis=0
    )
    high = record.astype(jnp.bfloat16).astype(jnp.float32)
    rest = record - high
    middle = rest.astype(jnp.bfloat16).astype(jnp.float32)
    low = rest - middle
    place = lax.shift_right_logical(
        lax.broadcasted_iota(jnp.int32, (SLOTS * WORDS, count), 0), 3
    )
    parts = []
    for part in (high, middle, low):
        tall = jnp.concatenate([part] * SLOTS, axis=0)
        parts.append(
            jnp.concatenate([jnp.where(place == k, tall, 0.0) for k in range(SLOTS)], axis=1)
        )
    parts.append(jnp.zeros_like(parts[0]))
    table = jnp.concatenate(parts, axis=0).astype(jnp.bfloat16)
    found = lax.dot_general(
        chosen, table, (((1,), (1,)), ((), ())), preferred_element_type=jnp.float32
    )
    found = found[:, :128] + found[:, 128:]
    found = found + pltpu.roll(found, 64, 1)
    lane = lax.broadcasted_iota(jnp.int32, (half, 128), 1)
    return jnp.where(lane < 64, found[:half], found[half:])


def unrolled(first, last, lane, step):
    tile, shift = divmod(step * PATCH, 128)
    out = []
    for table, base in ((first, 0), (last, 64)):
        value = table(tile)
        if shift + PATCH > 128:
            value = jnp.where(lane >= shift, value, table(tile + 1))
        turn = (base - shift) % 128
        out.append(pltpu.roll(value, turn, 1) if turn else value)
    return jnp.where(
        lane < PATCH, out[0], jnp.where((lane >= 64) & (lane < 64 + PATCH), out[1], 0.0)
    )


def exchange_kernel(
    n_band, n_ty, n_tx,
    tile_ref, off_ref, scale_ref, amp_ref, weight_ref, dirty_ref, psf_ref,
    place_ref, value_ref, list_ref, table_ref, taylor_table_ref, fit_ref,
    send, cross, got, psf, fit_send, fit_got, tab_send, tab_own, tab_got,
    x_send, x_recv, y_send, y_recv, b_send, b_recv, own_sem, pair_send, pair_recv,
):
    me_b, me_y, me_x = lax.axis_index("band"), lax.axis_index("ty"), lax.axis_index("tx")
    barrier = pltpu.get_barrier_semaphore()
    along_x = [lax.rem(me_x + o, n_tx) for o in range(1, n_tx)]
    along_y = [lax.rem(me_y + o, n_ty) for o in range(1, n_ty)]
    along_b = [lax.rem(me_b + o, n_band) for o in range(1, n_band)]
    partners = (
        [(me_b, me_y, x) for x in along_x]
        + [(me_b, y, me_x) for y in along_y]
        + [(b, me_y, me_x) for b in along_b]
    )
    for partner in partners:
        pl.semaphore_signal(barrier, inc=1, device_id=partner, device_id_type=MESH)

    records = sends_of_tiles(tile_ref[...], off_ref[...], scale_ref[...], amp_ref[...], n_ty, n_tx)
    n_yp = n_ty // 2
    for x in range(n_tx):
        send[x] = records[x * n_yp:(x + 1) * n_yp]

    for b in range(2):
        psf[b, 0:ROWS_K, :] = psf_ref[:, b, :].astype(jnp.float32)
        psf[b, ROWS_K:PAD_K, :] = jnp.zeros((PAD_K - ROWS_K, 2 * WIDE), jnp.float32)
    core = lax.rem(me_y, 2)
    mine = [
        jnp.where(core == 1, psf[b, :, WIDE:2 * WIDE], psf[b, :, 0:WIDE]) for b in range(2)
    ]
    for o in range(1, n_band):
        w0, w1 = weight_ref[0, along_b[o - 1]], weight_ref[1, along_b[o - 1]]
        tab_send[o - 1] = w0 * mine[0] + w1 * mine[1]
        fit_send[o - 1] = (w0 * dirty_ref[0] + w1 * dirty_ref[1]).astype(jnp.bfloat16)

    pl.semaphore_wait(barrier, len(partners))

    stage_x = []
    for o, x in enumerate(along_x):
        copy = pltpu.make_async_remote_copy(
            src_ref=send.at[x], dst_ref=cross.at[:, me_x, :],
            send_sem=x_send.at[o], recv_sem=x_recv.at[o],
            device_id=(me_b, me_y, x), device_id_type=MESH,
        )
        copy.start()
        stage_x.append(copy)
    own = pltpu.make_async_copy(send.at[me_x], cross.at[:, me_x, :], own_sem.at[0])
    own.start()
    stage_t, stage_f = [], []
    for source, target, which, copies in (
        (tab_send, tab_got, 0, stage_t), (fit_send, fit_got, 1, stage_f)
    ):
        for o, b in enumerate(along_b):
            copy = pltpu.make_async_remote_copy(
                src_ref=source.at[o], dst_ref=target.at[o],
                send_sem=b_send.at[which, o], recv_sem=b_recv.at[which, o],
                device_id=(b, me_y, me_x), device_id_type=MESH,
            )
            copy.start()
            copies.append(copy)

    w0, w1 = weight_ref[0, me_b], weight_ref[1, me_b]
    tab_own[core] = w0 * mine[0] + w1 * mine[1]
    lane24 = lax.broadcasted_iota(jnp.int32, (PAD_K, 128), 1)

    def piece(ref, half):
        return lambda t: ref[:, half * WIDE + t * 128:half * WIDE + (t + 1) * 128]

    def band_table(half):
        first, last = piece(psf.at[0], half), piece(psf.at[1], half)
        for step in range(HALF):
            table_ref[pl.ds(half * HALF + step, PAD_K, stride=PATCH), :] = unrolled(
                first, last, lane24, step
            )

    band_table(0)

    own.wait()
    for copy in stage_x:
        copy.wait_recv()
    stage_y = []
    for o, y in enumerate(along_y):
        copy = pltpu.make_async_remote_copy(
            src_ref=cross.at[y // 2], dst_ref=got.at[me_y],
            send_sem=y_send.at[o], recv_sem=y_recv.at[o],
            device_id=(me_b, y, me_x), device_id_type=MESH,
        )
        copy.start()
        stage_y.append(copy)
    own = pltpu.make_async_copy(cross.at[me_y // 2], got.at[me_y], own_sem.at[1])
    own.start()

    for copy in stage_t:
        copy.wait_recv()
    for o in range(n_band - 1):
        tab_own[core] += tab_got[o]
    band_table(1)
    pair = pltpu.make_async_remote_copy(
        src_ref=tab_own.at[core], dst_ref=tab_own.at[core],
        send_sem=pair_send.at[0], recv_sem=pair_recv.at[0],
        device_id=(me_b, me_y + 1 - 2 * core, me_x), device_id_type=MESH,
    )
    pair.start()

    own.wait()
    for copy in stage_y:
        copy.wait_recv()
    sources = n_ty * n_tx
    slots = jnp.concatenate([got[y] for y in range(n_ty)], axis=0)
    slots = jnp.where(lax.rem(me_y, 2) == 1, pltpu.roll(slots, 64, 1), slots)
    lane = lax.broadcasted_iota(jnp.int32, (sources, 128), 1)
    word = lax.bitwise_and(lane, WORDS - 1)
    move_r = (ROW_BASE - me_y * SIDE).astype(jnp.float32)
    move_c = (COL_BASE - me_x * SIDE).astype(jnp.float32)
    row = jnp.clip(slots + move_r, 0.0, float(ROW_BASE + SIDE)).astype(jnp.int32)
    col = jnp.clip(
        pltpu.roll(slots, 127, 1) + move_c, 0.0, float(COL_BASE + SIDE)
    ).astype(jnp.int32)
    scale = jnp.clip(pltpu.roll(slots, 126, 1), 0.0, float(SCALES)).astype(jnp.int32)
    place = row + lax.shift_right_logical(col, 6) * CANVAS
    place = place + lax.shift_left(lax.bitwise_and(col, 63), 12) + scale * (HALF << 18)
    lower = lax.broadcasted_iota(jnp.int32, (sources // 2, 128), 1) < 64
    for ref, value in ((place_ref, place), (value_ref, slots)):
        ref[0:sources // 2] = jnp.where(
            lower, value[:sources // 2], pltpu.roll(value[sources // 2:], 64, 1)
        )
        ref[sources // 2:sources // 2 + 8] = jnp.zeros((8, 128), ref.dtype)
    used = jnp.sum(
        jnp.where((word == 3) & (lane < 64), slots, 0.0), axis=1, keepdims=True
    )
    used = jnp.broadcast_to(used, (sources, 128))
    earlier = (
        lax.broadcasted_iota(jnp.int32, (sources, sources), 1)
        < lax.broadcasted_iota(jnp.int32, (sources, sources), 0)
    ).astype(jnp.float32).astype(jnp.bfloat16)
    start = jnp.dot(earlier, used.astype(jnp.bfloat16), preferred_element_type=jnp.float32)
    end = start + used
    lists = max(1, sources * SLOTS // 128)
    for i in range(lists):
        order = (lane + i * 128).astype(jnp.float32)
        source = jnp.sum(jnp.where(end <= order, 1.0, 0.0), axis=0, keepdims=True)
        base = jnp.max(jnp.where(start <= order, start, 0.0), axis=0, keepdims=True)
        upper = jnp.where(source >= float(sources // 2), 1.0, 0.0)
        index = (source - upper * (sources // 2)) * 128.0 + upper * 64.0
        index = index + (order[0:1] - base) * WORDS
        index = jnp.where(source < float(sources), index, float(sources // 2 * 128))
        list_ref[i:i + 1, :] = index.astype(jnp.int32)
    list_ref[lists:lists + 1, :] = end[sources - 1:sources].astype(jnp.int32)

    pair.wait_recv()
    first, last = piece(tab_own.at[0], 0), piece(tab_own.at[1], 0)
    for step in range(HALF):
        taylor_table_ref[pl.ds(step, PAD_K, stride=HALF), :] = unrolled(first, last, lane24, step)

    fit_ref[...] = w0 * dirty_ref[0] + w1 * dirty_ref[1]
    for copy in stage_f:
        copy.wait_recv()
    for o in range(n_band - 1):
        fit_ref[...] += fit_got[o].astype(jnp.float32)
    for copy in stage_x + stage_y + stage_t + stage_f + [pair]:
        copy.wait_send()


def render_kernel(
    place_ref, amp_ref, list_ref, table_ref, taylor_table_ref, dirty_ref, fit_ref,
    residual_ref, taylor_ref, canvas, spill, canvas_t, spill_t,
):
    for block in range(BLOCKS - 1):
        for ref, used, first in (
            (canvas, block > 0, ROW_BASE), (spill, block < 4, ROW_BASE),
            (canvas_t, block > 0, ROW_BASE - HALF), (spill_t, block < 4, ROW_BASE - HALF),
        ):
            if used:
                rows = ROW_BASE + SIDE - first
                ref[pl.ds(block * CANVAS + first, rows), :] = jnp.zeros((rows, 128), jnp.float32)
    half_lane = lax.bitwise_and(lax.broadcasted_iota(jnp.int32, (HALF, 128), 1), 63)
    count = list_ref[list_ref.shape[0] - 1024]

    def step(index, carry):
        for g in range(GROUP):
            slot = list_ref[index * GROUP + g]
            packed = place_ref[slot]
            amps = [amp_ref[slot + 4 + t] for t in range(TAYLOR)]
            first = lax.bitwise_and(packed, 4095)
            shift = lax.bitwise_and(lax.shift_right_logical(packed, 12), 63)
            base = lax.shift_right_logical(packed, 18)
            low = pl.multiple_of(base, HALF)
            high = pl.multiple_of(2 * base, PATCH)
            patch = fit = None
            for t in range(TAYLOR):
                term = amps[t] * table_ref[pl.ds(high + t * SCALES * PATCH, PATCH), :]
                patch = term if t == 0 else patch + term
                term = amps[t] * taylor_table_ref[pl.ds(low + t * SCALES * HALF, HALF), :]
                fit = term if t == 0 else fit + term
            patch = patch.astype(jnp.bfloat16).astype(jnp.float32)
            keep = half_lane >= shift
            other = jnp.logical_not(keep)
            sums = []
            for value, inside, beyond, at in (
                (patch[:HALF], canvas, spill, first),
                (patch[HALF:], canvas, spill, first + HALF),
                (fit, canvas_t, spill_t, first),
            ):
                value = pltpu.roll(value, shift, 1)
                for mask, target in ((keep, inside), (other, beyond)):
                    here = target.at[pl.ds(at, HALF), :]
                    sums.append((here, here[...] + value, mask))
            for here, value, mask in sums:
                pltpu.store(here, value, mask=mask)
        return carry

    lax.fori_loop(0, (count + GROUP - 1) // GROUP, step, 0)

    rows = 64
    lower = lax.broadcasted_iota(jnp.int32, (rows, 128), 1) < 64

    def mix(low, high):
        return jnp.where(lower, low, high)

    for r in range(0, SIDE, rows):
        for j in range(2):

            def at(ref, block, first):
                start = (block + 2 * j) * CANVAS + ROW_BASE + r + first
                return ref[pl.ds(start, rows), :]

            c1, c2 = at(canvas, 1, 0), at(canvas, 2, 0)
            s1, s2 = at(spill, 0, 0), at(spill, 1, 0)
            here = (slice(r, r + rows), slice(j * 128, j * 128 + 128))
            model = mix(c1, s2) + pltpu.roll(mix(c2, s1), 64, 1)
            residual_ref[(0,) + here] = dirty_ref[(0,) + here] - model
            model = mix(s1, c2) + pltpu.roll(mix(s2, c1), 64, 1)
            residual_ref[(1,) + here] = dirty_ref[(1,) + here] - model
            straight = mix(
                at(canvas_t, 1, 0) + at(spill_t, 0, -HALF), at(canvas_t, 2, -HALF) + at(spill_t, 1, 0)
            )
            crossed = mix(
                at(canvas_t, 2, 0) + at(spill_t, 1, -HALF), at(canvas_t, 1, -HALF) + at(spill_t, 0, 0)
            )
            taylor_ref[here] = fit_ref[here] - (straight + pltpu.roll(crossed, 64, 1))


def per_device(dirty, psf, comp_tile, comp_offset, comp_scale, comp_amp, fit_weight):
    n_band, n_ty, n_tx = (lax.axis_size(a) for a in ("band", "ty", "tx"))
    sources = n_ty * n_tx
    lists = max(1, sources * SLOTS // 128)
    n_yp = n_ty // 2
    vmem = pl.BlockSpec(memory_space=pltpu.VMEM)
    smem = pl.BlockSpec(memory_space=pltpu.SMEM)
    dma = pltpu.SemaphoreType.DMA
    f32, bf16 = jnp.float32, jnp.bfloat16
    place, value, order, table, taylor_table, fit = pl.pallas_call(
        functools.partial(exchange_kernel, n_band, n_ty, n_tx),
        out_shape=(
            jax.ShapeDtypeStruct((sources // 2 + 8, 128), jnp.int32),
            jax.ShapeDtypeStruct((sources // 2 + 8, 128), f32),
            jax.ShapeDtypeStruct((lists + 8, 128), jnp.int32),
            jax.ShapeDtypeStruct((PAD_K * PATCH, 128), f32),
            jax.ShapeDtypeStruct((PAD_K * HALF, 128), f32),
            jax.ShapeDtypeStruct((SIDE, SIDE), f32),
        ),
        in_specs=[vmem] * 4 + [smem] + [vmem] * 2,
        out_specs=(vmem,) * 6,
        scratch_shapes=[
            pltpu.VMEM((n_tx, n_yp, 128), f32),
            pltpu.VMEM((n_yp, n_tx, 128), f32),
            pltpu.VMEM((n_ty, n_tx, 128), f32),
            pltpu.VMEM((2, PAD_K, 2 * WIDE), f32),
            pltpu.VMEM((n_band - 1, SIDE, SIDE), bf16),
            pltpu.VMEM((n_band - 1, SIDE, SIDE), bf16),
            pltpu.VMEM((n_band - 1, PAD_K, WIDE), f32),
            pltpu.VMEM((2, PAD_K, WIDE), f32),
            pltpu.VMEM((n_band - 1, PAD_K, WIDE), f32),
            dma((n_tx - 1,)), dma((n_tx - 1,)),
            dma((n_ty - 1,)), dma((n_ty - 1,)),
            dma((2, n_band - 1)), dma((2, n_band - 1)),
            dma((2,)), dma((1,)), dma((1,)),
        ],
        compiler_params=pltpu.CompilerParams(
            collective_id=0, has_side_effects=True, vmem_limit_bytes=24 * 1024 * 1024
        ),
    )(
        comp_tile.T, comp_offset.T, comp_scale[None, :], comp_amp.T, fit_weight, dirty,
        psf.transpose(1, 0, 2),
    )
    residual, taylor = pl.pallas_call(
        render_kernel,
        out_shape=(
            jax.ShapeDtypeStruct((2, SIDE, SIDE), f32),
            jax.ShapeDtypeStruct((SIDE, SIDE), f32),
        ),
        in_specs=[smem] * 3 + [vmem] * 4,
        out_specs=(vmem,) * 2,
        scratch_shapes=[
            pltpu.VMEM(((BLOCKS - 1) * CANVAS, 128), f32) for _ in range(4)
        ],
        compiler_params=pltpu.CompilerParams(vmem_limit_bytes=24 * 1024 * 1024),
    )(
        place.reshape(-1), value.reshape(-1), order.reshape(-1), table, taylor_table, dirty, fit,
    )
    return residual, taylor[None]


def solution(mesh):
    return jax.shard_map(
        per_device,
        mesh=mesh,
        in_specs=(
            P("band", "ty", "tx"),
            P("band", None, None),
            P(("ty", "tx"), None),
            P(("ty", "tx"), None),
            P(("ty", "tx")),
            P(("ty", "tx"), None),
            P("band", None),
        ),
        out_specs=(P("band", "ty", "tx"), P("band", "ty", "tx")),
        check_vma=False,
    )
```

```python
import functools

import jax
import jax.numpy as jnp
from jax import lax
from jax.experimental import pallas as pl
from jax.experimental.pallas import tpu as pltpu
from jax.sharding import PartitionSpec as P

TAYLOR = 4
SCALES = 5
PATCH = 48
ROWS_K = TAYLOR * SCALES
PAD_K = 24
HALF = PATCH // 2
WIDE = HALF * PATCH
SIDE = 256
SLOTS = 8
WORDS = 8
ROW_BASE = 48
COL_BASE = 64
BLOCKS = 6
CANVAS = 352
GROUP = 8
MESH = pl.DeviceIdType.MESH


def sends_of_tiles(tile, off, scale, amp, n_ty, n_tx):
    count = tile.shape[1]
    tiles, n_yp = n_ty * n_tx, n_ty // 2
    comp_y = lax.shift_right_logical(tile, n_tx.bit_length() - 1)
    comp_x = lax.bitwise_and(tile, n_tx - 1)
    over_r = (off[0:1] + PATCH > SIDE).astype(jnp.int32)
    over_c = (off[1:2] + PATCH > SIDE).astype(jnp.int32)
    dest = lax.broadcasted_iota(jnp.int32, (tiles, count), 0)
    half = tiles // 2
    bits = n_yp.bit_length() - 1
    core = lax.shift_right_logical(dest, half.bit_length() - 1)
    inner = lax.bitwise_and(dest, half - 1)
    dest_x = lax.shift_right_logical(inner, bits)
    dest_y = 2 * lax.bitwise_and(inner, n_yp - 1) + core
    down, right = dest_y - comp_y, dest_x - comp_x
    touches = ((down == 0) | ((down == 1) & (over_r == 1))) & (
        (right == 0) | ((right == 1) & (over_c == 1))
    )
    before = (
        lax.broadcasted_iota(jnp.int32, (count, count), 0)
        < lax.broadcasted_iota(jnp.int32, (count, count), 1)
    ).astype(jnp.float32)
    rank = jnp.dot(
        jnp.where(touches, 1.0, 0.0).astype(jnp.bfloat16),
        before.astype(jnp.bfloat16),
        preferred_element_type=jnp.float32,
    )
    rank = jnp.where(touches, rank, -1.0)
    chosen = jnp.concatenate(
        [jnp.where(rank == float(k), 1.0, 0.0).astype(jnp.bfloat16) for k in range(SLOTS)], axis=1
    )
    rows = (comp_y * SIDE + off[0:1]).astype(jnp.float32)
    cols = (comp_x * SIDE + off[1:2]).astype(jnp.float32)
    record = jnp.concatenate(
        [rows, cols, scale.astype(jnp.float32), jnp.ones((1, count), jnp.float32), amp], axis=0
    )
    high = record.astype(jnp.bfloat16).astype(jnp.float32)
    rest = record - high
    middle = rest.astype(jnp.bfloat16).astype(jnp.float32)
    low = rest - middle
    place = lax.shift_right_logical(
        lax.broadcasted_iota(jnp.int32, (SLOTS * WORDS, count), 0), 3
    )
    parts = []
    for part in (high, middle, low):
        tall = jnp.concatenate([part] * SLOTS, axis=0)
        parts.append(
            jnp.concatenate([jnp.where(place == k, tall, 0.0) for k in range(SLOTS)], axis=1)
        )
    parts.append(jnp.zeros_like(parts[0]))
    table = jnp.concatenate(parts, axis=0).astype(jnp.bfloat16)
    found = lax.dot_general(
        chosen, table, (((1,), (1,)), ((), ())), preferred_element_type=jnp.float32
    )
    found = found[:, :128] + found[:, 128:]
    found = found + pltpu.roll(found, 64, 1)
    lane = lax.broadcasted_iota(jnp.int32, (half, 128), 1)
    return jnp.where(lane < 64, found[:half], found[half:])


def unrolled(first, last, lane, step):
    tile, shift = divmod(step * PATCH, 128)
    out = []
    for table, base in ((first, 0), (last, 64)):
        value = table(tile)
        if shift + PATCH > 128:
            value = jnp.where(lane >= shift, value, table(tile + 1))
        turn = (base - shift) % 128
        out.append(pltpu.roll(value, turn, 1) if turn else value)
    return jnp.where(
        lane < PATCH, out[0], jnp.where((lane >= 64) & (lane < 64 + PATCH), out[1], 0.0)
    )


def exchange_kernel(
    n_band, n_ty, n_tx,
    tile_ref, off_ref, scale_ref, amp_ref, weight_ref, dirty_hbm, psf_hbm,
    value_ref, list_ref, table_ref, taylor_table_ref, fit_ref,
    send, cross, got, dirty_ref, psf_ref, psf, fit_send, fit_got, tab_send, tab_own, tab_got,
    x_send, x_recv, y_send, y_recv, b_send, b_recv, own_sem, pair_send, pair_recv, load_sem,
):
    loads = [
        pltpu.make_async_copy(psf_hbm, psf_ref, load_sem.at[0]),
        pltpu.make_async_copy(dirty_hbm, dirty_ref, load_sem.at[1]),
    ]
    for load in loads:
        load.start()
    me_b, me_y, me_x = lax.axis_index("band"), lax.axis_index("ty"), lax.axis_index("tx")
    barrier = pltpu.get_barrier_semaphore()
    along_x = [lax.rem(me_x + o, n_tx) for o in range(1, n_tx)]
    along_y = [lax.rem(me_y + o, n_ty) for o in range(1, n_ty)]
    along_b = [lax.rem(me_b + o, n_band) for o in range(1, n_band)]
    partners = (
        [(me_b, me_y, x) for x in along_x]
        + [(me_b, y, me_x) for y in along_y]
        + [(b, me_y, me_x) for b in along_b]
    )
    for partner in partners:
        pl.semaphore_signal(barrier, inc=1, device_id=partner, device_id_type=MESH)

    records = sends_of_tiles(tile_ref[...], off_ref[...], scale_ref[...], amp_ref[...], n_ty, n_tx)
    n_yp = n_ty // 2
    for x in range(n_tx):
        send[x] = records[x * n_yp:(x + 1) * n_yp]

    pl.semaphore_wait(barrier, len(partners))

    stage_x = []
    for o, x in enumerate(along_x):
        copy = pltpu.make_async_remote_copy(
            src_ref=send.at[x], dst_ref=cross.at[:, me_x, :],
            send_sem=x_send.at[o], recv_sem=x_recv.at[o],
            device_id=(me_b, me_y, x), device_id_type=MESH,
        )
        copy.start()
        stage_x.append(copy)
    own = pltpu.make_async_copy(send.at[me_x], cross.at[:, me_x, :], own_sem.at[0])
    own.start()
    for load in loads:
        load.wait()
    for b in range(2):
        psf[b, 0:ROWS_K, :] = psf_ref[:, b, :].astype(jnp.float32)
        psf[b, ROWS_K:PAD_K, :] = jnp.zeros((PAD_K - ROWS_K, 2 * WIDE), jnp.float32)
    core = lax.rem(me_y, 2)
    mine = [
        jnp.where(core == 1, psf[b, :, WIDE:2 * WIDE], psf[b, :, 0:WIDE]) for b in range(2)
    ]
    for o in range(1, n_band):
        w0, w1 = weight_ref[0, along_b[o - 1]], weight_ref[1, along_b[o - 1]]
        tab_send[o - 1] = w0 * mine[0] + w1 * mine[1]
        fit_send[o - 1] = (w0 * dirty_ref[0] + w1 * dirty_ref[1]).astype(jnp.bfloat16)

    w0, w1 = weight_ref[0, me_b], weight_ref[1, me_b]
    tab_own[core] = w0 * mine[0] + w1 * mine[1]
    lane24 = lax.broadcasted_iota(jnp.int32, (PAD_K, 128), 1)

    def piece(ref, half):
        return lambda t: ref[:, half * WIDE + t * 128:half * WIDE + (t + 1) * 128]

    def band_table(half):
        first, last = piece(psf.at[0], half), piece(psf.at[1], half)
        for step in range(HALF):
            table_ref[pl.ds(half * HALF + step, PAD_K, stride=PATCH), :] = unrolled(
                first, last, lane24, step
            )

    band_table(0)

    stage_t, stage_f = [], []
    for source, target, which, copies in (
        (tab_send, tab_got, 0, stage_t), (fit_send, fit_got, 1, stage_f)
    ):
        for o, b in enumerate(along_b):
            copy = pltpu.make_async_remote_copy(
                src_ref=source.at[o], dst_ref=target.at[o],
                send_sem=b_send.at[which, o], recv_sem=b_recv.at[which, o],
                device_id=(b, me_y, me_x), device_id_type=MESH,
            )
            copy.start()
            copies.append(copy)

    own.wait()
    for copy in stage_x:
        copy.wait_recv()
    stage_y = []
    for o, y in enumerate(along_y):
        copy = pltpu.make_async_remote_copy(
            src_ref=cross.at[y // 2], dst_ref=got.at[me_y],
            send_sem=y_send.at[o], recv_sem=y_recv.at[o],
            device_id=(me_b, y, me_x), device_id_type=MESH,
        )
        copy.start()
        stage_y.append(copy)
    own = pltpu.make_async_copy(cross.at[me_y // 2], got.at[me_y], own_sem.at[1])
    own.start()

    for copy in stage_t:
        copy.wait_recv()
    for o in range(n_band - 1):
        tab_own[core] += tab_got[o]
    band_table(1)
    pair = pltpu.make_async_remote_copy(
        src_ref=tab_own.at[core], dst_ref=tab_own.at[core],
        send_sem=pair_send.at[0], recv_sem=pair_recv.at[0],
        device_id=(me_b, me_y + 1 - 2 * core, me_x), device_id_type=MESH,
    )
    pair.start()

    own.wait()
    for copy in stage_y:
        copy.wait_recv()
    sources = n_ty * n_tx
    slots = jnp.concatenate([got[y] for y in range(n_ty)], axis=0)
    slots = jnp.where(lax.rem(me_y, 2) == 1, pltpu.roll(slots, 64, 1), slots)
    lane = lax.broadcasted_iota(jnp.int32, (sources, 128), 1)
    word = lax.bitwise_and(lane, WORDS - 1)
    move_r = (ROW_BASE - me_y * SIDE).astype(jnp.float32)
    move_c = (COL_BASE - me_x * SIDE).astype(jnp.float32)
    row = jnp.clip(slots + move_r, 0.0, float(ROW_BASE + SIDE)).astype(jnp.int32)
    col = jnp.clip(
        pltpu.roll(slots, 127, 1) + move_c, 0.0, float(COL_BASE + SIDE)
    ).astype(jnp.int32)
    scale = jnp.clip(pltpu.roll(slots, 126, 1), 0.0, float(SCALES)).astype(jnp.int32)
    place = row + lax.shift_right_logical(col, 6) * CANVAS
    place = place + lax.shift_left(lax.bitwise_and(col, 63), 11) + lax.shift_left(scale, 17)
    value = jnp.where(word == 0, place.astype(jnp.float32), slots)
    lower = lax.broadcasted_iota(jnp.int32, (sources // 2, 128), 1) < 64
    value_ref[0:sources // 2] = jnp.where(
        lower, value[:sources // 2], pltpu.roll(value[sources // 2:], 64, 1)
    )
    value_ref[sources // 2:sources // 2 + 8] = jnp.zeros((8, 128), jnp.float32)
    used = jnp.sum(
        jnp.where((word == 3) & (lane < 64), slots, 0.0), axis=1, keepdims=True
    )
    used = jnp.broadcast_to(used, (sources, 128))
    earlier = (
        lax.broadcasted_iota(jnp.int32, (sources, sources), 1)
        < lax.broadcasted_iota(jnp.int32, (sources, sources), 0)
    ).astype(jnp.float32).astype(jnp.bfloat16)
    start = jnp.dot(earlier, used.astype(jnp.bfloat16), preferred_element_type=jnp.float32)
    end = start + used
    lists = max(1, sources * SLOTS // 128)
    for i in range(lists):
        order = (lane + i * 128).astype(jnp.float32)
        source = jnp.sum(jnp.where(end <= order, 1.0, 0.0), axis=0, keepdims=True)
        base = jnp.max(jnp.where(start <= order, start, 0.0), axis=0, keepdims=True)
        upper = jnp.where(source >= float(sources // 2), 1.0, 0.0)
        index = (source - upper * (sources // 2)) * 128.0 + upper * 64.0
        index = index + (order[0:1] - base) * WORDS
        index = jnp.where(source < float(sources), index, float(sources // 2 * 128))
        list_ref[i:i + 1, :] = index.astype(jnp.int32)
    list_ref[lists:lists + 1, :] = end[sources - 1:sources].astype(jnp.int32)

    pair.wait_recv()
    first, last = piece(tab_own.at[0], 0), piece(tab_own.at[1], 0)
    for step in range(HALF):
        taylor_table_ref[pl.ds(step, PAD_K, stride=HALF), :] = unrolled(first, last, lane24, step)

    fit_ref[...] = w0 * dirty_ref[0] + w1 * dirty_ref[1]
    for copy in stage_f:
        copy.wait_recv()
    for o in range(n_band - 1):
        fit_ref[...] += fit_got[o].astype(jnp.float32)
    for copy in stage_x + stage_y + stage_t + stage_f + [pair]:
        copy.wait_send()


def render_kernel(
    value_ref, order_ref, table_ref, taylor_table_ref, dirty_ref, fit_ref,
    residual_hbm, taylor_hbm,
    canvas, spill, canvas_t, spill_t, residual_ref, taylor_ref, amp_ref, list_ref, sems, out_sems,
):
    fetches = [
        pltpu.make_async_copy(value_ref, amp_ref, sems.at[0]),
        pltpu.make_async_copy(order_ref, list_ref, sems.at[1]),
    ]
    for fetch in fetches:
        fetch.start()
    for block in range(BLOCKS - 1):
        for ref, used, first in (
            (canvas, block > 0, ROW_BASE), (spill, block < 4, ROW_BASE),
            (canvas_t, block > 0, ROW_BASE - HALF), (spill_t, block < 4, ROW_BASE - HALF),
        ):
            if used:
                rows = ROW_BASE + SIDE - first
                ref[pl.ds(block * CANVAS + first, rows), :] = jnp.zeros((rows, 128), jnp.float32)
    for fetch in fetches:
        fetch.wait()
    half_lane = lax.bitwise_and(lax.broadcasted_iota(jnp.int32, (HALF, 128), 1), 63)
    count = list_ref[list_ref.shape[0] - 1024]

    def step(index, carry):
        for g in range(GROUP):
            slot = list_ref[index * GROUP + g]
            packed = amp_ref[slot].astype(jnp.int32)
            amps = [amp_ref[slot + 4 + t] for t in range(TAYLOR)]
            first = lax.bitwise_and(packed, 2047)
            shift = lax.bitwise_and(lax.shift_right_logical(packed, 11), 63)
            base = lax.shift_right_logical(packed, 17) * HALF
            low = pl.multiple_of(base, HALF)
            high = pl.multiple_of(2 * base, PATCH)
            patch = fit = None
            for t in range(TAYLOR):
                term = amps[t] * table_ref[pl.ds(high + t * SCALES * PATCH, PATCH), :]
                patch = term if t == 0 else patch + term
                term = amps[t] * taylor_table_ref[pl.ds(low + t * SCALES * HALF, HALF), :]
                fit = term if t == 0 else fit + term
            patch = patch.astype(jnp.bfloat16).astype(jnp.float32)
            keep = half_lane >= shift
            other = jnp.logical_not(keep)
            sums = []
            for value, inside, beyond, at in (
                (patch[:HALF], canvas, spill, first),
                (patch[HALF:], canvas, spill, first + HALF),
                (fit, canvas_t, spill_t, first),
            ):
                value = pltpu.roll(value, shift, 1)
                for mask, target in ((keep, inside), (other, beyond)):
                    here = target.at[pl.ds(at, HALF), :]
                    sums.append((here, here[...] + value, mask))
            for here, value, mask in sums:
                pltpu.store(here, value, mask=mask)
        return carry

    lax.fori_loop(0, (count + GROUP - 1) // GROUP, step, 0)

    rows = 64
    lower = lax.broadcasted_iota(jnp.int32, (rows, 128), 1) < 64

    def mix(low, high):
        return jnp.where(lower, low, high)

    copies = []
    for r in range(0, SIDE, rows):
        for j in range(2):

            def at(ref, block, first):
                start = (block + 2 * j) * CANVAS + ROW_BASE + r + first
                return ref[pl.ds(start, rows), :]

            c1, c2 = at(canvas, 1, 0), at(canvas, 2, 0)
            s1, s2 = at(spill, 0, 0), at(spill, 1, 0)
            here = (slice(r, r + rows), slice(j * 128, j * 128 + 128))
            model = mix(c1, s2) + pltpu.roll(mix(c2, s1), 64, 1)
            residual_ref[(0,) + here] = dirty_ref[(0,) + here] - model
            model = mix(s1, c2) + pltpu.roll(mix(s2, c1), 64, 1)
            residual_ref[(1,) + here] = dirty_ref[(1,) + here] - model
            straight = mix(
                at(canvas_t, 1, 0) + at(spill_t, 0, -HALF), at(canvas_t, 2, -HALF) + at(spill_t, 1, 0)
            )
            crossed = mix(
                at(canvas_t, 2, 0) + at(spill_t, 1, -HALF), at(canvas_t, 1, -HALF) + at(spill_t, 0, 0)
            )
            taylor_ref[here] = fit_ref[here] - (straight + pltpu.roll(crossed, 64, 1))
        part = r // rows
        copies.append(
            pltpu.make_async_copy(
                residual_ref.at[:, pl.ds(r, rows), :], residual_hbm.at[:, pl.ds(r, rows), :],
                out_sems.at[0, part],
            )
        )
        copies.append(
            pltpu.make_async_copy(
                taylor_ref.at[pl.ds(r, rows), :], taylor_hbm.at[pl.ds(r, rows), :],
                out_sems.at[1, part],
            )
        )
        copies[-2].start()
        copies[-1].start()
    for copy in copies:
        copy.wait()


def per_device(dirty, psf, comp_tile, comp_offset, comp_scale, comp_amp, fit_weight):
    n_band, n_ty, n_tx = (lax.axis_size(a) for a in ("band", "ty", "tx"))
    sources = n_ty * n_tx
    lists = max(1, sources * SLOTS // 128)
    n_yp = n_ty // 2
    vmem = pl.BlockSpec(memory_space=pltpu.VMEM)
    smem = pl.BlockSpec(memory_space=pltpu.SMEM)
    dma = pltpu.SemaphoreType.DMA
    f32, bf16 = jnp.float32, jnp.bfloat16
    value, order, table, taylor_table, fit = pl.pallas_call(
        functools.partial(exchange_kernel, n_band, n_ty, n_tx),
        out_shape=(
            jax.ShapeDtypeStruct((sources // 2 + 8, 128), f32),
            jax.ShapeDtypeStruct((lists + 8, 128), jnp.int32),
            jax.ShapeDtypeStruct((PAD_K * PATCH, 128), f32),
            jax.ShapeDtypeStruct((PAD_K * HALF, 128), f32),
            jax.ShapeDtypeStruct((SIDE, SIDE), f32),
        ),
        in_specs=[vmem] * 4 + [smem] + [pl.BlockSpec(memory_space=pltpu.HBM)] * 2,
        out_specs=(vmem,) * 5,
        scratch_shapes=[
            pltpu.VMEM((n_tx, n_yp, 128), f32),
            pltpu.VMEM((n_yp, n_tx, 128), f32),
            pltpu.VMEM((n_ty, n_tx, 128), f32),
            pltpu.VMEM((2, SIDE, SIDE), f32),
            pltpu.VMEM((ROWS_K, 2, 2 * WIDE), bf16),
            pltpu.VMEM((2, PAD_K, 2 * WIDE), f32),
            pltpu.VMEM((n_band - 1, SIDE, SIDE), bf16),
            pltpu.VMEM((n_band - 1, SIDE, SIDE), bf16),
            pltpu.VMEM((n_band - 1, PAD_K, WIDE), f32),
            pltpu.VMEM((2, PAD_K, WIDE), f32),
            pltpu.VMEM((n_band - 1, PAD_K, WIDE), f32),
            dma((n_tx - 1,)), dma((n_tx - 1,)),
            dma((n_ty - 1,)), dma((n_ty - 1,)),
            dma((2, n_band - 1)), dma((2, n_band - 1)),
            dma((2,)), dma((1,)), dma((1,)), dma((2,)),
        ],
        compiler_params=pltpu.CompilerParams(
            collective_id=0, has_side_effects=True, vmem_limit_bytes=24 * 1024 * 1024
        ),
    )(
        comp_tile.T, comp_offset.T, comp_scale[None, :], comp_amp.T, fit_weight,
        pltpu.with_memory_space_constraint(dirty, pltpu.HBM),
        pltpu.with_memory_space_constraint(psf.transpose(1, 0, 2), pltpu.HBM),
    )
    residual, taylor = pl.pallas_call(
        render_kernel,
        out_shape=(
            jax.ShapeDtypeStruct((2, SIDE, SIDE), f32),
            jax.ShapeDtypeStruct((SIDE, SIDE), f32),
        ),
        in_specs=[vmem] * 6,
        out_specs=(pl.BlockSpec(memory_space=pltpu.HBM),) * 2,
        scratch_shapes=[
            pltpu.VMEM(((BLOCKS - 1) * CANVAS, 128), f32) for _ in range(4)
        ] + [
            pltpu.VMEM((2, SIDE, SIDE), f32), pltpu.VMEM((SIDE, SIDE), f32),
            pltpu.SMEM((value.size,), f32), pltpu.SMEM((order.size,), jnp.int32),
            dma((2,)), dma((2, SIDE // 64)),
        ],
        compiler_params=pltpu.CompilerParams(vmem_limit_bytes=24 * 1024 * 1024),
    )(
        value.reshape(-1), order.reshape(-1), table, taylor_table, dirty, fit,
    )
    return residual, taylor[None]


def solution(mesh):
    return jax.shard_map(
        per_device,
        mesh=mesh,
        in_specs=(
            P("band", "ty", "tx"),
            P("band", None, None),
            P(("ty", "tx"), None),
            P(("ty", "tx"), None),
            P(("ty", "tx")),
            P(("ty", "tx"), None),
            P("band", None),
        ),
        out_specs=(P("band", "ty", "tx"), P("band", "ty", "tx")),
        check_vma=False,
    )
```

```python
import functools

import jax
import jax.numpy as jnp
from jax import lax
from jax.experimental import pallas as pl
from jax.experimental.pallas import tpu as pltpu
from jax.sharding import PartitionSpec as P

TAYLOR = 4
SCALES = 5
PATCH = 48
ROWS_K = TAYLOR * SCALES
PAD_K = 24
HALF = PATCH // 2
WIDE = HALF * PATCH
SIDE = 256
SLOTS = 8
WORDS = 8
ROW_BASE = 48
COL_BASE = 64
BLOCKS = 6
CANVAS = 352
GROUP = 8
MESH = pl.DeviceIdType.MESH


def sends_of_tiles(tile, off, scale, amp, n_ty, n_tx):
    count = tile.shape[1]
    tiles, n_yp = n_ty * n_tx, n_ty // 2
    comp_y = lax.shift_right_logical(tile, n_tx.bit_length() - 1)
    comp_x = lax.bitwise_and(tile, n_tx - 1)
    over_r = (off[0:1] + PATCH > SIDE).astype(jnp.int32)
    over_c = (off[1:2] + PATCH > SIDE).astype(jnp.int32)
    dest = lax.broadcasted_iota(jnp.int32, (tiles, count), 0)
    half = tiles // 2
    bits = n_yp.bit_length() - 1
    core = lax.shift_right_logical(dest, half.bit_length() - 1)
    inner = lax.bitwise_and(dest, half - 1)
    dest_x = lax.shift_right_logical(inner, bits)
    dest_y = 2 * lax.bitwise_and(inner, n_yp - 1) + core
    down, right = dest_y - comp_y, dest_x - comp_x
    touches = ((down == 0) | ((down == 1) & (over_r == 1))) & (
        (right == 0) | ((right == 1) & (over_c == 1))
    )
    before = (
        lax.broadcasted_iota(jnp.int32, (count, count), 0)
        < lax.broadcasted_iota(jnp.int32, (count, count), 1)
    ).astype(jnp.float32)
    rank = jnp.dot(
        jnp.where(touches, 1.0, 0.0).astype(jnp.bfloat16),
        before.astype(jnp.bfloat16),
        preferred_element_type=jnp.float32,
    )
    rank = jnp.where(touches, rank, -1.0)
    chosen = jnp.concatenate(
        [jnp.where(rank == float(k), 1.0, 0.0).astype(jnp.bfloat16) for k in range(SLOTS)], axis=1
    )
    rows = (comp_y * SIDE + off[0:1]).astype(jnp.float32)
    cols = (comp_x * SIDE + off[1:2]).astype(jnp.float32)
    record = jnp.concatenate(
        [rows, cols, scale.astype(jnp.float32), jnp.ones((1, count), jnp.float32), amp], axis=0
    )
    high = record.astype(jnp.bfloat16).astype(jnp.float32)
    rest = record - high
    middle = rest.astype(jnp.bfloat16).astype(jnp.float32)
    low = rest - middle
    place = lax.shift_right_logical(
        lax.broadcasted_iota(jnp.int32, (SLOTS * WORDS, count), 0), 3
    )
    parts = []
    for part in (high, middle, low):
        tall = jnp.concatenate([part] * SLOTS, axis=0)
        parts.append(
            jnp.concatenate([jnp.where(place == k, tall, 0.0) for k in range(SLOTS)], axis=1)
        )
    parts.append(jnp.zeros_like(parts[0]))
    table = jnp.concatenate(parts, axis=0).astype(jnp.bfloat16)
    found = lax.dot_general(
        chosen, table, (((1,), (1,)), ((), ())), preferred_element_type=jnp.float32
    )
    found = found[:, :128] + found[:, 128:]
    found = found + pltpu.roll(found, 64, 1)
    lane = lax.broadcasted_iota(jnp.int32, (half, 128), 1)
    return jnp.where(lane < 64, found[:half], found[half:])


def unrolled(first, last, lane, step):
    tile, shift = divmod(step * PATCH, 128)
    out = []
    for table, base in ((first, 0), (last, 64)):
        value = table(tile)
        if shift + PATCH > 128:
            value = jnp.where(lane >= shift, value, table(tile + 1))
        turn = (base - shift) % 128
        out.append(pltpu.roll(value, turn, 1) if turn else value)
    return jnp.where(
        lane < PATCH, out[0], jnp.where((lane >= 64) & (lane < 64 + PATCH), out[1], 0.0)
    )


def exchange_kernel(
    n_band, n_ty, n_tx,
    tile_hbm, off_hbm, scale_hbm, amp_hbm, weight_hbm, dirty_hbm, psf_hbm,
    value_ref, list_ref, table_ref, taylor_table_ref, fit_ref,
    tile_ref, off_ref, scale_ref, amp_ref, weight_ref, dirty_ref, psf_ref,
    send, cross, got, psf, fit_send, fit_got, tab_send, tab_own, tab_got,
    x_send, x_recv, y_send, y_recv, b_send, b_recv, own_sem, pair_send, pair_recv, load_sem,
):
    loads = [
        pltpu.make_async_copy(source, target, load_sem.at[i])
        for i, (source, target) in enumerate((
            (tile_hbm, tile_ref), (off_hbm, off_ref), (scale_hbm, scale_ref), (amp_hbm, amp_ref),
            (weight_hbm, weight_ref), (psf_hbm, psf_ref), (dirty_hbm, dirty_ref),
        ))
    ]
    for load in loads:
        load.start()
    me_b, me_y, me_x = lax.axis_index("band"), lax.axis_index("ty"), lax.axis_index("tx")
    barrier = pltpu.get_barrier_semaphore()
    along_x = [lax.rem(me_x + o, n_tx) for o in range(1, n_tx)]
    along_y = [lax.rem(me_y + o, n_ty) for o in range(1, n_ty)]
    along_b = [lax.rem(me_b + o, n_band) for o in range(1, n_band)]
    partners = (
        [(me_b, me_y, x) for x in along_x]
        + [(me_b, y, me_x) for y in along_y]
        + [(b, me_y, me_x) for b in along_b]
    )
    for partner in partners:
        pl.semaphore_signal(barrier, inc=1, device_id=partner, device_id_type=MESH)

    for load in loads[:4]:
        load.wait()
    records = sends_of_tiles(tile_ref[...], off_ref[...], scale_ref[...], amp_ref[...], n_ty, n_tx)
    n_yp = n_ty // 2
    for x in range(n_tx):
        send[x] = records[x * n_yp:(x + 1) * n_yp]

    pl.semaphore_wait(barrier, len(partners))

    stage_x = []
    for o, x in enumerate(along_x):
        copy = pltpu.make_async_remote_copy(
            src_ref=send.at[x], dst_ref=cross.at[:, me_x, :],
            send_sem=x_send.at[o], recv_sem=x_recv.at[o],
            device_id=(me_b, me_y, x), device_id_type=MESH,
        )
        copy.start()
        stage_x.append(copy)
    own = pltpu.make_async_copy(send.at[me_x], cross.at[:, me_x, :], own_sem.at[0])
    own.start()
    for load in loads[4:]:
        load.wait()
    for b in range(2):
        psf[b, 0:ROWS_K, :] = psf_ref[:, b, :].astype(jnp.float32)
        psf[b, ROWS_K:PAD_K, :] = jnp.zeros((PAD_K - ROWS_K, 2 * WIDE), jnp.float32)
    core = lax.rem(me_y, 2)
    mine = [
        jnp.where(core == 1, psf[b, :, WIDE:2 * WIDE], psf[b, :, 0:WIDE]) for b in range(2)
    ]
    for o in range(1, n_band):
        w0, w1 = weight_ref[0, along_b[o - 1]], weight_ref[1, along_b[o - 1]]
        tab_send[o - 1] = w0 * mine[0] + w1 * mine[1]
        fit_send[o - 1] = (w0 * dirty_ref[0] + w1 * dirty_ref[1]).astype(jnp.bfloat16)

    w0, w1 = weight_ref[0, me_b], weight_ref[1, me_b]
    tab_own[core] = w0 * mine[0] + w1 * mine[1]
    lane24 = lax.broadcasted_iota(jnp.int32, (PAD_K, 128), 1)

    def piece(ref, half):
        return lambda t: ref[:, half * WIDE + t * 128:half * WIDE + (t + 1) * 128]

    def band_table(half):
        first, last = piece(psf.at[0], half), piece(psf.at[1], half)
        for step in range(HALF):
            table_ref[pl.ds(half * HALF + step, PAD_K, stride=PATCH), :] = unrolled(
                first, last, lane24, step
            )

    band_table(0)

    stage_t, stage_f = [], []
    for source, target, which, copies in (
        (tab_send, tab_got, 0, stage_t), (fit_send, fit_got, 1, stage_f)
    ):
        for o, b in enumerate(along_b):
            copy = pltpu.make_async_remote_copy(
                src_ref=source.at[o], dst_ref=target.at[o],
                send_sem=b_send.at[which, o], recv_sem=b_recv.at[which, o],
                device_id=(b, me_y, me_x), device_id_type=MESH,
            )
            copy.start()
            copies.append(copy)

    own.wait()
    for copy in stage_x:
        copy.wait_recv()
    stage_y = []
    for o, y in enumerate(along_y):
        copy = pltpu.make_async_remote_copy(
            src_ref=cross.at[y // 2], dst_ref=got.at[me_y],
            send_sem=y_send.at[o], recv_sem=y_recv.at[o],
            device_id=(me_b, y, me_x), device_id_type=MESH,
        )
        copy.start()
        stage_y.append(copy)
    own = pltpu.make_async_copy(cross.at[me_y // 2], got.at[me_y], own_sem.at[1])
    own.start()

    for copy in stage_t:
        copy.wait_recv()
    for o in range(n_band - 1):
        tab_own[core] += tab_got[o]
    band_table(1)
    pair = pltpu.make_async_remote_copy(
        src_ref=tab_own.at[core], dst_ref=tab_own.at[core],
        send_sem=pair_send.at[0], recv_sem=pair_recv.at[0],
        device_id=(me_b, me_y + 1 - 2 * core, me_x), device_id_type=MESH,
    )
    pair.start()

    own.wait()
    for copy in stage_y:
        copy.wait_recv()
    sources = n_ty * n_tx
    slots = jnp.concatenate([got[y] for y in range(n_ty)], axis=0)
    slots = jnp.where(lax.rem(me_y, 2) == 1, pltpu.roll(slots, 64, 1), slots)
    lane = lax.broadcasted_iota(jnp.int32, (sources, 128), 1)
    word = lax.bitwise_and(lane, WORDS - 1)
    move_r = (ROW_BASE - me_y * SIDE).astype(jnp.float32)
    move_c = (COL_BASE - me_x * SIDE).astype(jnp.float32)
    row = jnp.clip(slots + move_r, 0.0, float(ROW_BASE + SIDE)).astype(jnp.int32)
    col = jnp.clip(
        pltpu.roll(slots, 127, 1) + move_c, 0.0, float(COL_BASE + SIDE)
    ).astype(jnp.int32)
    scale = jnp.clip(pltpu.roll(slots, 126, 1), 0.0, float(SCALES)).astype(jnp.int32)
    place = row + lax.shift_right_logical(col, 6) * CANVAS
    place = place + lax.shift_left(lax.bitwise_and(col, 63), 11) + lax.shift_left(scale, 17)
    value = jnp.where(word == 0, place.astype(jnp.float32), slots)
    lower = lax.broadcasted_iota(jnp.int32, (sources // 2, 128), 1) < 64
    value_ref[0:sources // 2] = jnp.where(
        lower, value[:sources // 2], pltpu.roll(value[sources // 2:], 64, 1)
    )
    value_ref[sources // 2:sources // 2 + 8] = jnp.zeros((8, 128), jnp.float32)
    used = jnp.sum(
        jnp.where((word == 3) & (lane < 64), slots, 0.0), axis=1, keepdims=True
    )
    used = jnp.broadcast_to(used, (sources, 128))
    earlier = (
        lax.broadcasted_iota(jnp.int32, (sources, sources), 1)
        < lax.broadcasted_iota(jnp.int32, (sources, sources), 0)
    ).astype(jnp.float32).astype(jnp.bfloat16)
    start = jnp.dot(earlier, used.astype(jnp.bfloat16), preferred_element_type=jnp.float32)
    end = start + used
    lists = max(1, sources * SLOTS // 128)
    for i in range(lists):
        order = (lane + i * 128).astype(jnp.float32)
        source = jnp.sum(jnp.where(end <= order, 1.0, 0.0), axis=0, keepdims=True)
        base = jnp.max(jnp.where(start <= order, start, 0.0), axis=0, keepdims=True)
        upper = jnp.where(source >= float(sources // 2), 1.0, 0.0)
        index = (source - upper * (sources // 2)) * 128.0 + upper * 64.0
        index = index + (order[0:1] - base) * WORDS
        index = jnp.where(source < float(sources), index, float(sources // 2 * 128))
        list_ref[i:i + 1, :] = index.astype(jnp.int32)
    list_ref[lists:lists + 1, :] = end[sources - 1:sources].astype(jnp.int32)

    pair.wait_recv()
    first, last = piece(tab_own.at[0], 0), piece(tab_own.at[1], 0)
    for step in range(HALF):
        taylor_table_ref[pl.ds(step, PAD_K, stride=HALF), :] = unrolled(first, last, lane24, step)

    fit_ref[...] = w0 * dirty_ref[0] + w1 * dirty_ref[1]
    for copy in stage_f:
        copy.wait_recv()
    for o in range(n_band - 1):
        fit_ref[...] += fit_got[o].astype(jnp.float32)
    for copy in stage_x + stage_y + stage_t + stage_f + [pair]:
        copy.wait_send()


def render_kernel(
    value_ref, order_ref, table_ref, taylor_table_ref, dirty_ref, fit_ref,
    residual_hbm, taylor_hbm,
    canvas, spill, canvas_t, spill_t, residual_ref, taylor_ref, amp_ref, list_ref, sems, out_sems,
):
    fetches = [
        pltpu.make_async_copy(value_ref, amp_ref, sems.at[0]),
        pltpu.make_async_copy(order_ref, list_ref, sems.at[1]),
    ]
    for fetch in fetches:
        fetch.start()
    for block in range(BLOCKS - 1):
        for ref, used, first in (
            (canvas, block > 0, ROW_BASE), (spill, block < 4, ROW_BASE),
            (canvas_t, block > 0, ROW_BASE - HALF), (spill_t, block < 4, ROW_BASE - HALF),
        ):
            if used:
                rows = ROW_BASE + SIDE - first
                ref[pl.ds(block * CANVAS + first, rows), :] = jnp.zeros((rows, 128), jnp.float32)
    for fetch in fetches:
        fetch.wait()
    half_lane = lax.bitwise_and(lax.broadcasted_iota(jnp.int32, (HALF, 128), 1), 63)
    count = list_ref[list_ref.shape[0] - 1024]

    def step(index, carry):
        for g in range(GROUP):
            slot = list_ref[index * GROUP + g]
            packed = amp_ref[slot].astype(jnp.int32)
            amps = [amp_ref[slot + 4 + t] for t in range(TAYLOR)]
            first = lax.bitwise_and(packed, 2047)
            shift = lax.bitwise_and(lax.shift_right_logical(packed, 11), 63)
            base = lax.shift_right_logical(packed, 17) * HALF
            low = pl.multiple_of(base, HALF)
            high = pl.multiple_of(2 * base, PATCH)
            patch = fit = None
            for t in range(TAYLOR):
                term = amps[t] * table_ref[pl.ds(high + t * SCALES * PATCH, PATCH), :]
                patch = term if t == 0 else patch + term
                term = amps[t] * taylor_table_ref[pl.ds(low + t * SCALES * HALF, HALF), :]
                fit = term if t == 0 else fit + term
            patch = patch.astype(jnp.bfloat16).astype(jnp.float32)
            keep = half_lane >= shift
            other = jnp.logical_not(keep)
            sums = []
            for value, inside, beyond, at in (
                (patch[:HALF], canvas, spill, first),
                (patch[HALF:], canvas, spill, first + HALF),
                (fit, canvas_t, spill_t, first),
            ):
                value = pltpu.roll(value, shift, 1)
                for mask, target in ((keep, inside), (other, beyond)):
                    here = target.at[pl.ds(at, HALF), :]
                    sums.append((here, here[...] + value, mask))
            for here, value, mask in sums:
                pltpu.store(here, value, mask=mask)
        return carry

    lax.fori_loop(0, (count + GROUP - 1) // GROUP, step, 0)

    rows = 64
    lower = lax.broadcasted_iota(jnp.int32, (rows, 128), 1) < 64

    def mix(low, high):
        return jnp.where(lower, low, high)

    copies = []
    for r in range(0, SIDE, rows):
        for j in range(2):

            def at(ref, block, first):
                start = (block + 2 * j) * CANVAS + ROW_BASE + r + first
                return ref[pl.ds(start, rows), :]

            c1, c2 = at(canvas, 1, 0), at(canvas, 2, 0)
            s1, s2 = at(spill, 0, 0), at(spill, 1, 0)
            here = (slice(r, r + rows), slice(j * 128, j * 128 + 128))
            model = mix(c1, s2) + pltpu.roll(mix(c2, s1), 64, 1)
            residual_ref[(0,) + here] = dirty_ref[(0,) + here] - model
            model = mix(s1, c2) + pltpu.roll(mix(s2, c1), 64, 1)
            residual_ref[(1,) + here] = dirty_ref[(1,) + here] - model
            straight = mix(
                at(canvas_t, 1, 0) + at(spill_t, 0, -HALF), at(canvas_t, 2, -HALF) + at(spill_t, 1, 0)
            )
            crossed = mix(
                at(canvas_t, 2, 0) + at(spill_t, 1, -HALF), at(canvas_t, 1, -HALF) + at(spill_t, 0, 0)
            )
            taylor_ref[here] = fit_ref[here] - (straight + pltpu.roll(crossed, 64, 1))
        part = r // rows
        copies.append(
            pltpu.make_async_copy(
                residual_ref.at[:, pl.ds(r, rows), :], residual_hbm.at[:, pl.ds(r, rows), :],
                out_sems.at[0, part],
            )
        )
        copies.append(
            pltpu.make_async_copy(
                taylor_ref.at[pl.ds(r, rows), :], taylor_hbm.at[pl.ds(r, rows), :],
                out_sems.at[1, part],
            )
        )
        copies[-2].start()
        copies[-1].start()
    for copy in copies:
        copy.wait()


def per_device(dirty, psf, comp_tile, comp_offset, comp_scale, comp_amp, fit_weight):
    n_band, n_ty, n_tx = (lax.axis_size(a) for a in ("band", "ty", "tx"))
    sources, listed = n_ty * n_tx, comp_tile.shape[0]
    lists = max(1, sources * SLOTS // 128)
    n_yp = n_ty // 2
    vmem = pl.BlockSpec(memory_space=pltpu.VMEM)
    hbm = pl.BlockSpec(memory_space=pltpu.HBM)
    dma = pltpu.SemaphoreType.DMA
    f32, bf16 = jnp.float32, jnp.bfloat16
    value, order, table, taylor_table, fit = pl.pallas_call(
        functools.partial(exchange_kernel, n_band, n_ty, n_tx),
        out_shape=(
            jax.ShapeDtypeStruct((sources // 2 + 8, 128), f32),
            jax.ShapeDtypeStruct((lists + 8, 128), jnp.int32),
            jax.ShapeDtypeStruct((PAD_K * PATCH, 128), f32),
            jax.ShapeDtypeStruct((PAD_K * HALF, 128), f32),
            jax.ShapeDtypeStruct((SIDE, SIDE), f32),
        ),
        in_specs=[hbm] * 7,
        out_specs=(vmem,) * 5,
        scratch_shapes=[
            pltpu.VMEM((1, listed), jnp.int32), pltpu.VMEM((2, listed), jnp.int32),
            pltpu.VMEM((1, listed), jnp.int32), pltpu.VMEM((TAYLOR, listed), f32),
            pltpu.SMEM((2, TAYLOR), f32), pltpu.VMEM((2, SIDE, SIDE), f32),
            pltpu.VMEM((ROWS_K, 2, 2 * WIDE), bf16),
            pltpu.VMEM((n_tx, n_yp, 128), f32),
            pltpu.VMEM((n_yp, n_tx, 128), f32),
            pltpu.VMEM((n_ty, n_tx, 128), f32),
            pltpu.VMEM((2, PAD_K, 2 * WIDE), f32),
            pltpu.VMEM((n_band - 1, SIDE, SIDE), bf16),
            pltpu.VMEM((n_band - 1, SIDE, SIDE), bf16),
            pltpu.VMEM((n_band - 1, PAD_K, WIDE), f32),
            pltpu.VMEM((2, PAD_K, WIDE), f32),
            pltpu.VMEM((n_band - 1, PAD_K, WIDE), f32),
            dma((n_tx - 1,)), dma((n_tx - 1,)),
            dma((n_ty - 1,)), dma((n_ty - 1,)),
            dma((2, n_band - 1)), dma((2, n_band - 1)),
            dma((2,)), dma((1,)), dma((1,)), dma((7,)),
        ],
        compiler_params=pltpu.CompilerParams(
            collective_id=0, has_side_effects=True, vmem_limit_bytes=24 * 1024 * 1024
        ),
    )(
        *(
            pltpu.with_memory_space_constraint(operand, pltpu.HBM)
            for operand in (
                comp_tile.T, comp_offset.T, comp_scale[None, :], comp_amp.T, fit_weight, dirty,
                psf.transpose(1, 0, 2),
            )
        ),
    )
    residual, taylor = pl.pallas_call(
        render_kernel,
        out_shape=(
            jax.ShapeDtypeStruct((2, SIDE, SIDE), f32),
            jax.ShapeDtypeStruct((SIDE, SIDE), f32),
        ),
        in_specs=[vmem] * 6,
        out_specs=(hbm,) * 2,
        scratch_shapes=[
            pltpu.VMEM(((BLOCKS - 1) * CANVAS, 128), f32) for _ in range(4)
        ] + [
            pltpu.VMEM((2, SIDE, SIDE), f32), pltpu.VMEM((SIDE, SIDE), f32),
            pltpu.SMEM((value.size,), f32), pltpu.SMEM((order.size,), jnp.int32),
            dma((2,)), dma((2, SIDE // 64)),
        ],
        compiler_params=pltpu.CompilerParams(vmem_limit_bytes=24 * 1024 * 1024),
    )(
        value.reshape(-1), order.reshape(-1), table, taylor_table, dirty, fit,
    )
    return residual, taylor[None]


def solution(mesh):
    return jax.shard_map(
        per_device,
        mesh=mesh,
        in_specs=(
            P("band", "ty", "tx"),
            P("band", None, None),
            P(("ty", "tx"), None),
            P(("ty", "tx"), None),
            P(("ty", "tx")),
            P(("ty", "tx"), None),
            P("band", None),
        ),
        out_specs=(P("band", "ty", "tx"), P("band", "ty", "tx")),
        check_vma=False,
    )
```

```python
import functools

import jax
import jax.numpy as jnp
from jax import lax
from jax.experimental import pallas as pl
from jax.experimental.pallas import tpu as pltpu
from jax.sharding import PartitionSpec as P

TAYLOR = 4
SCALES = 5
PATCH = 48
ROWS_K = TAYLOR * SCALES
PAD_K = 24
HALF = PATCH // 2
WIDE = HALF * PATCH
SIDE = 256
SLOTS = 8
WORDS = 8
ROW_BASE = 48
COL_BASE = 64
BLOCKS = 6
CANVAS = 352
GROUPS = (48, 16, 8)
MESH = pl.DeviceIdType.MESH


def sends_of_tiles(tile, off, scale, amp, n_ty, n_tx):
    count = tile.shape[1]
    tiles = n_ty * n_tx
    comp_y = lax.shift_right_logical(tile, n_tx.bit_length() - 1)
    comp_x = lax.bitwise_and(tile, n_tx - 1)
    over_r = (off[0:1] + PATCH > SIDE).astype(jnp.int32)
    over_c = (off[1:2] + PATCH > SIDE).astype(jnp.int32)
    dest = lax.broadcasted_iota(jnp.int32, (tiles, count), 0)
    half = tiles // 2
    bits = n_tx.bit_length() - 1
    core = lax.shift_right_logical(dest, half.bit_length() - 1)
    inner = lax.bitwise_and(dest, half - 1)
    dest_x = lax.bitwise_and(inner, n_tx - 1)
    dest_y = 2 * lax.shift_right_logical(inner, bits) + core
    down, right = dest_y - comp_y, dest_x - comp_x
    touches = ((down == 0) | ((down == 1) & (over_r == 1))) & (
        (right == 0) | ((right == 1) & (over_c == 1))
    )
    before = (
        lax.broadcasted_iota(jnp.int32, (count, count), 0)
        < lax.broadcasted_iota(jnp.int32, (count, count), 1)
    ).astype(jnp.float32)
    rank = jnp.dot(
        jnp.where(touches, 1.0, 0.0).astype(jnp.bfloat16),
        before.astype(jnp.bfloat16),
        preferred_element_type=jnp.float32,
    )
    rank = jnp.where(touches, rank, -1.0)
    chosen = jnp.concatenate(
        [jnp.where(rank == float(k), 1.0, 0.0).astype(jnp.bfloat16) for k in range(SLOTS)], axis=1
    )
    rows = (comp_y * SIDE + off[0:1]).astype(jnp.float32)
    cols = (comp_x * SIDE + off[1:2]).astype(jnp.float32)
    record = jnp.concatenate(
        [rows, cols, scale.astype(jnp.float32), jnp.ones((1, count), jnp.float32), amp], axis=0
    )
    high = record.astype(jnp.bfloat16).astype(jnp.float32)
    rest = record - high
    middle = rest.astype(jnp.bfloat16).astype(jnp.float32)
    low = rest - middle
    place = lax.shift_right_logical(
        lax.broadcasted_iota(jnp.int32, (SLOTS * WORDS, count), 0), 3
    )
    parts = []
    for part in (high, middle, low):
        tall = jnp.concatenate([part] * SLOTS, axis=0)
        parts.append(
            jnp.concatenate([jnp.where(place == k, tall, 0.0) for k in range(SLOTS)], axis=1)
        )
    parts.append(jnp.zeros_like(parts[0]))
    table = jnp.concatenate(parts, axis=0).astype(jnp.bfloat16)
    found = lax.dot_general(
        chosen, table, (((1,), (1,)), ((), ())), preferred_element_type=jnp.float32
    )
    found = found[:, :128] + found[:, 128:]
    found = found + pltpu.roll(found, 64, 1)
    lane = lax.broadcasted_iota(jnp.int32, (half, 128), 1)
    return jnp.where(lane < 64, found[:half], found[half:])


def unrolled(first, last, lane, step):
    tile, shift = divmod(step * PATCH, 128)
    out = []
    for table, base in ((first, 0), (last, 64)):
        value = table(tile)
        if shift + PATCH > 128:
            value = jnp.where(lane >= shift, value, table(tile + 1))
        turn = (base - shift) % 128
        out.append(pltpu.roll(value, turn, 1) if turn else value)
    return jnp.where(
        lane < PATCH, out[0], jnp.where((lane >= 64) & (lane < 64 + PATCH), out[1], 0.0)
    )


def exchange_kernel(
    n_band, n_ty, n_tx,
    tile_hbm, off_hbm, scale_hbm, amp_hbm, weight_hbm, dirty_hbm, psf_hbm,
    value_ref, list_ref, table_ref, taylor_table_ref, fit_ref,
    tile_ref, off_ref, scale_ref, amp_ref, weight_ref, dirty_ref, psf_ref,
    send, cross, got, psf, fit_send, fit_got, tab_send, tab_own, tab_got,
    x_send, x_recv, y_send, y_recv, b_send, b_recv, own_sem, pair_send, pair_recv, load_sem,
):
    loads = [
        pltpu.make_async_copy(source, target, load_sem.at[i])
        for i, (source, target) in enumerate((
            (tile_hbm, tile_ref), (off_hbm, off_ref), (scale_hbm, scale_ref), (amp_hbm, amp_ref),
            (weight_hbm, weight_ref), (psf_hbm, psf_ref), (dirty_hbm, dirty_ref),
        ))
    ]
    for load in loads:
        load.start()
    me_b, me_y, me_x = lax.axis_index("band"), lax.axis_index("ty"), lax.axis_index("tx")
    barrier = pltpu.get_barrier_semaphore()
    along_x = [lax.rem(me_x + o, n_tx) for o in range(1, n_tx)]
    along_y = [lax.rem(me_y + o, n_ty) for o in range(1, n_ty)]
    along_b = [lax.rem(me_b + o, n_band) for o in range(1, n_band)]
    partners = (
        [(me_b, me_y, x) for x in along_x]
        + [(me_b, y, me_x) for y in along_y]
        + [(b, me_y, me_x) for b in along_b]
    )
    for partner in partners:
        pl.semaphore_signal(barrier, inc=1, device_id=partner, device_id_type=MESH)

    for load in loads[:4]:
        load.wait()
    records = sends_of_tiles(tile_ref[...], off_ref[...], scale_ref[...], amp_ref[...], n_ty, n_tx)
    for y in range(n_ty // 2):
        send[y] = records[y * n_tx:(y + 1) * n_tx]

    pl.semaphore_wait(barrier, len(partners))

    stage_y = []
    for o, y in enumerate(along_y):
        copy = pltpu.make_async_remote_copy(
            src_ref=send.at[y // 2], dst_ref=cross.at[me_y],
            send_sem=y_send.at[o], recv_sem=y_recv.at[o],
            device_id=(me_b, y, me_x), device_id_type=MESH,
        )
        copy.start()
        stage_y.append(copy)
    own = pltpu.make_async_copy(send.at[me_y // 2], cross.at[me_y], own_sem.at[0])
    own.start()
    for load in loads[4:]:
        load.wait()
    for b in range(2):
        psf[b, 0:ROWS_K, :] = psf_ref[:, b, :].astype(jnp.float32)
        psf[b, ROWS_K:PAD_K, :] = jnp.zeros((PAD_K - ROWS_K, 2 * WIDE), jnp.float32)
    core = lax.rem(me_y, 2)
    mine = [
        jnp.where(core == 1, psf[b, :, WIDE:2 * WIDE], psf[b, :, 0:WIDE]) for b in range(2)
    ]
    for o in range(1, n_band):
        w0, w1 = weight_ref[0, along_b[o - 1]], weight_ref[1, along_b[o - 1]]
        tab_send[o - 1] = w0 * mine[0] + w1 * mine[1]
        fit_send[o - 1] = (w0 * dirty_ref[0] + w1 * dirty_ref[1]).astype(jnp.bfloat16)

    w0, w1 = weight_ref[0, me_b], weight_ref[1, me_b]
    tab_own[core] = w0 * mine[0] + w1 * mine[1]
    lane24 = lax.broadcasted_iota(jnp.int32, (PAD_K, 128), 1)

    def piece(ref, half):
        return lambda t: ref[:, half * WIDE + t * 128:half * WIDE + (t + 1) * 128]

    def band_table(half):
        first, last = piece(psf.at[0], half), piece(psf.at[1], half)
        for step in range(HALF):
            table_ref[pl.ds(half * HALF + step, PAD_K, stride=PATCH), :] = unrolled(
                first, last, lane24, step
            )

    band_table(0)

    stage_t, stage_f = [], []
    for source, target, which, copies in (
        (tab_send, tab_got, 0, stage_t), (fit_send, fit_got, 1, stage_f)
    ):
        for o, b in enumerate(along_b):
            copy = pltpu.make_async_remote_copy(
                src_ref=source.at[o], dst_ref=target.at[o],
                send_sem=b_send.at[which, o], recv_sem=b_recv.at[which, o],
                device_id=(b, me_y, me_x), device_id_type=MESH,
            )
            copy.start()
            copies.append(copy)

    own.wait()
    for copy in stage_y:
        copy.wait_recv()
    stage_x = []
    for o, x in enumerate(along_x):
        copy = pltpu.make_async_remote_copy(
            src_ref=cross.at[:, x, :], dst_ref=got.at[:, me_x, :],
            send_sem=x_send.at[o], recv_sem=x_recv.at[o],
            device_id=(me_b, me_y, x), device_id_type=MESH,
        )
        copy.start()
        stage_x.append(copy)
    own = pltpu.make_async_copy(cross.at[:, me_x, :], got.at[:, me_x, :], own_sem.at[1])
    own.start()

    for copy in stage_t:
        copy.wait_recv()
    for o in range(n_band - 1):
        tab_own[core] += tab_got[o]
    band_table(1)
    pair = pltpu.make_async_remote_copy(
        src_ref=tab_own.at[core], dst_ref=tab_own.at[core],
        send_sem=pair_send.at[0], recv_sem=pair_recv.at[0],
        device_id=(me_b, me_y + 1 - 2 * core, me_x), device_id_type=MESH,
    )
    pair.start()

    pair.wait_recv()
    first, last = piece(tab_own.at[0], 0), piece(tab_own.at[1], 0)
    for step in range(HALF):
        taylor_table_ref[pl.ds(step, PAD_K, stride=HALF), :] = unrolled(first, last, lane24, step)

    fit_ref[...] = w0 * dirty_ref[0] + w1 * dirty_ref[1]
    for copy in stage_f:
        copy.wait_recv()
    for o in range(n_band - 1):
        fit_ref[...] += fit_got[o].astype(jnp.float32)
    own.wait()
    for copy in stage_x:
        copy.wait_recv()
    sources = n_ty * n_tx
    slots = jnp.concatenate([got[y] for y in range(n_ty)], axis=0)
    slots = jnp.where(lax.rem(me_y, 2) == 1, pltpu.roll(slots, 64, 1), slots)
    lane = lax.broadcasted_iota(jnp.int32, (sources, 128), 1)
    word = lax.bitwise_and(lane, WORDS - 1)
    move_r = (ROW_BASE - me_y * SIDE).astype(jnp.float32)
    move_c = (COL_BASE - me_x * SIDE).astype(jnp.float32)
    row = jnp.clip(slots + move_r, 0.0, float(ROW_BASE + SIDE)).astype(jnp.int32)
    col = jnp.clip(
        pltpu.roll(slots, 127, 1) + move_c, 0.0, float(COL_BASE + SIDE)
    ).astype(jnp.int32)
    scale = jnp.clip(pltpu.roll(slots, 126, 1), 0.0, float(SCALES)).astype(jnp.int32)
    place = row + lax.shift_right_logical(col, 6) * CANVAS
    place = place + lax.shift_left(lax.bitwise_and(col, 63), 11) + lax.shift_left(scale, 17)
    value = jnp.where(word == 0, place.astype(jnp.float32), slots)
    lower = lax.broadcasted_iota(jnp.int32, (sources // 2, 128), 1) < 64
    value_ref[0:sources // 2] = jnp.where(
        lower, value[:sources // 2], pltpu.roll(value[sources // 2:], 64, 1)
    )
    value_ref[sources // 2:sources // 2 + 8] = jnp.zeros((8, 128), jnp.float32)
    used = jnp.sum(
        jnp.where((word == 3) & (lane < 64), slots, 0.0), axis=1, keepdims=True
    )
    used = jnp.broadcast_to(used, (sources, 128))
    earlier = (
        lax.broadcasted_iota(jnp.int32, (sources, sources), 1)
        < lax.broadcasted_iota(jnp.int32, (sources, sources), 0)
    ).astype(jnp.float32).astype(jnp.bfloat16)
    start = jnp.dot(earlier, used.astype(jnp.bfloat16), preferred_element_type=jnp.float32)
    end = start + used
    lists = max(1, sources * SLOTS // 128)
    for i in range(lists):
        order = (lane + i * 128).astype(jnp.float32)
        source = jnp.sum(jnp.where(end <= order, 1.0, 0.0), axis=0, keepdims=True)
        base = jnp.max(jnp.where(start <= order, start, 0.0), axis=0, keepdims=True)
        upper = jnp.where(source >= float(sources // 2), 1.0, 0.0)
        index = (source - upper * (sources // 2)) * 128.0 + upper * 64.0
        index = index + (order[0:1] - base) * WORDS
        index = jnp.where(source < float(sources), index, float(sources // 2 * 128))
        list_ref[i:i + 1, :] = index.astype(jnp.int32)
    list_ref[lists:lists + 1, :] = end[sources - 1:sources].astype(jnp.int32)

    for copy in stage_x + stage_y + stage_t + stage_f + [pair]:
        copy.wait_send()


def render_kernel(
    value_ref, order_ref, table_ref, taylor_table_ref, dirty_ref, fit_ref,
    residual_hbm, taylor_hbm,
    canvas, spill, canvas_t, spill_t, residual_ref, taylor_ref, amp_ref, list_ref, sems, out_sems,
):
    fetches = [
        pltpu.make_async_copy(value_ref, amp_ref, sems.at[0]),
        pltpu.make_async_copy(order_ref, list_ref, sems.at[1]),
    ]
    for fetch in fetches:
        fetch.start()
    for block in range(BLOCKS - 1):
        for ref, used, first in (
            (canvas, block > 0, ROW_BASE), (spill, block < 4, ROW_BASE),
            (canvas_t, block > 0, ROW_BASE - HALF), (spill_t, block < 4, ROW_BASE - HALF),
        ):
            if used:
                rows = ROW_BASE + SIDE - first
                ref[pl.ds(block * CANVAS + first, rows), :] = jnp.zeros((rows, 128), jnp.float32)
    for fetch in fetches:
        fetch.wait()
    half_lane = lax.bitwise_and(lax.broadcasted_iota(jnp.int32, (HALF, 128), 1), 63)
    count = list_ref[list_ref.shape[0] - 1024]

    def step(first_of_all, group, index, carry):
        for g in range(group):
            slot = list_ref[first_of_all + index * group + g]
            packed = amp_ref[slot].astype(jnp.int32)
            amps = [amp_ref[slot + 4 + t] for t in range(TAYLOR)]
            first = lax.bitwise_and(packed, 2047)
            shift = lax.bitwise_and(lax.shift_right_logical(packed, 11), 63)
            base = lax.shift_right_logical(packed, 17) * HALF
            low = pl.multiple_of(base, HALF)
            high = pl.multiple_of(2 * base, PATCH)
            patch = fit = None
            for t in range(TAYLOR):
                term = amps[t] * table_ref[pl.ds(high + t * SCALES * PATCH, PATCH), :]
                patch = term if t == 0 else patch + term
                term = amps[t] * taylor_table_ref[pl.ds(low + t * SCALES * HALF, HALF), :]
                fit = term if t == 0 else fit + term
            patch = patch.astype(jnp.bfloat16).astype(jnp.float32)
            keep = half_lane >= shift
            other = jnp.logical_not(keep)
            sums = []
            for value, inside, beyond, at in (
                (patch[:HALF], canvas, spill, first),
                (patch[HALF:], canvas, spill, first + HALF),
                (fit, canvas_t, spill_t, first),
            ):
                value = pltpu.roll(value, shift, 1)
                for mask, target in ((keep, inside), (other, beyond)):
                    here = target.at[pl.ds(at, HALF), :]
                    sums.append((here, here[...] + value, mask))
            for here, value, mask in sums:
                pltpu.store(here, value, mask=mask)
        return carry

    done = 0
    for group in GROUPS:
        left = count - done + (group - 1 if group == GROUPS[-1] else 0)
        turns = left // group
        lax.fori_loop(0, turns, functools.partial(step, done, group), 0)
        done = done + turns * group

    rows = 64
    lower = lax.broadcasted_iota(jnp.int32, (rows, 128), 1) < 64

    def mix(low, high):
        return jnp.where(lower, low, high)

    copies = []
    for r in range(0, SIDE, rows):
        for j in range(2):

            def at(ref, block, first):
                start = (block + 2 * j) * CANVAS + ROW_BASE + r + first
                return ref[pl.ds(start, rows), :]

            c1, c2 = at(canvas, 1, 0), at(canvas, 2, 0)
            s1, s2 = at(spill, 0, 0), at(spill, 1, 0)
            here = (slice(r, r + rows), slice(j * 128, j * 128 + 128))
            model = mix(c1, s2) + pltpu.roll(mix(c2, s1), 64, 1)
            residual_ref[(0,) + here] = dirty_ref[(0,) + here] - model
            model = mix(s1, c2) + pltpu.roll(mix(s2, c1), 64, 1)
            residual_ref[(1,) + here] = dirty_ref[(1,) + here] - model
            straight = mix(
                at(canvas_t, 1, 0) + at(spill_t, 0, -HALF), at(canvas_t, 2, -HALF) + at(spill_t, 1, 0)
            )
            crossed = mix(
                at(canvas_t, 2, 0) + at(spill_t, 1, -HALF), at(canvas_t, 1, -HALF) + at(spill_t, 0, 0)
            )
            taylor_ref[here] = fit_ref[here] - (straight + pltpu.roll(crossed, 64, 1))
        part = r // rows
        copies.append(
            pltpu.make_async_copy(
                residual_ref.at[:, pl.ds(r, rows), :], residual_hbm.at[:, pl.ds(r, rows), :],
                out_sems.at[0, part],
            )
        )
        copies.append(
            pltpu.make_async_copy(
                taylor_ref.at[pl.ds(r, rows), :], taylor_hbm.at[pl.ds(r, rows), :],
                out_sems.at[1, part],
            )
        )
        copies[-2].start()
        copies[-1].start()
    for copy in copies:
        copy.wait()


def per_device(dirty, psf, comp_tile, comp_offset, comp_scale, comp_amp, fit_weight):
    n_band, n_ty, n_tx = (lax.axis_size(a) for a in ("band", "ty", "tx"))
    sources, listed = n_ty * n_tx, comp_tile.shape[0]
    lists = max(1, sources * SLOTS // 128)
    vmem = pl.BlockSpec(memory_space=pltpu.VMEM)
    hbm = pl.BlockSpec(memory_space=pltpu.HBM)
    dma = pltpu.SemaphoreType.DMA
    f32, bf16 = jnp.float32, jnp.bfloat16
    value, order, table, taylor_table, fit = pl.pallas_call(
        functools.partial(exchange_kernel, n_band, n_ty, n_tx),
        out_shape=(
            jax.ShapeDtypeStruct((sources // 2 + 8, 128), f32),
            jax.ShapeDtypeStruct((lists + 8, 128), jnp.int32),
            jax.ShapeDtypeStruct((PAD_K * PATCH, 128), f32),
            jax.ShapeDtypeStruct((PAD_K * HALF, 128), f32),
            jax.ShapeDtypeStruct((SIDE, SIDE), f32),
        ),
        in_specs=[hbm] * 7,
        out_specs=(vmem,) * 5,
        scratch_shapes=[
            pltpu.VMEM((1, listed), jnp.int32), pltpu.VMEM((2, listed), jnp.int32),
            pltpu.VMEM((1, listed), jnp.int32), pltpu.VMEM((TAYLOR, listed), f32),
            pltpu.SMEM((2, TAYLOR), f32), pltpu.VMEM((2, SIDE, SIDE), f32),
            pltpu.VMEM((ROWS_K, 2, 2 * WIDE), bf16),
            pltpu.VMEM((n_ty // 2, n_tx, 128), f32),
            pltpu.VMEM((n_ty, n_tx, 128), f32),
            pltpu.VMEM((n_ty, n_tx, 128), f32),
            pltpu.VMEM((2, PAD_K, 2 * WIDE), f32),
            pltpu.VMEM((n_band - 1, SIDE, SIDE), bf16),
            pltpu.VMEM((n_band - 1, SIDE, SIDE), bf16),
            pltpu.VMEM((n_band - 1, PAD_K, WIDE), f32),
            pltpu.VMEM((2, PAD_K, WIDE), f32),
            pltpu.VMEM((n_band - 1, PAD_K, WIDE), f32),
            dma((n_tx - 1,)), dma((n_tx - 1,)),
            dma((n_ty - 1,)), dma((n_ty - 1,)),
            dma((2, n_band - 1)), dma((2, n_band - 1)),
            dma((2,)), dma((1,)), dma((1,)), dma((7,)),
        ],
        compiler_params=pltpu.CompilerParams(
            collective_id=0, has_side_effects=True, vmem_limit_bytes=24 * 1024 * 1024
        ),
    )(
        *(
            pltpu.with_memory_space_constraint(operand, pltpu.HBM)
            for operand in (
                comp_tile.T, comp_offset.T, comp_scale[None, :], comp_amp.T, fit_weight, dirty,
                psf.transpose(1, 0, 2),
            )
        ),
    )
    residual, taylor = pl.pallas_call(
        render_kernel,
        out_shape=(
            jax.ShapeDtypeStruct((2, SIDE, SIDE), f32),
            jax.ShapeDtypeStruct((SIDE, SIDE), f32),
        ),
        in_specs=[vmem] * 6,
        out_specs=(hbm,) * 2,
        scratch_shapes=[
            pltpu.VMEM(((BLOCKS - 1) * CANVAS, 128), f32) for _ in range(4)
        ] + [
            pltpu.VMEM((2, SIDE, SIDE), f32), pltpu.VMEM((SIDE, SIDE), f32),
            pltpu.SMEM((value.size,), f32), pltpu.SMEM((order.size,), jnp.int32),
            dma((2,)), dma((2, SIDE // 64)),
        ],
        compiler_params=pltpu.CompilerParams(vmem_limit_bytes=24 * 1024 * 1024),
    )(
        value.reshape(-1), order.reshape(-1), table, taylor_table, dirty, fit,
    )
    return residual, taylor[None]


def solution(mesh):
    return jax.shard_map(
        per_device,
        mesh=mesh,
        in_specs=(
            P("band", "ty", "tx"),
            P("band", None, None),
            P(("ty", "tx"), None),
            P(("ty", "tx"), None),
            P(("ty", "tx")),
            P(("ty", "tx"), None),
            P("band", None),
        ),
        out_specs=(P("band", "ty", "tx"), P("band", "ty", "tx")),
        check_vma=False,
    )
```

```python
import functools

import jax
import jax.numpy as jnp
from jax import lax
from jax.experimental import pallas as pl
from jax.experimental.pallas import tpu as pltpu
from jax.sharding import PartitionSpec as P

TAYLOR = 4
SCALES = 5
PATCH = 48
ROWS_K = TAYLOR * SCALES
PAD_K = 24
HALF = PATCH // 2
WIDE = HALF * PATCH
SIDE = 256
SLOTS = 8
WORDS = 8
ROW_BASE = 48
COL_BASE = 64
BLOCKS = 6
CANVAS = 352
GROUPS = (48, 16, 8)
OUT_ROWS = 64
MESH = pl.DeviceIdType.MESH


def sends_of_tiles(tile, off, scale, amp, n_ty, n_tx):
    count = tile.shape[1]
    tiles = n_ty * n_tx
    comp_y = lax.shift_right_logical(tile, n_tx.bit_length() - 1)
    comp_x = lax.bitwise_and(tile, n_tx - 1)
    over_r = (off[0:1] + PATCH > SIDE).astype(jnp.int32)
    over_c = (off[1:2] + PATCH > SIDE).astype(jnp.int32)
    dest = lax.broadcasted_iota(jnp.int32, (tiles, count), 0)
    half = tiles // 2
    bits = n_tx.bit_length() - 1
    core = lax.shift_right_logical(dest, half.bit_length() - 1)
    inner = lax.bitwise_and(dest, half - 1)
    dest_x = lax.bitwise_and(inner, n_tx - 1)
    dest_y = 2 * lax.shift_right_logical(inner, bits) + core
    down, right = dest_y - comp_y, dest_x - comp_x
    touches = ((down == 0) | ((down == 1) & (over_r == 1))) & (
        (right == 0) | ((right == 1) & (over_c == 1))
    )
    before = (
        lax.broadcasted_iota(jnp.int32, (count, count), 0)
        < lax.broadcasted_iota(jnp.int32, (count, count), 1)
    ).astype(jnp.float32)
    rank = jnp.dot(
        jnp.where(touches, 1.0, 0.0).astype(jnp.bfloat16),
        before.astype(jnp.bfloat16),
        preferred_element_type=jnp.float32,
    )
    rank = jnp.where(touches, rank, -1.0)
    chosen = jnp.concatenate(
        [jnp.where(rank == float(k), 1.0, 0.0).astype(jnp.bfloat16) for k in range(SLOTS)], axis=1
    )
    rows = (comp_y * SIDE + off[0:1]).astype(jnp.float32)
    cols = (comp_x * SIDE + off[1:2]).astype(jnp.float32)
    record = jnp.concatenate(
        [rows, cols, scale.astype(jnp.float32), jnp.ones((1, count), jnp.float32), amp], axis=0
    )
    high = record.astype(jnp.bfloat16).astype(jnp.float32)
    rest = record - high
    middle = rest.astype(jnp.bfloat16).astype(jnp.float32)
    low = rest - middle
    place = lax.shift_right_logical(
        lax.broadcasted_iota(jnp.int32, (SLOTS * WORDS, count), 0), 3
    )
    parts = []
    for part in (high, middle, low):
        tall = jnp.concatenate([part] * SLOTS, axis=0)
        parts.append(
            jnp.concatenate([jnp.where(place == k, tall, 0.0) for k in range(SLOTS)], axis=1)
        )
    parts.append(jnp.zeros_like(parts[0]))
    table = jnp.concatenate(parts, axis=0).astype(jnp.bfloat16)
    found = lax.dot_general(
        chosen, table, (((1,), (1,)), ((), ())), preferred_element_type=jnp.float32
    )
    found = found[:, :128] + found[:, 128:]
    found = found + pltpu.roll(found, 64, 1)
    lane = lax.broadcasted_iota(jnp.int32, (half, 128), 1)
    return jnp.where(lane < 64, found[:half], found[half:])


def unrolled(first, last, lane, step):
    tile, shift = divmod(step * PATCH, 128)
    out = []
    for table, base in ((first, 0), (last, 64)):
        value = table(tile)
        if shift + PATCH > 128:
            value = jnp.where(lane >= shift, value, table(tile + 1))
        turn = (base - shift) % 128
        out.append(pltpu.roll(value, turn, 1) if turn else value)
    return jnp.where(
        lane < PATCH, out[0], jnp.where((lane >= 64) & (lane < 64 + PATCH), out[1], 0.0)
    )


def exchange_kernel(
    n_band, n_ty, n_tx,
    tile_hbm, off_hbm, scale_hbm, amp_hbm, weight_hbm, dirty_hbm, psf_hbm,
    value_ref, list_ref, table_ref, taylor_table_ref, fit_ref,
    tile_ref, off_ref, scale_ref, amp_ref, weight_ref, dirty_ref, psf_ref,
    send, cross, got, psf, fit_send, fit_got, tab_send, tab_own, tab_got,
    x_send, x_recv, y_send, y_recv, b_send, b_recv, own_sem, pair_send, pair_recv, load_sem,
):
    me_b, me_y, me_x = lax.axis_index("band"), lax.axis_index("ty"), lax.axis_index("tx")
    barrier = pltpu.get_barrier_semaphore()
    along_x = [lax.rem(me_x + o, n_tx) for o in range(1, n_tx)]
    along_y = [lax.rem(me_y + o, n_ty) for o in range(1, n_ty)]
    along_b = [lax.rem(me_b + o, n_band) for o in range(1, n_band)]
    partners = (
        [(me_b, me_y, x) for x in along_x]
        + [(me_b, y, me_x) for y in along_y]
        + [(b, me_y, me_x) for b in along_b]
    )
    for partner in partners:
        pl.semaphore_signal(barrier, inc=1, device_id=partner, device_id_type=MESH)

    loads = [
        pltpu.make_async_copy(source, target, load_sem.at[i])
        for i, (source, target) in enumerate((
            (tile_hbm, tile_ref), (off_hbm, off_ref), (scale_hbm, scale_ref), (amp_hbm, amp_ref),
            (weight_hbm, weight_ref), (psf_hbm, psf_ref), (dirty_hbm, dirty_ref),
        ))
    ]
    for load in loads:
        load.start()

    for load in loads[:4]:
        load.wait()
    records = sends_of_tiles(tile_ref[...], off_ref[...], scale_ref[...], amp_ref[...], n_ty, n_tx)
    for y in range(n_ty // 2):
        send[y] = records[y * n_tx:(y + 1) * n_tx]

    pl.semaphore_wait(barrier, len(partners))

    stage_y = []
    for o, y in enumerate(along_y):
        copy = pltpu.make_async_remote_copy(
            src_ref=send.at[y // 2], dst_ref=cross.at[me_y],
            send_sem=y_send.at[o], recv_sem=y_recv.at[o],
            device_id=(me_b, y, me_x), device_id_type=MESH,
        )
        copy.start()
        stage_y.append(copy)
    own = pltpu.make_async_copy(send.at[me_y // 2], cross.at[me_y], own_sem.at[0])
    own.start()
    for load in loads[4:]:
        load.wait()
    for b in range(2):
        psf[b, 0:ROWS_K, :] = psf_ref[:, b, :].astype(jnp.float32)
        psf[b, ROWS_K:PAD_K, :] = jnp.zeros((PAD_K - ROWS_K, 2 * WIDE), jnp.float32)
    core = lax.rem(me_y, 2)
    mine = [
        jnp.where(core == 1, psf[b, :, WIDE:2 * WIDE], psf[b, :, 0:WIDE]) for b in range(2)
    ]
    for o in range(1, n_band):
        w0, w1 = weight_ref[0, along_b[o - 1]], weight_ref[1, along_b[o - 1]]
        tab_send[o - 1] = w0 * mine[0] + w1 * mine[1]
        fit_send[o - 1] = (w0 * dirty_ref[0] + w1 * dirty_ref[1]).astype(jnp.bfloat16)

    w0, w1 = weight_ref[0, me_b], weight_ref[1, me_b]
    tab_own[core] = w0 * mine[0] + w1 * mine[1]
    lane24 = lax.broadcasted_iota(jnp.int32, (PAD_K, 128), 1)

    def piece(ref, half):
        return lambda t: ref[:, half * WIDE + t * 128:half * WIDE + (t + 1) * 128]

    def band_table(half):
        first, last = piece(psf.at[0], half), piece(psf.at[1], half)
        for step in range(HALF):
            table_ref[pl.ds(half * HALF + step, PAD_K, stride=PATCH), :] = unrolled(
                first, last, lane24, step
            )

    band_table(0)

    stage_t, stage_f = [], []
    for source, target, which, copies in (
        (tab_send, tab_got, 0, stage_t), (fit_send, fit_got, 1, stage_f)
    ):
        for o, b in enumerate(along_b):
            copy = pltpu.make_async_remote_copy(
                src_ref=source.at[o], dst_ref=target.at[o],
                send_sem=b_send.at[which, o], recv_sem=b_recv.at[which, o],
                device_id=(b, me_y, me_x), device_id_type=MESH,
            )
            copy.start()
            copies.append(copy)

    own.wait()
    for copy in stage_y:
        copy.wait_recv()
    stage_x = []
    for o, x in enumerate(along_x):
        copy = pltpu.make_async_remote_copy(
            src_ref=cross.at[:, x, :], dst_ref=got.at[:, me_x, :],
            send_sem=x_send.at[o], recv_sem=x_recv.at[o],
            device_id=(me_b, me_y, x), device_id_type=MESH,
        )
        copy.start()
        stage_x.append(copy)
    own = pltpu.make_async_copy(cross.at[:, me_x, :], got.at[:, me_x, :], own_sem.at[1])
    own.start()

    for copy in stage_t:
        copy.wait_recv()
    for o in range(n_band - 1):
        tab_own[core] += tab_got[o]
    band_table(1)
    pair = pltpu.make_async_remote_copy(
        src_ref=tab_own.at[core], dst_ref=tab_own.at[core],
        send_sem=pair_send.at[0], recv_sem=pair_recv.at[0],
        device_id=(me_b, me_y + 1 - 2 * core, me_x), device_id_type=MESH,
    )
    pair.start()

    pair.wait_recv()
    first, last = piece(tab_own.at[0], 0), piece(tab_own.at[1], 0)
    for step in range(HALF):
        taylor_table_ref[pl.ds(step, PAD_K, stride=HALF), :] = unrolled(first, last, lane24, step)

    fit_ref[...] = w0 * dirty_ref[0] + w1 * dirty_ref[1]
    for copy in stage_f:
        copy.wait_recv()
    for o in range(n_band - 1):
        fit_ref[...] += fit_got[o].astype(jnp.float32)
    own.wait()
    for copy in stage_x:
        copy.wait_recv()
    sources = n_ty * n_tx
    slots = jnp.concatenate([got[y] for y in range(n_ty)], axis=0)
    slots = jnp.where(lax.rem(me_y, 2) == 1, pltpu.roll(slots, 64, 1), slots)
    lane = lax.broadcasted_iota(jnp.int32, (sources, 128), 1)
    word = lax.bitwise_and(lane, WORDS - 1)
    move_r = (ROW_BASE - me_y * SIDE).astype(jnp.float32)
    move_c = (COL_BASE - me_x * SIDE).astype(jnp.float32)
    row = jnp.clip(slots + move_r, 0.0, float(ROW_BASE + SIDE)).astype(jnp.int32)
    col = jnp.clip(
        pltpu.roll(slots, 127, 1) + move_c, 0.0, float(COL_BASE + SIDE)
    ).astype(jnp.int32)
    scale = jnp.clip(pltpu.roll(slots, 126, 1), 0.0, float(SCALES)).astype(jnp.int32)
    place = row + lax.shift_right_logical(col, 6) * CANVAS
    place = place + lax.shift_left(lax.bitwise_and(col, 63), 11) + lax.shift_left(scale, 17)
    value = jnp.where(word == 0, place.astype(jnp.float32), slots)
    quarter = sources // 4
    part = lax.shift_right_logical(lax.broadcasted_iota(jnp.int32, (quarter, 128), 1), 5)
    for first, turn in ((0, 0), (quarter + 8, 96)):
        packed = jnp.zeros((quarter, 128), jnp.float32)
        for q in range(4):
            own_rows = value[q * quarter:(q + 1) * quarter]
            moved = (q * 32 + turn) % 128
            packed = jnp.where(part == q, pltpu.roll(own_rows, moved, 1) if moved else own_rows, packed)
        value_ref[first:first + quarter] = packed
    used = jnp.sum(
        jnp.where((word == 3) & (lane < 64), slots, 0.0), axis=1, keepdims=True
    )
    used = jnp.broadcast_to(used, (sources, 128))
    earlier = (
        lax.broadcasted_iota(jnp.int32, (sources, sources), 1)
        < lax.broadcasted_iota(jnp.int32, (sources, sources), 0)
    ).astype(jnp.float32).astype(jnp.bfloat16)
    start = jnp.dot(earlier, used.astype(jnp.bfloat16), preferred_element_type=jnp.float32)
    end = start + used
    lists = max(1, sources * SLOTS // 128)
    for i in range(lists):
        order = (lane + i * 128).astype(jnp.float32)
        source = jnp.sum(jnp.where(end <= order, 1.0, 0.0), axis=0, keepdims=True)
        base = jnp.max(jnp.where(start <= order, start, 0.0), axis=0, keepdims=True)
        group = sum(jnp.where(source >= float(q * quarter), 1.0, 0.0) for q in (1, 2, 3))
        slot = order[0:1] - base
        far = jnp.where(slot >= 4.0, 1.0, 0.0)
        index = (source - group * quarter + far * (quarter + 8)) * 128.0 + group * 32.0
        index = index + (slot - 4.0 * far) * WORDS
        index = jnp.where(source < float(sources), index, float(quarter * 128))
        list_ref[i:i + 1, :] = index.astype(jnp.int32)
    spot = lax.broadcasted_iota(jnp.int32, (8, 128), 1)
    count = end[sources - 1:sources]
    most = jnp.max(used, axis=0, keepdims=True)
    value_ref[quarter:quarter + 8] = jnp.where(
        spot == WORDS, count, jnp.where(spot == WORDS + 1, most, 0.0)
    )

    for copy in stage_x + stage_y + stage_t + stage_f + [pair]:
        copy.wait_send()


def render_kernel(
    value_ref, order_ref, table_ref, taylor_table_ref, dirty_ref, fit_ref,
    residual_hbm, taylor_hbm,
    canvas, spill, canvas_t, spill_t, residual_ref, taylor_ref, amp_ref, list_ref, sems, out_sems,
):
    near = (value_ref.shape[0] + 1024) // 2
    ends = (pl.ds(0, near), pl.ds(near, value_ref.shape[0] - near))
    fetches = [
        pltpu.make_async_copy(value_ref.at[ends[0]], amp_ref.at[ends[0]], sems.at[0]),
        pltpu.make_async_copy(order_ref, list_ref, sems.at[1]),
        pltpu.make_async_copy(value_ref.at[ends[1]], amp_ref.at[ends[1]], sems.at[2]),
    ]
    for fetch in fetches:
        fetch.start()
    for block in range(BLOCKS - 1):
        for ref, used, first in (
            (canvas, block > 0, ROW_BASE), (spill, block < 4, ROW_BASE),
            (canvas_t, block > 0, ROW_BASE - HALF), (spill_t, block < 4, ROW_BASE - HALF),
        ):
            if used:
                rows = ROW_BASE + SIDE - first
                ref[pl.ds(block * CANVAS + first, rows), :] = jnp.zeros((rows, 128), jnp.float32)
    for fetch in fetches[:2]:
        fetch.wait()
    half_lane = lax.bitwise_and(lax.broadcasted_iota(jnp.int32, (HALF, 128), 1), 63)
    count = amp_ref[near - 1024 + WORDS].astype(jnp.int32)
    crowded = amp_ref[near - 1024 + WORDS + 1] > 4.0

    @pl.when(crowded)
    def _():
        fetches[2].wait()


    def step(first_of_all, group, index, carry):
        for g in range(group):
            slot = list_ref[first_of_all + index * group + g]
            packed = amp_ref[slot].astype(jnp.int32)
            amps = [amp_ref[slot + 4 + t] for t in range(TAYLOR)]
            first = lax.bitwise_and(packed, 2047)
            shift = lax.bitwise_and(lax.shift_right_logical(packed, 11), 63)
            base = lax.shift_right_logical(packed, 17) * HALF
            low = pl.multiple_of(base, HALF)
            high = pl.multiple_of(2 * base, PATCH)
            patch = fit = None
            for t in range(TAYLOR):
                term = amps[t] * table_ref[pl.ds(high + t * SCALES * PATCH, PATCH), :]
                patch = term if t == 0 else patch + term
                term = amps[t] * taylor_table_ref[pl.ds(low + t * SCALES * HALF, HALF), :]
                fit = term if t == 0 else fit + term
            patch = patch.astype(jnp.bfloat16).astype(jnp.float32)
            keep = half_lane >= shift
            other = jnp.logical_not(keep)
            sums = []
            for value, inside, beyond, at in (
                (patch[:HALF], canvas, spill, first),
                (patch[HALF:], canvas, spill, first + HALF),
                (fit, canvas_t, spill_t, first),
            ):
                value = pltpu.roll(value, shift, 1)
                for mask, target in ((keep, inside), (other, beyond)):
                    here = target.at[pl.ds(at, HALF), :]
                    sums.append((here, here[...] + value, mask))
            for here, value, mask in sums:
                pltpu.store(here, value, mask=mask)
        return carry

    done = 0
    for group in GROUPS:
        left = count - done + (group - 1 if group == GROUPS[-1] else 0)
        turns = left // group
        lax.fori_loop(0, turns, functools.partial(step, done, group), 0)
        done = done + turns * group

    @pl.when(jnp.logical_not(crowded))
    def _():
        fetches[2].wait()

    rows = OUT_ROWS
    lower = lax.broadcasted_iota(jnp.int32, (rows, 128), 1) < 64

    def mix(low, high):
        return jnp.where(lower, low, high)

    copies = []
    for r in range(0, SIDE, rows):
        for j in range(2):

            def at(ref, block, first):
                start = (block + 2 * j) * CANVAS + ROW_BASE + r + first
                return ref[pl.ds(start, rows), :]

            c1, c2 = at(canvas, 1, 0), at(canvas, 2, 0)
            s1, s2 = at(spill, 0, 0), at(spill, 1, 0)
            here = (slice(r, r + rows), slice(j * 128, j * 128 + 128))
            model = mix(c1, s2) + pltpu.roll(mix(c2, s1), 64, 1)
            residual_ref[(0,) + here] = dirty_ref[(0,) + here] - model
            model = mix(s1, c2) + pltpu.roll(mix(s2, c1), 64, 1)
            residual_ref[(1,) + here] = dirty_ref[(1,) + here] - model
            straight = mix(
                at(canvas_t, 1, 0) + at(spill_t, 0, -HALF), at(canvas_t, 2, -HALF) + at(spill_t, 1, 0)
            )
            crossed = mix(
                at(canvas_t, 2, 0) + at(spill_t, 1, -HALF), at(canvas_t, 1, -HALF) + at(spill_t, 0, 0)
            )
            taylor_ref[here] = fit_ref[here] - (straight + pltpu.roll(crossed, 64, 1))
        part = r // rows
        copies.append(
            pltpu.make_async_copy(
                residual_ref.at[:, pl.ds(r, rows), :], residual_hbm.at[:, pl.ds(r, rows), :],
                out_sems.at[0, part],
            )
        )
        copies.append(
            pltpu.make_async_copy(
                taylor_ref.at[pl.ds(r, rows), :], taylor_hbm.at[pl.ds(r, rows), :],
                out_sems.at[1, part],
            )
        )
        copies[-2].start()
        copies[-1].start()
    for copy in copies:
        copy.wait()


def per_device(dirty, psf, comp_tile, comp_offset, comp_scale, comp_amp, fit_weight):
    n_band, n_ty, n_tx = (lax.axis_size(a) for a in ("band", "ty", "tx"))
    sources, listed = n_ty * n_tx, comp_tile.shape[0]
    lists = max(1, sources * SLOTS // 128)
    vmem = pl.BlockSpec(memory_space=pltpu.VMEM)
    hbm = pl.BlockSpec(memory_space=pltpu.HBM)
    dma = pltpu.SemaphoreType.DMA
    f32, bf16 = jnp.float32, jnp.bfloat16
    value, order, table, taylor_table, fit = pl.pallas_call(
        functools.partial(exchange_kernel, n_band, n_ty, n_tx),
        out_shape=(
            jax.ShapeDtypeStruct((sources // 2 + 8, 128), f32),
            jax.ShapeDtypeStruct((lists, 128), jnp.int32),
            jax.ShapeDtypeStruct((PAD_K * PATCH, 128), f32),
            jax.ShapeDtypeStruct((PAD_K * HALF, 128), f32),
            jax.ShapeDtypeStruct((SIDE, SIDE), f32),
        ),
        in_specs=[hbm] * 7,
        out_specs=(vmem,) * 5,
        scratch_shapes=[
            pltpu.VMEM((1, listed), jnp.int32), pltpu.VMEM((2, listed), jnp.int32),
            pltpu.VMEM((1, listed), jnp.int32), pltpu.VMEM((TAYLOR, listed), f32),
            pltpu.SMEM((2, TAYLOR), f32), pltpu.VMEM((2, SIDE, SIDE), f32),
            pltpu.VMEM((ROWS_K, 2, 2 * WIDE), bf16),
            pltpu.VMEM((n_ty // 2, n_tx, 128), f32),
            pltpu.VMEM((n_ty, n_tx, 128), f32),
            pltpu.VMEM((n_ty, n_tx, 128), f32),
            pltpu.VMEM((2, PAD_K, 2 * WIDE), f32),
            pltpu.VMEM((n_band - 1, SIDE, SIDE), bf16),
            pltpu.VMEM((n_band - 1, SIDE, SIDE), bf16),
            pltpu.VMEM((n_band - 1, PAD_K, WIDE), f32),
            pltpu.VMEM((2, PAD_K, WIDE), f32),
            pltpu.VMEM((n_band - 1, PAD_K, WIDE), f32),
            dma((n_tx - 1,)), dma((n_tx - 1,)),
            dma((n_ty - 1,)), dma((n_ty - 1,)),
            dma((2, n_band - 1)), dma((2, n_band - 1)),
            dma((2,)), dma((1,)), dma((1,)), dma((7,)),
        ],
        compiler_params=pltpu.CompilerParams(
            collective_id=0, has_side_effects=True, vmem_limit_bytes=24 * 1024 * 1024
        ),
    )(
        *(
            pltpu.with_memory_space_constraint(operand, pltpu.HBM)
            for operand in (
                comp_tile.T, comp_offset.T, comp_scale[None, :], comp_amp.T, fit_weight, dirty,
                psf.transpose(1, 0, 2),
            )
        ),
    )
    residual, taylor = pl.pallas_call(
        render_kernel,
        out_shape=(
            jax.ShapeDtypeStruct((2, SIDE, SIDE), f32),
            jax.ShapeDtypeStruct((SIDE, SIDE), f32),
        ),
        in_specs=[vmem] * 6,
        out_specs=(hbm,) * 2,
        scratch_shapes=[
            pltpu.VMEM(((BLOCKS - 1) * CANVAS, 128), f32) for _ in range(4)
        ] + [
            pltpu.VMEM((2, SIDE, SIDE), f32), pltpu.VMEM((SIDE, SIDE), f32),
            pltpu.SMEM((value.size,), f32), pltpu.SMEM((order.size,), jnp.int32),
            dma((3,)), dma((2, SIDE // OUT_ROWS)),
        ],
        compiler_params=pltpu.CompilerParams(vmem_limit_bytes=24 * 1024 * 1024),
    )(
        value.reshape(-1), order.reshape(-1), table, taylor_table, dirty, fit,
    )
    return residual, taylor[None]


def solution(mesh):
    return jax.shard_map(
        per_device,
        mesh=mesh,
        in_specs=(
            P("band", "ty", "tx"),
            P("band", None, None),
            P(("ty", "tx"), None),
            P(("ty", "tx"), None),
            P(("ty", "tx")),
            P(("ty", "tx"), None),
            P("band", None),
        ),
        out_specs=(P("band", "ty", "tx"), P("band", "ty", "tx")),
        check_vma=False,
    )
```

```python
import functools

import jax
import jax.numpy as jnp
from jax import lax
from jax.experimental import pallas as pl
from jax.experimental.pallas import tpu as pltpu
from jax.sharding import PartitionSpec as P

TAYLOR = 4
SCALES = 5
PATCH = 48
ROWS_K = TAYLOR * SCALES
PAD_K = 24
HALF = PATCH // 2
WIDE = HALF * PATCH
SIDE = 256
SLOTS = 8
WORDS = 8
ROW_BASE = 48
COL_BASE = 64
BLOCKS = 6
CANVAS = 352
GROUPS = (48, 16, 8)
OUT_ROWS = 64
MESH = pl.DeviceIdType.MESH


def sends_of_tiles(tile, off, scale, amp, n_ty, n_tx):
    count = tile.shape[1]
    tiles = n_ty * n_tx
    comp_y = lax.shift_right_logical(tile, n_tx.bit_length() - 1)
    comp_x = lax.bitwise_and(tile, n_tx - 1)
    over_r = (off[0:1] + PATCH > SIDE).astype(jnp.int32)
    over_c = (off[1:2] + PATCH > SIDE).astype(jnp.int32)
    dest = lax.broadcasted_iota(jnp.int32, (tiles, count), 0)
    half = tiles // 2
    bits = n_tx.bit_length() - 1
    core = lax.shift_right_logical(dest, half.bit_length() - 1)
    inner = lax.bitwise_and(dest, half - 1)
    dest_x = lax.bitwise_and(inner, n_tx - 1)
    dest_y = 2 * lax.shift_right_logical(inner, bits) + core
    down, right = dest_y - comp_y, dest_x - comp_x
    touches = ((down == 0) | ((down == 1) & (over_r == 1))) & (
        (right == 0) | ((right == 1) & (over_c == 1))
    )
    before = (
        lax.broadcasted_iota(jnp.int32, (count, count), 0)
        < lax.broadcasted_iota(jnp.int32, (count, count), 1)
    ).astype(jnp.float32)
    rank = jnp.dot(
        jnp.where(touches, 1.0, 0.0).astype(jnp.bfloat16),
        before.astype(jnp.bfloat16),
        preferred_element_type=jnp.float32,
    )
    rank = jnp.where(touches, rank, -1.0)
    chosen = jnp.concatenate(
        [jnp.where(rank == float(k), 1.0, 0.0).astype(jnp.bfloat16) for k in range(SLOTS)], axis=1
    )
    rows = (comp_y * SIDE + off[0:1]).astype(jnp.float32)
    cols = (comp_x * SIDE + off[1:2]).astype(jnp.float32)
    record = jnp.concatenate(
        [rows, cols, scale.astype(jnp.float32), jnp.ones((1, count), jnp.float32), amp], axis=0
    )
    high = record.astype(jnp.bfloat16).astype(jnp.float32)
    rest = record - high
    middle = rest.astype(jnp.bfloat16).astype(jnp.float32)
    low = rest - middle
    place = lax.shift_right_logical(
        lax.broadcasted_iota(jnp.int32, (SLOTS * WORDS, count), 0), 3
    )
    parts = []
    for part in (high, middle, low):
        tall = jnp.concatenate([part] * SLOTS, axis=0)
        parts.append(
            jnp.concatenate([jnp.where(place == k, tall, 0.0) for k in range(SLOTS)], axis=1)
        )
    parts.append(jnp.zeros_like(parts[0]))
    table = jnp.concatenate(parts, axis=0).astype(jnp.bfloat16)
    found = lax.dot_general(
        chosen, table, (((1,), (1,)), ((), ())), preferred_element_type=jnp.float32
    )
    found = found[:, :128] + found[:, 128:]
    found = found + pltpu.roll(found, 64, 1)
    lane = lax.broadcasted_iota(jnp.int32, (half, 128), 1)
    return jnp.where(lane < 64, found[:half], found[half:])


def unrolled(first, last, lane, step):
    tile, shift = divmod(step * PATCH, 128)
    out = []
    for table, base in ((first, 0), (last, 64)):
        value = table(tile)
        if shift + PATCH > 128:
            value = jnp.where(lane >= shift, value, table(tile + 1))
        turn = (base - shift) % 128
        out.append(pltpu.roll(value, turn, 1) if turn else value)
    return jnp.where(
        lane < PATCH, out[0], jnp.where((lane >= 64) & (lane < 64 + PATCH), out[1], 0.0)
    )


def exchange_kernel(
    n_band, n_ty, n_tx,
    tile_hbm, off_hbm, scale_hbm, amp_hbm, weight_hbm, dirty_hbm, psf_hbm,
    value_ref, list_ref, table_ref, taylor_table_ref, fit_ref,
    tile_ref, off_ref, scale_ref, amp_ref, weight_ref, dirty_ref, psf_ref,
    send, cross, got, psf, fit_send, fit_got, tab_send, tab_own, tab_got,
    x_send, x_recv, y_send, y_recv, b_send, b_recv, own_sem, pair_send, pair_recv, load_sem,
):
    me_b, me_y, me_x = lax.axis_index("band"), lax.axis_index("ty"), lax.axis_index("tx")
    barrier = pltpu.get_barrier_semaphore()
    along_x = [lax.rem(me_x + o, n_tx) for o in range(1, n_tx)]
    along_y = [lax.rem(me_y + o, n_ty) for o in range(1, n_ty)]
    along_b = [lax.rem(me_b + o, n_band) for o in range(1, n_band)]
    partners = (
        [(me_b, me_y, x) for x in along_x]
        + [(me_b, y, me_x) for y in along_y]
        + [(b, me_y, me_x) for b in along_b]
    )
    for partner in partners:
        pl.semaphore_signal(barrier, inc=1, device_id=partner, device_id_type=MESH)

    loads = [
        pltpu.make_async_copy(source, target, load_sem.at[i])
        for i, (source, target) in enumerate((
            (tile_hbm, tile_ref), (off_hbm, off_ref), (scale_hbm, scale_ref), (amp_hbm, amp_ref),
            (weight_hbm, weight_ref), (psf_hbm, psf_ref), (dirty_hbm, dirty_ref),
        ))
    ]
    for load in loads:
        load.start()

    for load in loads[:4]:
        load.wait()
    records = sends_of_tiles(tile_ref[...], off_ref[...], scale_ref[...], amp_ref[...], n_ty, n_tx)
    for y in range(n_ty // 2):
        send[y] = records[y * n_tx:(y + 1) * n_tx]

    pl.semaphore_wait(barrier, len(partners))

    def in_all(ref, send_sem, recv_sem, partner):
        return pltpu.make_async_remote_copy(
            src_ref=ref, dst_ref=ref, send_sem=send_sem.at[0], recv_sem=recv_sem.at[0],
            device_id=partner, device_id_type=MESH,
        )

    for y in along_y:
        copy = pltpu.make_async_remote_copy(
            src_ref=send.at[y // 2], dst_ref=cross.at[me_y],
            send_sem=y_send.at[0], recv_sem=y_recv.at[0],
            device_id=(me_b, y, me_x), device_id_type=MESH,
        )
        copy.start()
    stage_y = in_all(cross.at[pl.ds(0, n_ty - 1)], y_send, y_recv, partners[-n_band])
    own = pltpu.make_async_copy(send.at[me_y // 2], cross.at[me_y], own_sem.at[0])
    own.start()
    for load in loads[4:]:
        load.wait()
    for b in range(2):
        psf[b, 0:ROWS_K, :] = psf_ref[:, b, :].astype(jnp.float32)
        psf[b, ROWS_K:PAD_K, :] = jnp.zeros((PAD_K - ROWS_K, 2 * WIDE), jnp.float32)
    core = lax.rem(me_y, 2)
    mine = [
        jnp.where(core == 1, psf[b, :, WIDE:2 * WIDE], psf[b, :, 0:WIDE]) for b in range(2)
    ]
    for o in range(1, n_band):
        w0, w1 = weight_ref[0, along_b[o - 1]], weight_ref[1, along_b[o - 1]]
        tab_send[o - 1] = w0 * mine[0] + w1 * mine[1]
        fit_send[o - 1] = (w0 * dirty_ref[0] + w1 * dirty_ref[1]).astype(jnp.bfloat16)

    w0, w1 = weight_ref[0, me_b], weight_ref[1, me_b]
    tab_own[core] = w0 * mine[0] + w1 * mine[1]
    lane24 = lax.broadcasted_iota(jnp.int32, (PAD_K, 128), 1)

    def piece(ref, half):
        return lambda t: ref[:, half * WIDE + t * 128:half * WIDE + (t + 1) * 128]

    def band_table(half):
        first, last = piece(psf.at[0], half), piece(psf.at[1], half)
        for step in range(HALF):
            table_ref[pl.ds(half * HALF + step, PAD_K, stride=PATCH), :] = unrolled(
                first, last, lane24, step
            )

    band_table(0)

    stage_t, stage_f = [], []
    for source, target, which, copies in (
        (tab_send, tab_got, 0, stage_t), (fit_send, fit_got, 1, stage_f)
    ):
        for o, b in enumerate(along_b):
            copy = pltpu.make_async_remote_copy(
                src_ref=source.at[o], dst_ref=target.at[o],
                send_sem=b_send.at[which, o], recv_sem=b_recv.at[which, o],
                device_id=(b, me_y, me_x), device_id_type=MESH,
            )
            copy.start()
            copies.append(copy)

    own.wait()
    stage_y.wait_recv()
    for x in along_x:
        copy = pltpu.make_async_remote_copy(
            src_ref=cross.at[:, x, :], dst_ref=got.at[:, me_x, :],
            send_sem=x_send.at[0], recv_sem=x_recv.at[0],
            device_id=(me_b, me_y, x), device_id_type=MESH,
        )
        copy.start()
    stage_x = in_all(got.at[:, pl.ds(0, n_tx - 1), :], x_send, x_recv, partners[0])
    own = pltpu.make_async_copy(cross.at[:, me_x, :], got.at[:, me_x, :], own_sem.at[1])
    own.start()

    for copy in stage_t:
        copy.wait_recv()
    for o in range(n_band - 1):
        tab_own[core] += tab_got[o]
    band_table(1)
    pair = pltpu.make_async_remote_copy(
        src_ref=tab_own.at[core], dst_ref=tab_own.at[core],
        send_sem=pair_send.at[0], recv_sem=pair_recv.at[0],
        device_id=(me_b, me_y + 1 - 2 * core, me_x), device_id_type=MESH,
    )
    pair.start()

    pair.wait_recv()
    first, last = piece(tab_own.at[0], 0), piece(tab_own.at[1], 0)
    for step in range(HALF):
        taylor_table_ref[pl.ds(step, PAD_K, stride=HALF), :] = unrolled(first, last, lane24, step)

    fit_ref[...] = w0 * dirty_ref[0] + w1 * dirty_ref[1]
    for copy in stage_f:
        copy.wait_recv()
    for o in range(n_band - 1):
        fit_ref[...] += fit_got[o].astype(jnp.float32)
    own.wait()
    stage_x.wait_recv()
    sources = n_ty * n_tx
    slots = jnp.concatenate([got[y] for y in range(n_ty)], axis=0)
    slots = jnp.where(lax.rem(me_y, 2) == 1, pltpu.roll(slots, 64, 1), slots)
    lane = lax.broadcasted_iota(jnp.int32, (sources, 128), 1)
    word = lax.bitwise_and(lane, WORDS - 1)
    move_r = (ROW_BASE - me_y * SIDE).astype(jnp.float32)
    move_c = (COL_BASE - me_x * SIDE).astype(jnp.float32)
    row = jnp.clip(slots + move_r, 0.0, float(ROW_BASE + SIDE)).astype(jnp.int32)
    col = jnp.clip(
        pltpu.roll(slots, 127, 1) + move_c, 0.0, float(COL_BASE + SIDE)
    ).astype(jnp.int32)
    scale = jnp.clip(pltpu.roll(slots, 126, 1), 0.0, float(SCALES)).astype(jnp.int32)
    place = row + lax.shift_right_logical(col, 6) * CANVAS
    place = place + lax.shift_left(lax.bitwise_and(col, 63), 11) + lax.shift_left(scale, 17)
    value = jnp.where(word == 0, place.astype(jnp.float32), slots)
    quarter = sources // 4
    part = lax.shift_right_logical(lax.broadcasted_iota(jnp.int32, (quarter, 128), 1), 5)
    for first, turn in ((0, 0), (quarter + 8, 96)):
        packed = jnp.zeros((quarter, 128), jnp.float32)
        for q in range(4):
            own_rows = value[q * quarter:(q + 1) * quarter]
            moved = (q * 32 + turn) % 128
            packed = jnp.where(part == q, pltpu.roll(own_rows, moved, 1) if moved else own_rows, packed)
        value_ref[first:first + quarter] = packed
    used = jnp.sum(
        jnp.where((word == 3) & (lane < 64), slots, 0.0), axis=1, keepdims=True
    )
    used = jnp.broadcast_to(used, (sources, 128))
    earlier = (
        lax.broadcasted_iota(jnp.int32, (sources, sources), 1)
        < lax.broadcasted_iota(jnp.int32, (sources, sources), 0)
    ).astype(jnp.float32).astype(jnp.bfloat16)
    start = jnp.dot(earlier, used.astype(jnp.bfloat16), preferred_element_type=jnp.float32)
    end = start + used
    lists = max(1, sources * SLOTS // 128)
    for i in range(lists):
        order = (lane + i * 128).astype(jnp.float32)
        source = jnp.sum(jnp.where(end <= order, 1.0, 0.0), axis=0, keepdims=True)
        base = jnp.max(jnp.where(start <= order, start, 0.0), axis=0, keepdims=True)
        group = sum(jnp.where(source >= float(q * quarter), 1.0, 0.0) for q in (1, 2, 3))
        slot = order[0:1] - base
        far = jnp.where(slot >= 4.0, 1.0, 0.0)
        index = (source - group * quarter + far * (quarter + 8)) * 128.0 + group * 32.0
        index = index + (slot - 4.0 * far) * WORDS
        index = jnp.where(source < float(sources), index, float(quarter * 128))
        list_ref[i:i + 1, :] = index.astype(jnp.int32)
    spot = lax.broadcasted_iota(jnp.int32, (8, 128), 1)
    count = end[sources - 1:sources]
    most = jnp.max(used, axis=0, keepdims=True)
    value_ref[quarter:quarter + 8] = jnp.where(
        spot == WORDS, count, jnp.where(spot == WORDS + 1, most, 0.0)
    )

    for copy in [stage_x, stage_y, pair] + stage_t + stage_f:
        copy.wait_send()


def render_kernel(
    value_ref, order_ref, table_ref, taylor_table_ref, dirty_ref, fit_ref,
    residual_hbm, taylor_hbm,
    canvas, spill, canvas_t, spill_t, residual_ref, taylor_ref, amp_ref, list_ref, sems, out_sems,
):
    near = (value_ref.shape[0] + 1024) // 2
    ends = (pl.ds(0, near), pl.ds(near, value_ref.shape[0] - near))
    fetches = [
        pltpu.make_async_copy(value_ref.at[ends[0]], amp_ref.at[ends[0]], sems.at[0]),
        pltpu.make_async_copy(order_ref, list_ref, sems.at[1]),
        pltpu.make_async_copy(value_ref.at[ends[1]], amp_ref.at[ends[1]], sems.at[2]),
    ]
    for fetch in fetches:
        fetch.start()
    for block in range(BLOCKS - 1):
        for ref, used, first in (
            (canvas, block > 0, ROW_BASE), (spill, block < 4, ROW_BASE),
            (canvas_t, block > 0, ROW_BASE - HALF), (spill_t, block < 4, ROW_BASE - HALF),
        ):
            if used:
                rows = ROW_BASE + SIDE - first
                ref[pl.ds(block * CANVAS + first, rows), :] = jnp.zeros((rows, 128), jnp.float32)
    for fetch in fetches[:2]:
        fetch.wait()
    half_lane = lax.bitwise_and(lax.broadcasted_iota(jnp.int32, (HALF, 128), 1), 63)
    count = amp_ref[near - 1024 + WORDS].astype(jnp.int32)
    crowded = amp_ref[near - 1024 + WORDS + 1] > 4.0

    @pl.when(crowded)
    def _():
        fetches[2].wait()


    def step(first_of_all, group, index, carry):
        for g in range(group):
            slot = list_ref[first_of_all + index * group + g]
            packed = amp_ref[slot].astype(jnp.int32)
            amps = [amp_ref[slot + 4 + t] for t in range(TAYLOR)]
            first = lax.bitwise_and(packed, 2047)
            shift = lax.bitwise_and(lax.shift_right_logical(packed, 11), 63)
            base = lax.shift_right_logical(packed, 17) * HALF
            low = pl.multiple_of(base, HALF)
            high = pl.multiple_of(2 * base, PATCH)
            patch = fit = None
            for t in range(TAYLOR):
                term = amps[t] * table_ref[pl.ds(high + t * SCALES * PATCH, PATCH), :]
                patch = term if t == 0 else patch + term
                term = amps[t] * taylor_table_ref[pl.ds(low + t * SCALES * HALF, HALF), :]
                fit = term if t == 0 else fit + term
            patch = patch.astype(jnp.bfloat16).astype(jnp.float32)
            keep = half_lane >= shift
            other = jnp.logical_not(keep)
            sums = []
            for value, inside, beyond, at in (
                (patch[:HALF], canvas, spill, first),
                (patch[HALF:], canvas, spill, first + HALF),
                (fit, canvas_t, spill_t, first),
            ):
                value = pltpu.roll(value, shift, 1)
                for mask, target in ((keep, inside), (other, beyond)):
                    here = target.at[pl.ds(at, HALF), :]
                    sums.append((here, here[...] + value, mask))
            for here, value, mask in sums:
                pltpu.store(here, value, mask=mask)
        return carry

    done = 0
    for group in GROUPS:
        left = count - done + (group - 1 if group == GROUPS[-1] else 0)
        turns = left // group
        lax.fori_loop(0, turns, functools.partial(step, done, group), 0)
        done = done + turns * group

    @pl.when(jnp.logical_not(crowded))
    def _():
        fetches[2].wait()

    rows = OUT_ROWS
    lower = lax.broadcasted_iota(jnp.int32, (rows, 128), 1) < 64

    def mix(low, high):
        return jnp.where(lower, low, high)

    copies = []
    for r in range(0, SIDE, rows):
        for j in range(2):

            def at(ref, block, first):
                start = (block + 2 * j) * CANVAS + ROW_BASE + r + first
                return ref[pl.ds(start, rows), :]

            c1, c2 = at(canvas, 1, 0), at(canvas, 2, 0)
            s1, s2 = at(spill, 0, 0), at(spill, 1, 0)
            here = (slice(r, r + rows), slice(j * 128, j * 128 + 128))
            model = mix(c1, s2) + pltpu.roll(mix(c2, s1), 64, 1)
            residual_ref[(0,) + here] = dirty_ref[(0,) + here] - model
            model = mix(s1, c2) + pltpu.roll(mix(s2, c1), 64, 1)
            residual_ref[(1,) + here] = dirty_ref[(1,) + here] - model
            straight = mix(
                at(canvas_t, 1, 0) + at(spill_t, 0, -HALF), at(canvas_t, 2, -HALF) + at(spill_t, 1, 0)
            )
            crossed = mix(
                at(canvas_t, 2, 0) + at(spill_t, 1, -HALF), at(canvas_t, 1, -HALF) + at(spill_t, 0, 0)
            )
            taylor_ref[here] = fit_ref[here] - (straight + pltpu.roll(crossed, 64, 1))
        part = r // rows
        copies.append(
            pltpu.make_async_copy(
                residual_ref.at[:, pl.ds(r, rows), :], residual_hbm.at[:, pl.ds(r, rows), :],
                out_sems.at[0, part],
            )
        )
        copies.append(
            pltpu.make_async_copy(
                taylor_ref.at[pl.ds(r, rows), :], taylor_hbm.at[pl.ds(r, rows), :],
                out_sems.at[1, part],
            )
        )
        copies[-2].start()
        copies[-1].start()
    for copy in copies:
        copy.wait()


def per_device(dirty, psf, comp_tile, comp_offset, comp_scale, comp_amp, fit_weight):
    n_band, n_ty, n_tx = (lax.axis_size(a) for a in ("band", "ty", "tx"))
    sources, listed = n_ty * n_tx, comp_tile.shape[0]
    lists = max(1, sources * SLOTS // 128)
    vmem = pl.BlockSpec(memory_space=pltpu.VMEM)
    hbm = pl.BlockSpec(memory_space=pltpu.HBM)
    dma = pltpu.SemaphoreType.DMA
    f32, bf16 = jnp.float32, jnp.bfloat16
    value, order, table, taylor_table, fit = pl.pallas_call(
        functools.partial(exchange_kernel, n_band, n_ty, n_tx),
        out_shape=(
            jax.ShapeDtypeStruct((sources // 2 + 8, 128), f32),
            jax.ShapeDtypeStruct((lists, 128), jnp.int32),
            jax.ShapeDtypeStruct((PAD_K * PATCH, 128), f32),
            jax.ShapeDtypeStruct((PAD_K * HALF, 128), f32),
            jax.ShapeDtypeStruct((SIDE, SIDE), f32),
        ),
        in_specs=[hbm] * 7,
        out_specs=(vmem,) * 5,
        scratch_shapes=[
            pltpu.VMEM((1, listed), jnp.int32), pltpu.VMEM((2, listed), jnp.int32),
            pltpu.VMEM((1, listed), jnp.int32), pltpu.VMEM((TAYLOR, listed), f32),
            pltpu.SMEM((2, TAYLOR), f32), pltpu.VMEM((2, SIDE, SIDE), f32),
            pltpu.VMEM((ROWS_K, 2, 2 * WIDE), bf16),
            pltpu.VMEM((n_ty // 2, n_tx, 128), f32),
            pltpu.VMEM((n_ty, n_tx, 128), f32),
            pltpu.VMEM((n_ty, n_tx, 128), f32),
            pltpu.VMEM((2, PAD_K, 2 * WIDE), f32),
            pltpu.VMEM((n_band - 1, SIDE, SIDE), bf16),
            pltpu.VMEM((n_band - 1, SIDE, SIDE), bf16),
            pltpu.VMEM((n_band - 1, PAD_K, WIDE), f32),
            pltpu.VMEM((2, PAD_K, WIDE), f32),
            pltpu.VMEM((n_band - 1, PAD_K, WIDE), f32),
            dma((1,)), dma((1,)), dma((1,)), dma((1,)),
            dma((2, n_band - 1)), dma((2, n_band - 1)),
            dma((2,)), dma((1,)), dma((1,)), dma((7,)),
        ],
        compiler_params=pltpu.CompilerParams(
            collective_id=0, has_side_effects=True, vmem_limit_bytes=24 * 1024 * 1024
        ),
    )(
        *(
            pltpu.with_memory_space_constraint(operand, pltpu.HBM)
            for operand in (
                comp_tile.T, comp_offset.T, comp_scale[None, :], comp_amp.T, fit_weight, dirty,
                psf.transpose(1, 0, 2),
            )
        ),
    )
    residual, taylor = pl.pallas_call(
        render_kernel,
        out_shape=(
            jax.ShapeDtypeStruct((2, SIDE, SIDE), f32),
            jax.ShapeDtypeStruct((SIDE, SIDE), f32),
        ),
        in_specs=[vmem] * 6,
        out_specs=(hbm,) * 2,
        scratch_shapes=[
            pltpu.VMEM(((BLOCKS - 1) * CANVAS, 128), f32) for _ in range(4)
        ] + [
            pltpu.VMEM((2, SIDE, SIDE), f32), pltpu.VMEM((SIDE, SIDE), f32),
            pltpu.SMEM((value.size,), f32), pltpu.SMEM((order.size,), jnp.int32),
            dma((3,)), dma((2, SIDE // OUT_ROWS)),
        ],
        compiler_params=pltpu.CompilerParams(vmem_limit_bytes=24 * 1024 * 1024),
    )(
        value.reshape(-1), order.reshape(-1), table, taylor_table, dirty, fit,
    )
    return residual, taylor[None]


def solution(mesh):
    return jax.shard_map(
        per_device,
        mesh=mesh,
        in_specs=(
            P("band", "ty", "tx"),
            P("band", None, None),
            P(("ty", "tx"), None),
            P(("ty", "tx"), None),
            P(("ty", "tx")),
            P(("ty", "tx"), None),
            P("band", None),
        ),
        out_specs=(P("band", "ty", "tx"), P("band", "ty", "tx")),
        check_vma=False,
    )
```

```python
import functools

import jax
import jax.numpy as jnp
from jax import lax
from jax.experimental import pallas as pl
from jax.experimental.pallas import tpu as pltpu
from jax.sharding import PartitionSpec as P

TAYLOR = 4
SCALES = 5
PATCH = 48
ROWS_K = TAYLOR * SCALES
PAD_K = 24
HALF = PATCH // 2
WIDE = HALF * PATCH
SIDE = 256
SLOTS = 8
WORDS = 8
ROW_BASE = 48
COL_BASE = 64
BLOCKS = 6
CANVAS = 352
GROUPS = (48, 16, 8)
OUT_ROWS = 64
MESH = pl.DeviceIdType.MESH


def sends_of_tiles(tile, off, scale, amp, n_ty, n_tx):
    count = tile.shape[1]
    tiles = n_ty * n_tx
    comp_y = lax.shift_right_logical(tile, n_tx.bit_length() - 1)
    comp_x = lax.bitwise_and(tile, n_tx - 1)
    over_r = (off[0:1] + PATCH > SIDE).astype(jnp.int32)
    over_c = (off[1:2] + PATCH > SIDE).astype(jnp.int32)
    dest = lax.broadcasted_iota(jnp.int32, (tiles, count), 0)
    half = tiles // 2
    bits = n_tx.bit_length() - 1
    core = lax.shift_right_logical(dest, half.bit_length() - 1)
    inner = lax.bitwise_and(dest, half - 1)
    dest_x = lax.bitwise_and(inner, n_tx - 1)
    dest_y = 2 * lax.shift_right_logical(inner, bits) + core
    down, right = dest_y - comp_y, dest_x - comp_x
    touches = ((down == 0) | ((down == 1) & (over_r == 1))) & (
        (right == 0) | ((right == 1) & (over_c == 1))
    )
    before = (
        lax.broadcasted_iota(jnp.int32, (count, count), 0)
        < lax.broadcasted_iota(jnp.int32, (count, count), 1)
    ).astype(jnp.float32)
    rank = jnp.dot(
        jnp.where(touches, 1.0, 0.0).astype(jnp.bfloat16),
        before.astype(jnp.bfloat16),
        preferred_element_type=jnp.float32,
    )
    rank = jnp.where(touches, rank, -1.0)
    chosen = jnp.concatenate(
        [jnp.where(rank == float(k), 1.0, 0.0).astype(jnp.bfloat16) for k in range(SLOTS)], axis=1
    )
    rows = (comp_y * SIDE + off[0:1]).astype(jnp.float32)
    cols = (comp_x * SIDE + off[1:2]).astype(jnp.float32)
    record = jnp.concatenate(
        [rows, cols, scale.astype(jnp.float32), jnp.ones((1, count), jnp.float32), amp], axis=0
    )
    high = record.astype(jnp.bfloat16).astype(jnp.float32)
    rest = record - high
    middle = rest.astype(jnp.bfloat16).astype(jnp.float32)
    low = rest - middle
    place = lax.shift_right_logical(
        lax.broadcasted_iota(jnp.int32, (SLOTS * WORDS, count), 0), 3
    )
    parts = []
    for part in (high, middle, low):
        tall = jnp.concatenate([part] * SLOTS, axis=0)
        parts.append(
            jnp.concatenate([jnp.where(place == k, tall, 0.0) for k in range(SLOTS)], axis=1)
        )
    parts.append(jnp.zeros_like(parts[0]))
    table = jnp.concatenate(parts, axis=0).astype(jnp.bfloat16)
    found = lax.dot_general(
        chosen, table, (((1,), (1,)), ((), ())), preferred_element_type=jnp.float32
    )
    found = found[:, :128] + found[:, 128:]
    found = found + pltpu.roll(found, 64, 1)
    lane = lax.broadcasted_iota(jnp.int32, (half, 128), 1)
    return jnp.where(lane < 64, found[:half], found[half:])


def unrolled(first, last, lane, step):
    tile, shift = divmod(step * PATCH, 128)
    out = []
    for table, base in ((first, 0), (last, 64)):
        value = table(tile)
        if shift + PATCH > 128:
            value = jnp.where(lane >= shift, value, table(tile + 1))
        turn = (base - shift) % 128
        out.append(pltpu.roll(value, turn, 1) if turn else value)
    return jnp.where(
        lane < PATCH, out[0], jnp.where((lane >= 64) & (lane < 64 + PATCH), out[1], 0.0)
    )


def exchange_kernel(
    n_band, n_ty, n_tx,
    tile_hbm, off_hbm, scale_hbm, amp_hbm, weight_hbm, dirty_hbm, psf_hbm,
    value_ref, list_ref, table_ref, taylor_table_ref, fit_ref,
    tile_ref, off_ref, scale_ref, amp_ref, weight_ref, dirty_ref, psf_ref,
    send, cross, got, psf, fit_send, fit_got, tab_send, tab_own, tab_got,
    x_send, x_recv, y_send, y_recv, b_send, b_recv, own_sem, pair_send, pair_recv, load_sem,
):
    me_b, me_y, me_x = lax.axis_index("band"), lax.axis_index("ty"), lax.axis_index("tx")
    barrier = pltpu.get_barrier_semaphore()
    along_x = [lax.rem(me_x + o, n_tx) for o in range(1, n_tx)]
    along_y = [lax.rem(me_y + o, n_ty) for o in range(1, n_ty)]
    along_b = [lax.rem(me_b + o, n_band) for o in range(1, n_band)]
    partners = (
        [(me_b, me_y, x) for x in along_x]
        + [(me_b, y, me_x) for y in along_y]
        + [(b, me_y, me_x) for b in along_b]
    )
    for partner in partners:
        pl.semaphore_signal(barrier, inc=1, device_id=partner, device_id_type=MESH)

    loads = [
        pltpu.make_async_copy(source, target, load_sem.at[i])
        for i, (source, target) in enumerate((
            (tile_hbm, tile_ref), (off_hbm, off_ref), (scale_hbm, scale_ref), (amp_hbm, amp_ref),
            (weight_hbm, weight_ref), (psf_hbm, psf_ref), (dirty_hbm, dirty_ref),
        ))
    ]
    for load in loads:
        load.start()

    for load in loads[:4]:
        load.wait()
    records = sends_of_tiles(tile_ref[...], off_ref[...], scale_ref[...], amp_ref[...], n_ty, n_tx)
    for y in range(n_ty // 2):
        send[y] = records[y * n_tx:(y + 1) * n_tx]

    pl.semaphore_wait(barrier, len(partners))

    def in_all(ref, send_sem, recv_sem, partner):
        return pltpu.make_async_remote_copy(
            src_ref=ref, dst_ref=ref, send_sem=send_sem.at[0], recv_sem=recv_sem.at[0],
            device_id=partner, device_id_type=MESH,
        )

    for y in along_y:
        copy = pltpu.make_async_remote_copy(
            src_ref=send.at[y // 2], dst_ref=cross.at[me_y],
            send_sem=y_send.at[0], recv_sem=y_recv.at[0],
            device_id=(me_b, y, me_x), device_id_type=MESH,
        )
        copy.start()
    stage_y = in_all(cross.at[pl.ds(0, n_ty - 1)], y_send, y_recv, partners[-n_band])
    own = pltpu.make_async_copy(send.at[me_y // 2], cross.at[me_y], own_sem.at[0])
    own.start()
    for load in loads[4:]:
        load.wait()
    for b in range(2):
        psf[b, 0:ROWS_K, :] = psf_ref[:, b, :].astype(jnp.float32)
        psf[b, ROWS_K:PAD_K, :] = jnp.zeros((PAD_K - ROWS_K, 2 * WIDE), jnp.float32)
    core = lax.rem(me_y, 2)
    mine = [
        jnp.where(core == 1, psf[b, :, WIDE:2 * WIDE], psf[b, :, 0:WIDE]) for b in range(2)
    ]
    for o in range(1, n_band):
        w0, w1 = weight_ref[0, along_b[o - 1]], weight_ref[1, along_b[o - 1]]
        tab_send[o - 1] = (w0 * mine[0] + w1 * mine[1])[:ROWS_K]
        fit_send[o - 1] = (w0 * dirty_ref[0] + w1 * dirty_ref[1]).astype(jnp.bfloat16)

    w0, w1 = weight_ref[0, me_b], weight_ref[1, me_b]
    tab_own[core] = w0 * mine[0] + w1 * mine[1]
    lane24 = lax.broadcasted_iota(jnp.int32, (PAD_K, 128), 1)

    def piece(ref, half):
        return lambda t: ref[:, half * WIDE + t * 128:half * WIDE + (t + 1) * 128]

    def band_table(half):
        first, last = piece(psf.at[0], half), piece(psf.at[1], half)
        for step in range(HALF):
            table_ref[pl.ds(half * HALF + step, PAD_K, stride=PATCH), :] = unrolled(
                first, last, lane24, step
            )

    band_table(0)

    stage_t, stage_f = [], []
    for source, target, which, copies in (
        (tab_send, tab_got, 0, stage_t), (fit_send, fit_got, 1, stage_f)
    ):
        for o, b in enumerate(along_b):
            copy = pltpu.make_async_remote_copy(
                src_ref=source.at[o], dst_ref=target.at[o],
                send_sem=b_send.at[which, o], recv_sem=b_recv.at[which, o],
                device_id=(b, me_y, me_x), device_id_type=MESH,
            )
            copy.start()
            copies.append(copy)

    own.wait()
    stage_y.wait_recv()
    for x in along_x:
        copy = pltpu.make_async_remote_copy(
            src_ref=cross.at[:, x, :], dst_ref=got.at[:, me_x, :],
            send_sem=x_send.at[0], recv_sem=x_recv.at[0],
            device_id=(me_b, me_y, x), device_id_type=MESH,
        )
        copy.start()
    stage_x = in_all(got.at[:, pl.ds(0, n_tx - 1), :], x_send, x_recv, partners[0])
    own = pltpu.make_async_copy(cross.at[:, me_x, :], got.at[:, me_x, :], own_sem.at[1])
    own.start()

    for copy in stage_t:
        copy.wait_recv()
    for o in range(n_band - 1):
        tab_own[core, 0:ROWS_K] += tab_got[o]
    band_table(1)
    pair = pltpu.make_async_remote_copy(
        src_ref=tab_own.at[core], dst_ref=tab_own.at[core],
        send_sem=pair_send.at[0], recv_sem=pair_recv.at[0],
        device_id=(me_b, me_y + 1 - 2 * core, me_x), device_id_type=MESH,
    )
    pair.start()

    pair.wait_recv()
    first, last = piece(tab_own.at[0], 0), piece(tab_own.at[1], 0)
    for step in range(HALF):
        taylor_table_ref[pl.ds(step, PAD_K, stride=HALF), :] = unrolled(first, last, lane24, step)

    fit_ref[...] = w0 * dirty_ref[0] + w1 * dirty_ref[1]
    for copy in stage_f:
        copy.wait_recv()
    for o in range(n_band - 1):
        fit_ref[...] += fit_got[o].astype(jnp.float32)
    own.wait()
    stage_x.wait_recv()
    sources = n_ty * n_tx
    slots = jnp.concatenate([got[y] for y in range(n_ty)], axis=0)
    slots = jnp.where(lax.rem(me_y, 2) == 1, pltpu.roll(slots, 64, 1), slots)
    lane = lax.broadcasted_iota(jnp.int32, (sources, 128), 1)
    word = lax.bitwise_and(lane, WORDS - 1)
    move_r = (ROW_BASE - me_y * SIDE).astype(jnp.float32)
    move_c = (COL_BASE - me_x * SIDE).astype(jnp.float32)
    row = jnp.clip(slots + move_r, 0.0, float(ROW_BASE + SIDE)).astype(jnp.int32)
    col = jnp.clip(
        pltpu.roll(slots, 127, 1) + move_c, 0.0, float(COL_BASE + SIDE)
    ).astype(jnp.int32)
    scale = jnp.clip(pltpu.roll(slots, 126, 1), 0.0, float(SCALES)).astype(jnp.int32)
    place = row + lax.shift_right_logical(col, 6) * CANVAS
    place = place + lax.shift_left(lax.bitwise_and(col, 63), 11) + lax.shift_left(scale, 17)
    value = jnp.where(word == 0, place.astype(jnp.float32), slots)
    quarter = sources // 4
    part = lax.shift_right_logical(lax.broadcasted_iota(jnp.int32, (quarter, 128), 1), 5)
    for first, turn in ((0, 0), (quarter + 8, 96)):
        packed = jnp.zeros((quarter, 128), jnp.float32)
        for q in range(4):
            own_rows = value[q * quarter:(q + 1) * quarter]
            moved = (q * 32 + turn) % 128
            packed = jnp.where(part == q, pltpu.roll(own_rows, moved, 1) if moved else own_rows, packed)
        value_ref[first:first + quarter] = packed
    used = jnp.sum(
        jnp.where((word == 3) & (lane < 64), slots, 0.0), axis=1, keepdims=True
    )
    used = jnp.broadcast_to(used, (sources, 128))
    earlier = (
        lax.broadcasted_iota(jnp.int32, (sources, sources), 1)
        < lax.broadcasted_iota(jnp.int32, (sources, sources), 0)
    ).astype(jnp.float32).astype(jnp.bfloat16)
    start = jnp.dot(earlier, used.astype(jnp.bfloat16), preferred_element_type=jnp.float32)
    end = start + used
    lists = max(1, sources * SLOTS // 128)
    for i in range(lists):
        order = (lane + i * 128).astype(jnp.float32)
        source = jnp.sum(jnp.where(end <= order, 1.0, 0.0), axis=0, keepdims=True)
        base = jnp.max(jnp.where(start <= order, start, 0.0), axis=0, keepdims=True)
        group = sum(jnp.where(source >= float(q * quarter), 1.0, 0.0) for q in (1, 2, 3))
        slot = order[0:1] - base
        far = jnp.where(slot >= 4.0, 1.0, 0.0)
        index = (source - group * quarter + far * (quarter + 8)) * 128.0 + group * 32.0
        index = index + (slot - 4.0 * far) * WORDS
        index = jnp.where(source < float(sources), index, float(quarter * 128))
        list_ref[i:i + 1, :] = index.astype(jnp.int32)
    spot = lax.broadcasted_iota(jnp.int32, (8, 128), 1)
    count = end[sources - 1:sources]
    most = jnp.max(used, axis=0, keepdims=True)
    value_ref[quarter:quarter + 8] = jnp.where(
        spot == WORDS, count, jnp.where(spot == WORDS + 1, most, 0.0)
    )

    for copy in [stage_x, stage_y, pair] + stage_t + stage_f:
        copy.wait_send()


def render_kernel(
    value_ref, order_ref, table_ref, taylor_table_ref, dirty_ref, fit_ref,
    residual_hbm, taylor_hbm,
    canvas, spill, canvas_t, spill_t, residual_ref, taylor_ref, amp_ref, list_ref, sems, out_sems,
):
    near = (value_ref.shape[0] + 1024) // 2
    ends = (pl.ds(0, near), pl.ds(near, value_ref.shape[0] - near))
    fetches = [
        pltpu.make_async_copy(value_ref.at[ends[0]], amp_ref.at[ends[0]], sems.at[0]),
        pltpu.make_async_copy(order_ref, list_ref, sems.at[1]),
        pltpu.make_async_copy(value_ref.at[ends[1]], amp_ref.at[ends[1]], sems.at[2]),
    ]
    for fetch in fetches:
        fetch.start()
    for block in range(BLOCKS - 1):
        for ref, used, first in (
            (canvas, block > 0, ROW_BASE), (spill, block < 4, ROW_BASE),
            (canvas_t, block > 0, ROW_BASE - HALF), (spill_t, block < 4, ROW_BASE - HALF),
        ):
            if used:
                rows = ROW_BASE + SIDE - first
                ref[pl.ds(block * CANVAS + first, rows), :] = jnp.zeros((rows, 128), jnp.float32)
    for fetch in fetches[:2]:
        fetch.wait()
    half_lane = lax.bitwise_and(lax.broadcasted_iota(jnp.int32, (HALF, 128), 1), 63)
    count = amp_ref[near - 1024 + WORDS].astype(jnp.int32)
    crowded = amp_ref[near - 1024 + WORDS + 1] > 4.0

    @pl.when(crowded)
    def _():
        fetches[2].wait()


    def step(first_of_all, group, index, carry):
        for g in range(group):
            slot = list_ref[first_of_all + index * group + g]
            packed = amp_ref[slot].astype(jnp.int32)
            amps = [amp_ref[slot + 4 + t] for t in range(TAYLOR)]
            first = lax.bitwise_and(packed, 2047)
            shift = lax.bitwise_and(lax.shift_right_logical(packed, 11), 63)
            base = lax.shift_right_logical(packed, 17) * HALF
            low = pl.multiple_of(base, HALF)
            high = pl.multiple_of(2 * base, PATCH)
            patch = fit = None
            for t in range(TAYLOR):
                term = amps[t] * table_ref[pl.ds(high + t * SCALES * PATCH, PATCH), :]
                patch = term if t == 0 else patch + term
                term = amps[t] * taylor_table_ref[pl.ds(low + t * SCALES * HALF, HALF), :]
                fit = term if t == 0 else fit + term
            patch = patch.astype(jnp.bfloat16).astype(jnp.float32)
            keep = half_lane >= shift
            other = jnp.logical_not(keep)
            sums = []
            for value, inside, beyond, at in (
                (patch[:HALF], canvas, spill, first),
                (patch[HALF:], canvas, spill, first + HALF),
                (fit, canvas_t, spill_t, first),
            ):
                value = pltpu.roll(value, shift, 1)
                for mask, target in ((keep, inside), (other, beyond)):
                    here = target.at[pl.ds(at, HALF), :]
                    sums.append((here, here[...] + value, mask))
            for here, value, mask in sums:
                pltpu.store(here, value, mask=mask)
        return carry

    done = 0
    for group in GROUPS:
        left = count - done + (group - 1 if group == GROUPS[-1] else 0)
        turns = left // group
        lax.fori_loop(0, turns, functools.partial(step, done, group), 0)
        done = done + turns * group

    @pl.when(jnp.logical_not(crowded))
    def _():
        fetches[2].wait()

    rows = OUT_ROWS
    lower = lax.broadcasted_iota(jnp.int32, (rows, 128), 1) < 64

    def mix(low, high):
        return jnp.where(lower, low, high)

    copies = []
    for r in range(0, SIDE, rows):
        for j in range(2):

            def at(ref, block, first):
                start = (block + 2 * j) * CANVAS + ROW_BASE + r + first
                return ref[pl.ds(start, rows), :]

            c1, c2 = at(canvas, 1, 0), at(canvas, 2, 0)
            s1, s2 = at(spill, 0, 0), at(spill, 1, 0)
            here = (slice(r, r + rows), slice(j * 128, j * 128 + 128))
            model = mix(c1, s2) + pltpu.roll(mix(c2, s1), 64, 1)
            residual_ref[(0,) + here] = dirty_ref[(0,) + here] - model
            model = mix(s1, c2) + pltpu.roll(mix(s2, c1), 64, 1)
            residual_ref[(1,) + here] = dirty_ref[(1,) + here] - model
            straight = mix(
                at(canvas_t, 1, 0) + at(spill_t, 0, -HALF), at(canvas_t, 2, -HALF) + at(spill_t, 1, 0)
            )
            crossed = mix(
                at(canvas_t, 2, 0) + at(spill_t, 1, -HALF), at(canvas_t, 1, -HALF) + at(spill_t, 0, 0)
            )
            taylor_ref[here] = fit_ref[here] - (straight + pltpu.roll(crossed, 64, 1))
        part = r // rows
        copies.append(
            pltpu.make_async_copy(
                residual_ref.at[:, pl.ds(r, rows), :], residual_hbm.at[:, pl.ds(r, rows), :],
                out_sems.at[0, part],
            )
        )
        copies.append(
            pltpu.make_async_copy(
                taylor_ref.at[pl.ds(r, rows), :], taylor_hbm.at[pl.ds(r, rows), :],
                out_sems.at[1, part],
            )
        )
        copies[-2].start()
        copies[-1].start()
    for copy in copies:
        copy.wait()


def per_device(dirty, psf, comp_tile, comp_offset, comp_scale, comp_amp, fit_weight):
    n_band, n_ty, n_tx = (lax.axis_size(a) for a in ("band", "ty", "tx"))
    sources, listed = n_ty * n_tx, comp_tile.shape[0]
    lists = max(1, sources * SLOTS // 128)
    vmem = pl.BlockSpec(memory_space=pltpu.VMEM)
    hbm = pl.BlockSpec(memory_space=pltpu.HBM)
    dma = pltpu.SemaphoreType.DMA
    f32, bf16 = jnp.float32, jnp.bfloat16
    value, order, table, taylor_table, fit = pl.pallas_call(
        functools.partial(exchange_kernel, n_band, n_ty, n_tx),
        out_shape=(
            jax.ShapeDtypeStruct((sources // 2 + 8, 128), f32),
            jax.ShapeDtypeStruct((lists, 128), jnp.int32),
            jax.ShapeDtypeStruct((PAD_K * PATCH, 128), f32),
            jax.ShapeDtypeStruct((PAD_K * HALF, 128), f32),
            jax.ShapeDtypeStruct((SIDE, SIDE), f32),
        ),
        in_specs=[hbm] * 7,
        out_specs=(vmem,) * 5,
        scratch_shapes=[
            pltpu.VMEM((1, listed), jnp.int32), pltpu.VMEM((2, listed), jnp.int32),
            pltpu.VMEM((1, listed), jnp.int32), pltpu.VMEM((TAYLOR, listed), f32),
            pltpu.SMEM((2, TAYLOR), f32), pltpu.VMEM((2, SIDE, SIDE), f32),
            pltpu.VMEM((ROWS_K, 2, 2 * WIDE), bf16),
            pltpu.VMEM((n_ty // 2, n_tx, 128), f32),
            pltpu.VMEM((n_ty, n_tx, 128), f32),
            pltpu.VMEM((n_ty, n_tx, 128), f32),
            pltpu.VMEM((2, PAD_K, 2 * WIDE), f32),
            pltpu.VMEM((n_band - 1, SIDE, SIDE), bf16),
            pltpu.VMEM((n_band - 1, SIDE, SIDE), bf16),
            pltpu.VMEM((n_band - 1, ROWS_K, WIDE), f32),
            pltpu.VMEM((2, PAD_K, WIDE), f32),
            pltpu.VMEM((n_band - 1, ROWS_K, WIDE), f32),
            dma((1,)), dma((1,)), dma((1,)), dma((1,)),
            dma((2, n_band - 1)), dma((2, n_band - 1)),
            dma((2,)), dma((1,)), dma((1,)), dma((7,)),
        ],
        compiler_params=pltpu.CompilerParams(
            collective_id=0, has_side_effects=True, vmem_limit_bytes=24 * 1024 * 1024
        ),
    )(
        *(
            pltpu.with_memory_space_constraint(operand, pltpu.HBM)
            for operand in (
                comp_tile.T, comp_offset.T, comp_scale[None, :], comp_amp.T, fit_weight, dirty,
                psf.transpose(1, 0, 2),
            )
        ),
    )
    residual, taylor = pl.pallas_call(
        render_kernel,
        out_shape=(
            jax.ShapeDtypeStruct((2, SIDE, SIDE), f32),
            jax.ShapeDtypeStruct((SIDE, SIDE), f32),
        ),
        in_specs=[vmem] * 6,
        out_specs=(hbm,) * 2,
        scratch_shapes=[
            pltpu.VMEM(((BLOCKS - 1) * CANVAS, 128), f32) for _ in range(4)
        ] + [
            pltpu.VMEM((2, SIDE, SIDE), f32), pltpu.VMEM((SIDE, SIDE), f32),
            pltpu.SMEM((value.size,), f32), pltpu.SMEM((order.size,), jnp.int32),
            dma((3,)), dma((2, SIDE // OUT_ROWS)),
        ],
        compiler_params=pltpu.CompilerParams(vmem_limit_bytes=24 * 1024 * 1024),
    )(
        value.reshape(-1), order.reshape(-1), table, taylor_table, dirty, fit,
    )
    return residual, taylor[None]


def solution(mesh):
    return jax.shard_map(
        per_device,
        mesh=mesh,
        in_specs=(
            P("band", "ty", "tx"),
            P("band", None, None),
            P(("ty", "tx"), None),
            P(("ty", "tx"), None),
            P(("ty", "tx")),
            P(("ty", "tx"), None),
            P("band", None),
        ),
        out_specs=(P("band", "ty", "tx"), P("band", "ty", "tx")),
        check_vma=False,
    )
```

```python
import functools

import jax
import jax.numpy as jnp
from jax import lax
from jax.experimental import pallas as pl
from jax.experimental.pallas import tpu as pltpu
from jax.sharding import PartitionSpec as P

TAYLOR = 4
SCALES = 5
PATCH = 48
ROWS_K = TAYLOR * SCALES
PAD_K = 24
HALF = PATCH // 2
WIDE = HALF * PATCH
SIDE = 256
SLOTS = 8
WORDS = 8
ROW_BASE = 48
COL_BASE = 64
BLOCKS = 6
CANVAS = 352
GROUPS = (48, 16, 8)
OUT_ROWS = 64
MESH = pl.DeviceIdType.MESH


def sends_of_tiles(tile, off, scale, amp, n_ty, n_tx):
    count = tile.shape[1]
    tiles = n_ty * n_tx
    comp_y = lax.shift_right_logical(tile, n_tx.bit_length() - 1)
    comp_x = lax.bitwise_and(tile, n_tx - 1)
    over_r = (off[0:1] + PATCH > SIDE).astype(jnp.int32)
    over_c = (off[1:2] + PATCH > SIDE).astype(jnp.int32)
    dest = lax.broadcasted_iota(jnp.int32, (tiles, count), 0)
    half = tiles // 2
    bits = n_tx.bit_length() - 1
    core = lax.shift_right_logical(dest, half.bit_length() - 1)
    inner = lax.bitwise_and(dest, half - 1)
    dest_x = lax.bitwise_and(inner, n_tx - 1)
    dest_y = 2 * lax.shift_right_logical(inner, bits) + core
    down, right = dest_y - comp_y, dest_x - comp_x
    touches = ((down == 0) | ((down == 1) & (over_r == 1))) & (
        (right == 0) | ((right == 1) & (over_c == 1))
    )
    before = (
        lax.broadcasted_iota(jnp.int32, (count, count), 0)
        < lax.broadcasted_iota(jnp.int32, (count, count), 1)
    ).astype(jnp.float32)
    rank = jnp.dot(
        jnp.where(touches, 1.0, 0.0).astype(jnp.bfloat16),
        before.astype(jnp.bfloat16),
        preferred_element_type=jnp.float32,
    )
    rank = jnp.where(touches, rank, -1.0)
    chosen = jnp.concatenate(
        [jnp.where(rank == float(k), 1.0, 0.0).astype(jnp.bfloat16) for k in range(SLOTS)], axis=1
    )
    rows = (comp_y * SIDE + off[0:1]).astype(jnp.float32)
    cols = (comp_x * SIDE + off[1:2]).astype(jnp.float32)
    record = jnp.concatenate(
        [rows, cols, scale.astype(jnp.float32), jnp.ones((1, count), jnp.float32), amp], axis=0
    )
    high = record.astype(jnp.bfloat16).astype(jnp.float32)
    rest = record - high
    middle = rest.astype(jnp.bfloat16).astype(jnp.float32)
    low = rest - middle
    place = lax.shift_right_logical(
        lax.broadcasted_iota(jnp.int32, (SLOTS * WORDS, count), 0), 3
    )
    parts = []
    for part in (high, middle, low):
        tall = jnp.concatenate([part] * SLOTS, axis=0)
        parts.append(
            jnp.concatenate([jnp.where(place == k, tall, 0.0) for k in range(SLOTS)], axis=1)
        )
    parts.append(jnp.zeros_like(parts[0]))
    table = jnp.concatenate(parts, axis=0).astype(jnp.bfloat16)
    found = lax.dot_general(
        chosen, table, (((1,), (1,)), ((), ())), preferred_element_type=jnp.float32
    )
    found = found[:, :128] + found[:, 128:]
    found = found + pltpu.roll(found, 64, 1)
    lane = lax.broadcasted_iota(jnp.int32, (half, 128), 1)
    return jnp.where(lane < 64, found[:half], found[half:])


def unrolled(first, last, lane, step):
    tile, shift = divmod(step * PATCH, 128)
    out = []
    for table, base in ((first, 0), (last, 64)):
        value = table(tile)
        if shift + PATCH > 128:
            value = jnp.where(lane >= shift, value, table(tile + 1))
        turn = (base - shift) % 128
        out.append(pltpu.roll(value, turn, 1) if turn else value)
    return jnp.where(
        lane < PATCH, out[0], jnp.where((lane >= 64) & (lane < 64 + PATCH), out[1], 0.0)
    )


def exchange_kernel(
    n_band, n_ty, n_tx,
    tile_hbm, off_hbm, scale_hbm, amp_hbm, weight_hbm, dirty_hbm, psf_hbm,
    value_ref, list_ref, table_ref, taylor_table_ref, fit_ref,
    tile_ref, off_ref, scale_ref, amp_ref, weight_ref, dirty_ref, psf_ref,
    send, cross, got, psf, fit_send, fit_got, tab_send, tab_own, tab_got,
    x_send, x_recv, y_send, y_recv, b_send, b_recv, own_sem, pair_send, pair_recv, load_sem,
):
    me_b, me_y, me_x = lax.axis_index("band"), lax.axis_index("ty"), lax.axis_index("tx")
    barrier = pltpu.get_barrier_semaphore()
    def far_first(count):
        return sorted(range(1, count), key=lambda o: -min(o, count - o))

    along_x = [lax.rem(me_x + o, n_tx) for o in far_first(n_tx)]
    along_y = [lax.rem(me_y + o, n_ty) for o in far_first(n_ty)]
    along_b = [lax.rem(me_b + o, n_band) for o in range(1, n_band)]
    partners = (
        [(me_b, y, me_x) for y in along_y]
        + [(me_b, me_y, x) for x in along_x]
        + [(b, me_y, me_x) for b in along_b]
    )
    for partner in partners:
        pl.semaphore_signal(barrier, inc=1, device_id=partner, device_id_type=MESH)

    loads = [
        pltpu.make_async_copy(source, target, load_sem.at[i])
        for i, (source, target) in enumerate((
            (tile_hbm, tile_ref), (off_hbm, off_ref), (scale_hbm, scale_ref), (amp_hbm, amp_ref),
            (weight_hbm, weight_ref), (psf_hbm, psf_ref), (dirty_hbm, dirty_ref),
        ))
    ]
    for load in loads:
        load.start()

    for load in loads[:4]:
        load.wait()
    records = sends_of_tiles(tile_ref[...], off_ref[...], scale_ref[...], amp_ref[...], n_ty, n_tx)
    for y in range(n_ty // 2):
        send[y] = records[y * n_tx:(y + 1) * n_tx]

    pl.semaphore_wait(barrier, len(partners))

    def in_all(ref, send_sem, recv_sem, partner):
        return pltpu.make_async_remote_copy(
            src_ref=ref, dst_ref=ref, send_sem=send_sem.at[0], recv_sem=recv_sem.at[0],
            device_id=partner, device_id_type=MESH,
        )

    for y in along_y:
        copy = pltpu.make_async_remote_copy(
            src_ref=send.at[y // 2], dst_ref=cross.at[me_y],
            send_sem=y_send.at[0], recv_sem=y_recv.at[0],
            device_id=(me_b, y, me_x), device_id_type=MESH,
        )
        copy.start()
    stage_y = in_all(cross.at[pl.ds(0, n_ty - 1)], y_send, y_recv, partners[0])
    own = pltpu.make_async_copy(send.at[me_y // 2], cross.at[me_y], own_sem.at[0])
    own.start()
    for load in loads[4:]:
        load.wait()
    for b in range(2):
        psf[b, 0:ROWS_K, :] = psf_ref[:, b, :].astype(jnp.float32)
        psf[b, ROWS_K:PAD_K, :] = jnp.zeros((PAD_K - ROWS_K, 2 * WIDE), jnp.float32)
    core = lax.rem(me_y, 2)
    mine = [
        jnp.where(core == 1, psf[b, :, WIDE:2 * WIDE], psf[b, :, 0:WIDE]) for b in range(2)
    ]
    for o in range(1, n_band):
        w0, w1 = weight_ref[0, along_b[o - 1]], weight_ref[1, along_b[o - 1]]
        tab_send[o - 1] = (w0 * mine[0] + w1 * mine[1])[:ROWS_K]
        fit_send[o - 1] = (w0 * dirty_ref[0] + w1 * dirty_ref[1]).astype(jnp.bfloat16)

    w0, w1 = weight_ref[0, me_b], weight_ref[1, me_b]
    tab_own[core] = w0 * mine[0] + w1 * mine[1]
    lane24 = lax.broadcasted_iota(jnp.int32, (PAD_K, 128), 1)

    def piece(ref, half):
        return lambda t: ref[:, half * WIDE + t * 128:half * WIDE + (t + 1) * 128]

    def band_table(half):
        first, last = piece(psf.at[0], half), piece(psf.at[1], half)
        for step in range(HALF):
            table_ref[pl.ds(half * HALF + step, PAD_K, stride=PATCH), :] = unrolled(
                first, last, lane24, step
            )

    band_table(0)

    stage_t, stage_f = [], []
    for source, target, which, copies in (
        (tab_send, tab_got, 0, stage_t), (fit_send, fit_got, 1, stage_f)
    ):
        for o, b in enumerate(along_b):
            copy = pltpu.make_async_remote_copy(
                src_ref=source.at[o], dst_ref=target.at[o],
                send_sem=b_send.at[which, o], recv_sem=b_recv.at[which, o],
                device_id=(b, me_y, me_x), device_id_type=MESH,
            )
            copy.start()
            copies.append(copy)

    own.wait()
    stage_y.wait_recv()
    for x in along_x:
        copy = pltpu.make_async_remote_copy(
            src_ref=cross.at[:, x, :], dst_ref=got.at[:, me_x, :],
            send_sem=x_send.at[0], recv_sem=x_recv.at[0],
            device_id=(me_b, me_y, x), device_id_type=MESH,
        )
        copy.start()
    stage_x = in_all(got.at[:, pl.ds(0, n_tx - 1), :], x_send, x_recv, partners[-n_band])
    own = pltpu.make_async_copy(cross.at[:, me_x, :], got.at[:, me_x, :], own_sem.at[1])
    own.start()

    for copy in stage_t:
        copy.wait_recv()
    for o in range(n_band - 1):
        tab_own[core, 0:ROWS_K] += tab_got[o]
    band_table(1)
    pair = pltpu.make_async_remote_copy(
        src_ref=tab_own.at[core], dst_ref=tab_own.at[core],
        send_sem=pair_send.at[0], recv_sem=pair_recv.at[0],
        device_id=(me_b, me_y + 1 - 2 * core, me_x), device_id_type=MESH,
    )
    pair.start()

    pair.wait_recv()
    first, last = piece(tab_own.at[0], 0), piece(tab_own.at[1], 0)
    for step in range(HALF):
        taylor_table_ref[pl.ds(step, PAD_K, stride=HALF), :] = unrolled(first, last, lane24, step)

    fit_ref[...] = w0 * dirty_ref[0] + w1 * dirty_ref[1]
    for copy in stage_f:
        copy.wait_recv()
    for o in range(n_band - 1):
        fit_ref[...] += fit_got[o].astype(jnp.float32)
    own.wait()
    stage_x.wait_recv()
    sources = n_ty * n_tx
    slots = jnp.concatenate([got[y] for y in range(n_ty)], axis=0)
    slots = jnp.where(lax.rem(me_y, 2) == 1, pltpu.roll(slots, 64, 1), slots)
    lane = lax.broadcasted_iota(jnp.int32, (sources, 128), 1)
    word = lax.bitwise_and(lane, WORDS - 1)
    move_r = (ROW_BASE - me_y * SIDE).astype(jnp.float32)
    move_c = (COL_BASE - me_x * SIDE).astype(jnp.float32)
    row = jnp.clip(slots + move_r, 0.0, float(ROW_BASE + SIDE)).astype(jnp.int32)
    col = jnp.clip(
        pltpu.roll(slots, 127, 1) + move_c, 0.0, float(COL_BASE + SIDE)
    ).astype(jnp.int32)
    scale = jnp.clip(pltpu.roll(slots, 126, 1), 0.0, float(SCALES)).astype(jnp.int32)
    place = row + lax.shift_right_logical(col, 6) * CANVAS
    place = place + lax.shift_left(lax.bitwise_and(col, 63), 11) + lax.shift_left(scale, 17)
    value = jnp.where(word == 0, place.astype(jnp.float32), slots)
    quarter = sources // 4
    part = lax.shift_right_logical(lax.broadcasted_iota(jnp.int32, (quarter, 128), 1), 5)
    for first, turn in ((0, 0), (quarter + 8, 96)):
        packed = jnp.zeros((quarter, 128), jnp.float32)
        for q in range(4):
            own_rows = value[q * quarter:(q + 1) * quarter]
            moved = (q * 32 + turn) % 128
            packed = jnp.where(part == q, pltpu.roll(own_rows, moved, 1) if moved else own_rows, packed)
        value_ref[first:first + quarter] = packed
    used = jnp.sum(
        jnp.where((word == 3) & (lane < 64), slots, 0.0), axis=1, keepdims=True
    )
    used = jnp.broadcast_to(used, (sources, 128))
    earlier = (
        lax.broadcasted_iota(jnp.int32, (sources, sources), 1)
        < lax.broadcasted_iota(jnp.int32, (sources, sources), 0)
    ).astype(jnp.float32).astype(jnp.bfloat16)
    start = jnp.dot(earlier, used.astype(jnp.bfloat16), preferred_element_type=jnp.float32)
    end = start + used
    lists = max(1, sources * SLOTS // 128)
    for i in range(lists):
        order = (lane + i * 128).astype(jnp.float32)
        source = jnp.sum(jnp.where(end <= order, 1.0, 0.0), axis=0, keepdims=True)
        base = jnp.max(jnp.where(start <= order, start, 0.0), axis=0, keepdims=True)
        group = sum(jnp.where(source >= float(q * quarter), 1.0, 0.0) for q in (1, 2, 3))
        slot = order[0:1] - base
        far = jnp.where(slot >= 4.0, 1.0, 0.0)
        index = (source - group * quarter + far * (quarter + 8)) * 128.0 + group * 32.0
        index = index + (slot - 4.0 * far) * WORDS
        index = jnp.where(source < float(sources), index, float(quarter * 128))
        list_ref[i:i + 1, :] = index.astype(jnp.int32)
    spot = lax.broadcasted_iota(jnp.int32, (8, 128), 1)
    count = end[sources - 1:sources]
    most = jnp.max(used, axis=0, keepdims=True)
    value_ref[quarter:quarter + 8] = jnp.where(
        spot == WORDS, count, jnp.where(spot == WORDS + 1, most, 0.0)
    )

    for copy in [stage_x, stage_y, pair] + stage_t + stage_f:
        copy.wait_send()


def render_kernel(
    value_ref, order_ref, table_ref, taylor_table_ref, dirty_ref, fit_ref,
    residual_hbm, taylor_hbm,
    canvas, spill, canvas_t, spill_t, residual_ref, taylor_ref, amp_ref, list_ref, sems, out_sems,
):
    near = (value_ref.shape[0] + 1024) // 2
    ends = (pl.ds(0, near), pl.ds(near, value_ref.shape[0] - near))
    fetches = [
        pltpu.make_async_copy(value_ref.at[ends[0]], amp_ref.at[ends[0]], sems.at[0]),
        pltpu.make_async_copy(order_ref, list_ref, sems.at[1]),
        pltpu.make_async_copy(value_ref.at[ends[1]], amp_ref.at[ends[1]], sems.at[2]),
    ]
    for fetch in fetches:
        fetch.start()
    for block in range(BLOCKS - 1):
        for ref, used, first in (
            (canvas, block > 0, ROW_BASE), (spill, block < 4, ROW_BASE),
            (canvas_t, block > 0, ROW_BASE - HALF), (spill_t, block < 4, ROW_BASE - HALF),
        ):
            if used:
                rows = ROW_BASE + SIDE - first
                ref[pl.ds(block * CANVAS + first, rows), :] = jnp.zeros((rows, 128), jnp.float32)
    for fetch in fetches[:2]:
        fetch.wait()
    half_lane = lax.bitwise_and(lax.broadcasted_iota(jnp.int32, (HALF, 128), 1), 63)
    count = amp_ref[near - 1024 + WORDS].astype(jnp.int32)
    crowded = amp_ref[near - 1024 + WORDS + 1] > 4.0

    @pl.when(crowded)
    def _():
        fetches[2].wait()


    def step(first_of_all, group, index, carry):
        for g in range(group):
            slot = list_ref[first_of_all + index * group + g]
            packed = amp_ref[slot].astype(jnp.int32)
            amps = [amp_ref[slot + 4 + t] for t in range(TAYLOR)]
            first = lax.bitwise_and(packed, 2047)
            shift = lax.bitwise_and(lax.shift_right_logical(packed, 11), 63)
            base = lax.shift_right_logical(packed, 17) * HALF
            low = pl.multiple_of(base, HALF)
            high = pl.multiple_of(2 * base, PATCH)
            patch = fit = None
            for t in range(TAYLOR):
                term = amps[t] * table_ref[pl.ds(high + t * SCALES * PATCH, PATCH), :]
                patch = term if t == 0 else patch + term
                term = amps[t] * taylor_table_ref[pl.ds(low + t * SCALES * HALF, HALF), :]
                fit = term if t == 0 else fit + term
            patch = patch.astype(jnp.bfloat16).astype(jnp.float32)
            keep = half_lane >= shift
            other = jnp.logical_not(keep)
            sums = []
            for value, inside, beyond, at in (
                (patch[:HALF], canvas, spill, first),
                (patch[HALF:], canvas, spill, first + HALF),
                (fit, canvas_t, spill_t, first),
            ):
                value = pltpu.roll(value, shift, 1)
                for mask, target in ((keep, inside), (other, beyond)):
                    here = target.at[pl.ds(at, HALF), :]
                    sums.append((here, here[...] + value, mask))
            for here, value, mask in sums:
                pltpu.store(here, value, mask=mask)
        return carry

    done = 0
    for group in GROUPS:
        left = count - done + (group - 1 if group == GROUPS[-1] else 0)
        turns = left // group
        lax.fori_loop(0, turns, functools.partial(step, done, group), 0)
        done = done + turns * group

    @pl.when(jnp.logical_not(crowded))
    def _():
        fetches[2].wait()

    rows = OUT_ROWS
    lower = lax.broadcasted_iota(jnp.int32, (rows, 128), 1) < 64

    def mix(low, high):
        return jnp.where(lower, low, high)

    copies = []
    for r in range(0, SIDE, rows):
        for j in range(2):

            def at(ref, block, first):
                start = (block + 2 * j) * CANVAS + ROW_BASE + r + first
                return ref[pl.ds(start, rows), :]

            c1, c2 = at(canvas, 1, 0), at(canvas, 2, 0)
            s1, s2 = at(spill, 0, 0), at(spill, 1, 0)
            here = (slice(r, r + rows), slice(j * 128, j * 128 + 128))
            model = mix(c1, s2) + pltpu.roll(mix(c2, s1), 64, 1)
            residual_ref[(0,) + here] = dirty_ref[(0,) + here] - model
            model = mix(s1, c2) + pltpu.roll(mix(s2, c1), 64, 1)
            residual_ref[(1,) + here] = dirty_ref[(1,) + here] - model
            straight = mix(
                at(canvas_t, 1, 0) + at(spill_t, 0, -HALF), at(canvas_t, 2, -HALF) + at(spill_t, 1, 0)
            )
            crossed = mix(
                at(canvas_t, 2, 0) + at(spill_t, 1, -HALF), at(canvas_t, 1, -HALF) + at(spill_t, 0, 0)
            )
            taylor_ref[here] = fit_ref[here] - (straight + pltpu.roll(crossed, 64, 1))
        part = r // rows
        copies.append(
            pltpu.make_async_copy(
                residual_ref.at[:, pl.ds(r, rows), :], residual_hbm.at[:, pl.ds(r, rows), :],
                out_sems.at[0, part],
            )
        )
        copies.append(
            pltpu.make_async_copy(
                taylor_ref.at[pl.ds(r, rows), :], taylor_hbm.at[pl.ds(r, rows), :],
                out_sems.at[1, part],
            )
        )
        copies[-2].start()
        copies[-1].start()
    for copy in copies:
        copy.wait()


def per_device(dirty, psf, comp_tile, comp_offset, comp_scale, comp_amp, fit_weight):
    n_band, n_ty, n_tx = (lax.axis_size(a) for a in ("band", "ty", "tx"))
    sources, listed = n_ty * n_tx, comp_tile.shape[0]
    lists = max(1, sources * SLOTS // 128)
    vmem = pl.BlockSpec(memory_space=pltpu.VMEM)
    hbm = pl.BlockSpec(memory_space=pltpu.HBM)
    dma = pltpu.SemaphoreType.DMA
    f32, bf16 = jnp.float32, jnp.bfloat16
    value, order, table, taylor_table, fit = pl.pallas_call(
        functools.partial(exchange_kernel, n_band, n_ty, n_tx),
        out_shape=(
            jax.ShapeDtypeStruct((sources // 2 + 8, 128), f32),
            jax.ShapeDtypeStruct((lists, 128), jnp.int32),
            jax.ShapeDtypeStruct((PAD_K * PATCH, 128), f32),
            jax.ShapeDtypeStruct((PAD_K * HALF, 128), f32),
            jax.ShapeDtypeStruct((SIDE, SIDE), f32),
        ),
        in_specs=[hbm] * 7,
        out_specs=(vmem,) * 5,
        scratch_shapes=[
            pltpu.VMEM((1, listed), jnp.int32), pltpu.VMEM((2, listed), jnp.int32),
            pltpu.VMEM((1, listed), jnp.int32), pltpu.VMEM((TAYLOR, listed), f32),
            pltpu.SMEM((2, TAYLOR), f32), pltpu.VMEM((2, SIDE, SIDE), f32),
            pltpu.VMEM((ROWS_K, 2, 2 * WIDE), bf16),
            pltpu.VMEM((n_ty // 2, n_tx, 128), f32),
            pltpu.VMEM((n_ty, n_tx, 128), f32),
            pltpu.VMEM((n_ty, n_tx, 128), f32),
            pltpu.VMEM((2, PAD_K, 2 * WIDE), f32),
            pltpu.VMEM((n_band - 1, SIDE, SIDE), bf16),
            pltpu.VMEM((n_band - 1, SIDE, SIDE), bf16),
            pltpu.VMEM((n_band - 1, ROWS_K, WIDE), f32),
            pltpu.VMEM((2, PAD_K, WIDE), f32),
            pltpu.VMEM((n_band - 1, ROWS_K, WIDE), f32),
            dma((1,)), dma((1,)), dma((1,)), dma((1,)),
            dma((2, n_band - 1)), dma((2, n_band - 1)),
            dma((2,)), dma((1,)), dma((1,)), dma((7,)),
        ],
        compiler_params=pltpu.CompilerParams(
            collective_id=0, has_side_effects=True, vmem_limit_bytes=24 * 1024 * 1024
        ),
    )(
        *(
            pltpu.with_memory_space_constraint(operand, pltpu.HBM)
            for operand in (
                comp_tile.T, comp_offset.T, comp_scale[None, :], comp_amp.T, fit_weight, dirty,
                psf.transpose(1, 0, 2),
            )
        ),
    )
    residual, taylor = pl.pallas_call(
        render_kernel,
        out_shape=(
            jax.ShapeDtypeStruct((2, SIDE, SIDE), f32),
            jax.ShapeDtypeStruct((SIDE, SIDE), f32),
        ),
        in_specs=[vmem] * 6,
        out_specs=(hbm,) * 2,
        scratch_shapes=[
            pltpu.VMEM(((BLOCKS - 1) * CANVAS, 128), f32) for _ in range(4)
        ] + [
            pltpu.VMEM((2, SIDE, SIDE), f32), pltpu.VMEM((SIDE, SIDE), f32),
            pltpu.SMEM((value.size,), f32), pltpu.SMEM((order.size,), jnp.int32),
            dma((3,)), dma((2, SIDE // OUT_ROWS)),
        ],
        compiler_params=pltpu.CompilerParams(vmem_limit_bytes=24 * 1024 * 1024),
    )(
        value.reshape(-1), order.reshape(-1), table, taylor_table, dirty, fit,
    )
    return residual, taylor[None]


def solution(mesh):
    return jax.shard_map(
        per_device,
        mesh=mesh,
        in_specs=(
            P("band", "ty", "tx"),
            P("band", None, None),
            P(("ty", "tx"), None),
            P(("ty", "tx"), None),
            P(("ty", "tx")),
            P(("ty", "tx"), None),
            P("band", None),
        ),
        out_specs=(P("band", "ty", "tx"), P("band", "ty", "tx")),
        check_vma=False,
    )
```

```python
import functools

import jax
import jax.numpy as jnp
from jax import lax
from jax.experimental import pallas as pl
from jax.experimental.pallas import tpu as pltpu
from jax.sharding import PartitionSpec as P

TAYLOR = 4
SCALES = 5
PATCH = 48
ROWS_K = TAYLOR * SCALES
PAD_K = 24
HALF = PATCH // 2
WIDE = HALF * PATCH
SIDE = 256
SLOTS = 8
WORDS = 8
ROW_BASE = 48
COL_BASE = 64
BLOCKS = 6
CANVAS = 352
GROUPS = (64, 16, 8)
OUT_ROWS = 64
MESH = pl.DeviceIdType.MESH


def sends_of_tiles(tile, off, scale, amp, n_ty, n_tx):
    count = tile.shape[1]
    tiles = n_ty * n_tx
    comp_y = lax.shift_right_logical(tile, n_tx.bit_length() - 1)
    comp_x = lax.bitwise_and(tile, n_tx - 1)
    over_r = (off[0:1] + PATCH > SIDE).astype(jnp.int32)
    over_c = (off[1:2] + PATCH > SIDE).astype(jnp.int32)
    dest = lax.broadcasted_iota(jnp.int32, (tiles, count), 0)
    half = tiles // 2
    bits = n_tx.bit_length() - 1
    core = lax.shift_right_logical(dest, half.bit_length() - 1)
    inner = lax.bitwise_and(dest, half - 1)
    dest_x = lax.bitwise_and(inner, n_tx - 1)
    dest_y = 2 * lax.shift_right_logical(inner, bits) + core
    down, right = dest_y - comp_y, dest_x - comp_x
    touches = ((down == 0) | ((down == 1) & (over_r == 1))) & (
        (right == 0) | ((right == 1) & (over_c == 1))
    )
    before = (
        lax.broadcasted_iota(jnp.int32, (count, count), 0)
        < lax.broadcasted_iota(jnp.int32, (count, count), 1)
    ).astype(jnp.float32)
    rank = jnp.dot(
        jnp.where(touches, 1.0, 0.0).astype(jnp.bfloat16),
        before.astype(jnp.bfloat16),
        preferred_element_type=jnp.float32,
    )
    rank = jnp.where(touches, rank, -1.0)
    chosen = jnp.concatenate(
        [jnp.where(rank == float(k), 1.0, 0.0).astype(jnp.bfloat16) for k in range(SLOTS)], axis=1
    )
    rows = (comp_y * SIDE + off[0:1]).astype(jnp.float32)
    cols = (comp_x * SIDE + off[1:2]).astype(jnp.float32)
    record = jnp.concatenate(
        [rows, cols, scale.astype(jnp.float32), jnp.ones((1, count), jnp.float32), amp], axis=0
    )
    high = record.astype(jnp.bfloat16).astype(jnp.float32)
    rest = record - high
    middle = rest.astype(jnp.bfloat16).astype(jnp.float32)
    low = rest - middle
    place = lax.shift_right_logical(
        lax.broadcasted_iota(jnp.int32, (SLOTS * WORDS, count), 0), 3
    )
    parts = []
    for part in (high, middle, low):
        tall = jnp.concatenate([part] * SLOTS, axis=0)
        parts.append(
            jnp.concatenate([jnp.where(place == k, tall, 0.0) for k in range(SLOTS)], axis=1)
        )
    parts.append(jnp.zeros_like(parts[0]))
    table = jnp.concatenate(parts, axis=0).astype(jnp.bfloat16)
    found = lax.dot_general(
        chosen, table, (((1,), (1,)), ((), ())), preferred_element_type=jnp.float32
    )
    found = found[:, :128] + found[:, 128:]
    found = found + pltpu.roll(found, 64, 1)
    lane = lax.broadcasted_iota(jnp.int32, (half, 128), 1)
    return jnp.where(lane < 64, found[:half], found[half:])


def unrolled(first, last, lane, step):
    tile, shift = divmod(step * PATCH, 128)
    out = []
    for table, base in ((first, 0), (last, 64)):
        value = table(tile)
        if shift + PATCH > 128:
            value = jnp.where(lane >= shift, value, table(tile + 1))
        turn = (base - shift) % 128
        out.append(pltpu.roll(value, turn, 1) if turn else value)
    return jnp.where(
        lane < PATCH, out[0], jnp.where((lane >= 64) & (lane < 64 + PATCH), out[1], 0.0)
    )


def exchange_kernel(
    n_band, n_ty, n_tx,
    tile_hbm, off_hbm, scale_hbm, amp_hbm, weight_hbm, dirty_hbm, psf_hbm,
    value_ref, list_ref, table_ref, taylor_table_ref, fit_ref,
    tile_ref, off_ref, scale_ref, amp_ref, weight_ref, dirty_ref, psf_ref,
    send, cross, got, psf, fit_send, fit_got, tab_send, tab_own, tab_got,
    x_send, x_recv, y_send, y_recv, b_send, b_recv, own_sem, pair_send, pair_recv, load_sem,
):
    me_b, me_y, me_x = lax.axis_index("band"), lax.axis_index("ty"), lax.axis_index("tx")
    barrier = pltpu.get_barrier_semaphore()
    along_x = [lax.rem(me_x + o, n_tx) for o in range(1, n_tx)]
    along_y = [lax.rem(me_y + o, n_ty) for o in range(1, n_ty)]
    along_b = [lax.rem(me_b + o, n_band) for o in range(1, n_band)]
    partners = (
        [(me_b, me_y, x) for x in along_x]
        + [(me_b, y, me_x) for y in along_y]
        + [(b, me_y, me_x) for b in along_b]
    )
    for partner in partners:
        pl.semaphore_signal(barrier, inc=1, device_id=partner, device_id_type=MESH)

    loads = [
        pltpu.make_async_copy(source, target, load_sem.at[i])
        for i, (source, target) in enumerate((
            (tile_hbm, tile_ref), (off_hbm, off_ref), (scale_hbm, scale_ref), (amp_hbm, amp_ref),
            (weight_hbm, weight_ref), (psf_hbm, psf_ref), (dirty_hbm, dirty_ref),
        ))
    ]
    for load in loads:
        load.start()

    for load in loads[:4]:
        load.wait()
    records = sends_of_tiles(tile_ref[...], off_ref[...], scale_ref[...], amp_ref[...], n_ty, n_tx)
    for y in range(n_ty // 2):
        send[y] = records[y * n_tx:(y + 1) * n_tx]

    pl.semaphore_wait(barrier, len(partners))

    def in_all(ref, send_sem, recv_sem, partner):
        return pltpu.make_async_remote_copy(
            src_ref=ref, dst_ref=ref, send_sem=send_sem.at[0], recv_sem=recv_sem.at[0],
            device_id=partner, device_id_type=MESH,
        )

    for y in along_y:
        copy = pltpu.make_async_remote_copy(
            src_ref=send.at[y // 2], dst_ref=cross.at[me_y],
            send_sem=y_send.at[0], recv_sem=y_recv.at[0],
            device_id=(me_b, y, me_x), device_id_type=MESH,
        )
        copy.start()
    stage_y = in_all(cross.at[pl.ds(0, n_ty - 1)], y_send, y_recv, partners[-n_band])
    own = pltpu.make_async_copy(send.at[me_y // 2], cross.at[me_y], own_sem.at[0])
    own.start()
    for load in loads[4:]:
        load.wait()
    for b in range(2):
        psf[b, 0:ROWS_K, :] = psf_ref[:, b, :].astype(jnp.float32)
        psf[b, ROWS_K:PAD_K, :] = jnp.zeros((PAD_K - ROWS_K, 2 * WIDE), jnp.float32)
    core = lax.rem(me_y, 2)
    mine = [
        jnp.where(core == 1, psf[b, :, WIDE:2 * WIDE], psf[b, :, 0:WIDE]) for b in range(2)
    ]
    for o in range(1, n_band):
        w0, w1 = weight_ref[0, along_b[o - 1]], weight_ref[1, along_b[o - 1]]
        tab_send[o - 1] = w0 * mine[0] + w1 * mine[1]
        fit_send[o - 1] = (w0 * dirty_ref[0] + w1 * dirty_ref[1]).astype(jnp.bfloat16)

    w0, w1 = weight_ref[0, me_b], weight_ref[1, me_b]
    tab_own[core] = w0 * mine[0] + w1 * mine[1]
    lane24 = lax.broadcasted_iota(jnp.int32, (PAD_K, 128), 1)

    def piece(ref, half):
        return lambda t: ref[:, half * WIDE + t * 128:half * WIDE + (t + 1) * 128]

    def band_table(half):
        first, last = piece(psf.at[0], half), piece(psf.at[1], half)
        for step in range(HALF):
            table_ref[pl.ds(half * HALF + step, PAD_K, stride=PATCH), :] = unrolled(
                first, last, lane24, step
            )

    band_table(0)

    stage_t, stage_f = [], []
    for source, target, which, copies in (
        (tab_send, tab_got, 0, stage_t), (fit_send, fit_got, 1, stage_f)
    ):
        for o, b in enumerate(along_b):
            copy = pltpu.make_async_remote_copy(
                src_ref=source.at[o], dst_ref=target.at[o],
                send_sem=b_send.at[which, o], recv_sem=b_recv.at[which, o],
                device_id=(b, me_y, me_x), device_id_type=MESH,
            )
            copy.start()
            copies.append(copy)

    own.wait()
    stage_y.wait_recv()
    for x in along_x:
        copy = pltpu.make_async_remote_copy(
            src_ref=cross.at[:, x, :], dst_ref=got.at[:, me_x, :],
            send_sem=x_send.at[0], recv_sem=x_recv.at[0],
            device_id=(me_b, me_y, x), device_id_type=MESH,
        )
        copy.start()
    stage_x = in_all(got.at[:, pl.ds(0, n_tx - 1), :], x_send, x_recv, partners[0])
    own = pltpu.make_async_copy(cross.at[:, me_x, :], got.at[:, me_x, :], own_sem.at[1])
    own.start()

    for copy in stage_t:
        copy.wait_recv()
    for o in range(n_band - 1):
        tab_own[core] += tab_got[o]
    band_table(1)
    pair = pltpu.make_async_remote_copy(
        src_ref=tab_own.at[core], dst_ref=tab_own.at[core],
        send_sem=pair_send.at[0], recv_sem=pair_recv.at[0],
        device_id=(me_b, me_y + 1 - 2 * core, me_x), device_id_type=MESH,
    )
    pair.start()

    pair.wait_recv()
    first, last = piece(tab_own.at[0], 0), piece(tab_own.at[1], 0)
    for step in range(HALF):
        taylor_table_ref[pl.ds(step, PAD_K, stride=HALF), :] = unrolled(first, last, lane24, step)

    fit_ref[...] = w0 * dirty_ref[0] + w1 * dirty_ref[1]
    for copy in stage_f:
        copy.wait_recv()
    for o in range(n_band - 1):
        fit_ref[...] += fit_got[o].astype(jnp.float32)
    own.wait()
    stage_x.wait_recv()
    sources = n_ty * n_tx
    slots = jnp.concatenate([got[y] for y in range(n_ty)], axis=0)
    slots = jnp.where(lax.rem(me_y, 2) == 1, pltpu.roll(slots, 64, 1), slots)
    lane = lax.broadcasted_iota(jnp.int32, (sources, 128), 1)
    word = lax.bitwise_and(lane, WORDS - 1)
    move_r = (ROW_BASE - me_y * SIDE).astype(jnp.float32)
    move_c = (COL_BASE - me_x * SIDE).astype(jnp.float32)
    row = jnp.clip(slots + move_r, 0.0, float(ROW_BASE + SIDE)).astype(jnp.int32)
    col = jnp.clip(
        pltpu.roll(slots, 127, 1) + move_c, 0.0, float(COL_BASE + SIDE)
    ).astype(jnp.int32)
    scale = jnp.clip(pltpu.roll(slots, 126, 1), 0.0, float(SCALES)).astype(jnp.int32)
    place = row + lax.shift_right_logical(col, 6) * CANVAS
    place = place + lax.shift_left(lax.bitwise_and(col, 63), 11) + lax.shift_left(scale, 17)
    value = jnp.where(word == 0, place.astype(jnp.float32), slots)
    quarter = sources // 4
    part = lax.shift_right_logical(lax.broadcasted_iota(jnp.int32, (quarter, 128), 1), 5)
    for first, turn in ((0, 0), (quarter + 8, 96)):
        packed = jnp.zeros((quarter, 128), jnp.float32)
        for q in range(4):
            own_rows = value[q * quarter:(q + 1) * quarter]
            moved = (q * 32 + turn) % 128
            packed = jnp.where(part == q, pltpu.roll(own_rows, moved, 1) if moved else own_rows, packed)
        value_ref[first:first + quarter] = packed
    used = jnp.sum(
        jnp.where((word == 3) & (lane < 64), slots, 0.0), axis=1, keepdims=True
    )
    used = jnp.broadcast_to(used, (sources, 128))
    earlier = (
        lax.broadcasted_iota(jnp.int32, (sources, sources), 1)
        < lax.broadcasted_iota(jnp.int32, (sources, sources), 0)
    ).astype(jnp.float32).astype(jnp.bfloat16)
    start = jnp.dot(earlier, used.astype(jnp.bfloat16), preferred_element_type=jnp.float32)
    end = start + used
    lists = max(1, sources * SLOTS // 128)
    for i in range(lists):
        order = (lane + i * 128).astype(jnp.float32)
        source = jnp.sum(jnp.where(end <= order, 1.0, 0.0), axis=0, keepdims=True)
        base = jnp.max(jnp.where(start <= order, start, 0.0), axis=0, keepdims=True)
        group = sum(jnp.where(source >= float(q * quarter), 1.0, 0.0) for q in (1, 2, 3))
        slot = order[0:1] - base
        far = jnp.where(slot >= 4.0, 1.0, 0.0)
        index = (source - group * quarter + far * (quarter + 8)) * 128.0 + group * 32.0
        index = index + (slot - 4.0 * far) * WORDS
        index = jnp.where(source < float(sources), index, float(quarter * 128))
        list_ref[i:i + 1, :] = index.astype(jnp.int32)
    spot = lax.broadcasted_iota(jnp.int32, (8, 128), 1)
    count = end[sources - 1:sources]
    most = jnp.max(used, axis=0, keepdims=True)
    value_ref[quarter:quarter + 8] = jnp.where(
        spot == WORDS, count, jnp.where(spot == WORDS + 1, most, 0.0)
    )

    for copy in [stage_x, stage_y, pair] + stage_t + stage_f:
        copy.wait_send()


def render_kernel(
    value_ref, order_ref, table_ref, taylor_table_ref, dirty_ref, fit_ref,
    residual_hbm, taylor_hbm,
    canvas, spill, canvas_t, spill_t, residual_ref, taylor_ref, amp_ref, list_ref, sems, out_sems,
):
    near = (value_ref.shape[0] + 1024) // 2
    ends = (pl.ds(0, near), pl.ds(near, value_ref.shape[0] - near))
    fetches = [
        pltpu.make_async_copy(value_ref.at[ends[0]], amp_ref.at[ends[0]], sems.at[0]),
        pltpu.make_async_copy(order_ref, list_ref, sems.at[1]),
        pltpu.make_async_copy(value_ref.at[ends[1]], amp_ref.at[ends[1]], sems.at[2]),
    ]
    for fetch in fetches:
        fetch.start()
    for block in range(BLOCKS - 1):
        for ref, used, first in (
            (canvas, block > 0, ROW_BASE), (spill, block < 4, ROW_BASE),
            (canvas_t, block > 0, ROW_BASE - HALF), (spill_t, block < 4, ROW_BASE - HALF),
        ):
            if used:
                rows = ROW_BASE + SIDE - first
                ref[pl.ds(block * CANVAS + first, rows), :] = jnp.zeros((rows, 128), jnp.float32)
    for fetch in fetches[:2]:
        fetch.wait()
    half_lane = lax.bitwise_and(lax.broadcasted_iota(jnp.int32, (HALF, 128), 1), 63)
    count = amp_ref[near - 1024 + WORDS].astype(jnp.int32)
    crowded = amp_ref[near - 1024 + WORDS + 1] > 4.0

    @pl.when(crowded)
    def _():
        fetches[2].wait()


    def step(first_of_all, group, index, carry):
        for g in range(group):
            slot = list_ref[first_of_all + index * group + g]
            packed = amp_ref[slot].astype(jnp.int32)
            amps = [amp_ref[slot + 4 + t] for t in range(TAYLOR)]
            first = lax.bitwise_and(packed, 2047)
            shift = lax.bitwise_and(lax.shift_right_logical(packed, 11), 63)
            base = lax.shift_right_logical(packed, 17) * HALF
            low = pl.multiple_of(base, HALF)
            high = pl.multiple_of(2 * base, PATCH)
            patch = fit = None
            for t in range(TAYLOR):
                term = amps[t] * table_ref[pl.ds(high + t * SCALES * PATCH, PATCH), :]
                patch = term if t == 0 else patch + term
                term = amps[t] * taylor_table_ref[pl.ds(low + t * SCALES * HALF, HALF), :]
                fit = term if t == 0 else fit + term
            patch = patch.astype(jnp.bfloat16).astype(jnp.float32)
            keep = half_lane >= shift
            other = jnp.logical_not(keep)
            sums = []
            for value, inside, beyond, at in (
                (patch[:HALF], canvas, spill, first),
                (patch[HALF:], canvas, spill, first + HALF),
                (fit, canvas_t, spill_t, first),
            ):
                value = pltpu.roll(value, shift, 1)
                for mask, target in ((keep, inside), (other, beyond)):
                    here = target.at[pl.ds(at, HALF), :]
                    sums.append((here, here[...] + value, mask))
            for here, value, mask in sums:
                pltpu.store(here, value, mask=mask)
        return carry

    done = 0
    for group in GROUPS:
        left = count - done + (group - 1 if group == GROUPS[-1] else 0)
        turns = left // group
        lax.fori_loop(0, turns, functools.partial(step, done, group), 0)
        done = done + turns * group

    @pl.when(jnp.logical_not(crowded))
    def _():
        fetches[2].wait()

    rows = OUT_ROWS
    lower = lax.broadcasted_iota(jnp.int32, (rows, 128), 1) < 64

    def mix(low, high):
        return jnp.where(lower, low, high)

    copies = []
    for r in range(0, SIDE, rows):
        for j in range(2):

            def at(ref, block, first):
                start = (block + 2 * j) * CANVAS + ROW_BASE + r + first
                return ref[pl.ds(start, rows), :]

            c1, c2 = at(canvas, 1, 0), at(canvas, 2, 0)
            s1, s2 = at(spill, 0, 0), at(spill, 1, 0)
            here = (slice(r, r + rows), slice(j * 128, j * 128 + 128))
            model = mix(c1, s2) + pltpu.roll(mix(c2, s1), 64, 1)
            residual_ref[(0,) + here] = dirty_ref[(0,) + here] - model
            model = mix(s1, c2) + pltpu.roll(mix(s2, c1), 64, 1)
            residual_ref[(1,) + here] = dirty_ref[(1,) + here] - model
            straight = mix(
                at(canvas_t, 1, 0) + at(spill_t, 0, -HALF), at(canvas_t, 2, -HALF) + at(spill_t, 1, 0)
            )
            crossed = mix(
                at(canvas_t, 2, 0) + at(spill_t, 1, -HALF), at(canvas_t, 1, -HALF) + at(spill_t, 0, 0)
            )
            taylor_ref[here] = fit_ref[here] - (straight + pltpu.roll(crossed, 64, 1))
        part = r // rows
        copies.append(
            pltpu.make_async_copy(
                residual_ref.at[:, pl.ds(r, rows), :], residual_hbm.at[:, pl.ds(r, rows), :],
                out_sems.at[0, part],
            )
        )
        copies.append(
            pltpu.make_async_copy(
                taylor_ref.at[pl.ds(r, rows), :], taylor_hbm.at[pl.ds(r, rows), :],
                out_sems.at[1, part],
            )
        )
        copies[-2].start()
        copies[-1].start()
    for copy in copies:
        copy.wait()


def per_device(dirty, psf, comp_tile, comp_offset, comp_scale, comp_amp, fit_weight):
    n_band, n_ty, n_tx = (lax.axis_size(a) for a in ("band", "ty", "tx"))
    sources, listed = n_ty * n_tx, comp_tile.shape[0]
    lists = max(1, sources * SLOTS // 128)
    vmem = pl.BlockSpec(memory_space=pltpu.VMEM)
    hbm = pl.BlockSpec(memory_space=pltpu.HBM)
    dma = pltpu.SemaphoreType.DMA
    f32, bf16 = jnp.float32, jnp.bfloat16
    value, order, table, taylor_table, fit = pl.pallas_call(
        functools.partial(exchange_kernel, n_band, n_ty, n_tx),
        out_shape=(
            jax.ShapeDtypeStruct((sources // 2 + 8, 128), f32),
            jax.ShapeDtypeStruct((lists, 128), jnp.int32),
            jax.ShapeDtypeStruct((PAD_K * PATCH, 128), f32),
            jax.ShapeDtypeStruct((PAD_K * HALF, 128), f32),
            jax.ShapeDtypeStruct((SIDE, SIDE), f32),
        ),
        in_specs=[hbm] * 7,
        out_specs=(vmem,) * 5,
        scratch_shapes=[
            pltpu.VMEM((1, listed), jnp.int32), pltpu.VMEM((2, listed), jnp.int32),
            pltpu.VMEM((1, listed), jnp.int32), pltpu.VMEM((TAYLOR, listed), f32),
            pltpu.SMEM((2, TAYLOR), f32), pltpu.VMEM((2, SIDE, SIDE), f32),
            pltpu.VMEM((ROWS_K, 2, 2 * WIDE), bf16),
            pltpu.VMEM((n_ty // 2, n_tx, 128), f32),
            pltpu.VMEM((n_ty, n_tx, 128), f32),
            pltpu.VMEM((n_ty, n_tx, 128), f32),
            pltpu.VMEM((2, PAD_K, 2 * WIDE), f32),
            pltpu.VMEM((n_band - 1, SIDE, SIDE), bf16),
            pltpu.VMEM((n_band - 1, SIDE, SIDE), bf16),
            pltpu.VMEM((n_band - 1, PAD_K, WIDE), f32),
            pltpu.VMEM((2, PAD_K, WIDE), f32),
            pltpu.VMEM((n_band - 1, PAD_K, WIDE), f32),
            dma((1,)), dma((1,)), dma((1,)), dma((1,)),
            dma((2, n_band - 1)), dma((2, n_band - 1)),
            dma((2,)), dma((1,)), dma((1,)), dma((7,)),
        ],
        compiler_params=pltpu.CompilerParams(
            collective_id=0, has_side_effects=True, vmem_limit_bytes=24 * 1024 * 1024
        ),
    )(
        *(
            pltpu.with_memory_space_constraint(operand, pltpu.HBM)
            for operand in (
                comp_tile.T, comp_offset.T, comp_scale[None, :], comp_amp.T, fit_weight, dirty,
                psf.transpose(1, 0, 2),
            )
        ),
    )
    residual, taylor = pl.pallas_call(
        render_kernel,
        out_shape=(
            jax.ShapeDtypeStruct((2, SIDE, SIDE), f32),
            jax.ShapeDtypeStruct((SIDE, SIDE), f32),
        ),
        in_specs=[vmem] * 6,
        out_specs=(hbm,) * 2,
        scratch_shapes=[
            pltpu.VMEM(((BLOCKS - 1) * CANVAS, 128), f32) for _ in range(4)
        ] + [
            pltpu.VMEM((2, SIDE, SIDE), f32), pltpu.VMEM((SIDE, SIDE), f32),
            pltpu.SMEM((value.size,), f32), pltpu.SMEM((order.size,), jnp.int32),
            dma((3,)), dma((2, SIDE // OUT_ROWS)),
        ],
        compiler_params=pltpu.CompilerParams(vmem_limit_bytes=24 * 1024 * 1024),
    )(
        value.reshape(-1), order.reshape(-1), table, taylor_table, dirty, fit,
    )
    return residual, taylor[None]


def solution(mesh):
    return jax.shard_map(
        per_device,
        mesh=mesh,
        in_specs=(
            P("band", "ty", "tx"),
            P("band", None, None),
            P(("ty", "tx"), None),
            P(("ty", "tx"), None),
            P(("ty", "tx")),
            P(("ty", "tx"), None),
            P("band", None),
        ),
        out_specs=(P("band", "ty", "tx"), P("band", "ty", "tx")),
        check_vma=False,
    )
```
